32 devices in a mesh: dp: 8 (over z, x), mp: 4 (over y, core).
Axes of the slice: x: 2, y: 2, z: 4, core: 2. Of those that a mesh axis runs over, the one named last changes fastest.
Arguments:
- tokens: bfloat16 [16, 1024, 768], P('dp', 'mp'), may hold values from -6 to 6
- lengths: int32 [16, 30], P('dp'), may hold values from 24 to 32, as said below
- view_masks: int32 [16, 30, 2, 768], P('dp'), may hold values 0 or 1
- w_qkv: bfloat16 [3, 768, 768], P(None, None, 'mp'), may hold values from -0.21875 to 0.21875
- b_qv: float32 [2, 768], P(None, 'mp'), may hold values from -3 to 3
- w_out: bfloat16 [768, 768], P('mp'), may hold values from -0.625 to 0.625
- b_out: float32 [768], replicated, may hold values from -3 to 3
- ln1_gain: float32 [768], replicated, may hold values from 0.5 to 1.5
- ln1_bias: float32 [768], replicated, may hold values from -2 to 2
- w_in: bfloat16 [768, 3072], P(None, 'mp'), may hold values from -0.21875 to 0.21875
- b_in: float32 [3072], P('mp'), may hold values from -3 to 3
- w_back: bfloat16 [3072, 768], P('mp'), may hold values from -0.109375 to 0.109375
- b_back: float32 [768], replicated, may hold values from -3 to 3
- ln2_gain: float32 [768], replicated, may hold values from 0.5 to 1.5
- ln2_bias: float32 [768], replicated, may hold values from -2 to 2
- w_pool: bfloat16 [768, 768], replicated, may hold values from -0.21875 to 0.21875
- b_pool: float32 [768], replicated, may hold values from -2 to 2
- cotangent: bfloat16 [16, 1024, 768], P('dp', 'mp'), may hold values from -6 to 6
Outputs:
- hidden: bfloat16 [16, 1024, 768], P('dp', 'mp')
- loss: float32 [], replicated
- tokens_grad: float32 [16, 1024, 768], P('dp', 'mp')
- w_qkv_grad: float32 [3, 768, 768], P(None, None, 'mp')
- b_qv_grad: float32 [2, 768], P(None, 'mp')
- w_out_grad: float32 [768, 768], P('mp')
- b_out_grad: float32 [768], replicated
- ln1_gain_grad: float32 [768], replicated
- ln1_bias_grad: float32 [768], replicated
- w_in_grad: float32 [768, 3072], P(None, 'mp')
- b_in_grad: float32 [3072], P('mp')
- w_back_grad: float32 [3072, 768], P('mp')
- b_back_grad: float32 [768], replicated
- ln2_gain_grad: float32 [768], replicated
- ln2_bias_grad: float32 [768], replicated
- w_pool_grad: float32 [768, 768], replicated
- b_pool_grad: float32 [768], replicated
The draws below stay inside these ranges and needn't reach their ends.
Inputs may be any that keep to these rules, and one draw needn't show every extreme that they name: In each row the 30 sentence lengths are 24 to 32, one of them exactly 32; the positions after the last sentence are padding.
All inputs are finite; a program needn't handle non-finite values. No bound on the sum of `view_masks` on one device may be relied on, other than what follows from the above.
Results may differ from the reference program's by a relative error of at most 0.018.
Values may be sent and summed in bfloat16 or wider, within the bound.
A program may use at most 128 MiB of HBM per device.

```python
import jax
import jax.numpy as jnp
from jax import lax

D = 768
HEADS = 12
HDIM = 64
FF = 3072
L = 1024
SPR = 30
MAXLEN = 32
SEQS = 16
SENTS = 480


def draw_lengths(key, part):
    key_base = jax.random.fold_in(key, 11)
    key_column = jax.random.fold_in(key, 12)
    drawn_lengths = jax.random.randint(key_base, (SEQS, SPR), 3 * MAXLEN // 4, MAXLEN + 1, dtype=jnp.int32)
    column_pick = jax.random.randint(key_column, (SEQS, 1), 0, SPR, dtype=jnp.int32)
    positions = jnp.arange(SPR, dtype=jnp.int32)[None, :]
    return jnp.where(positions == column_pick, MAXLEN, drawn_lengths).astype(jnp.int32)


def set_ends(values, key, least, largest):
    dims = values.shape
    spot = [jax.random.randint(jax.random.fold_in(key, axis), (), 0, dims[axis]) for axis in range(len(dims))]
    values = values.at[tuple(spot)].set(least)
    longest = dims.index(max(dims))
    spot[longest] = (spot[longest] + 1) % dims[longest]
    return values.at[tuple(spot)].set(largest)


def block_levels(key, shape, pieces, low, top_value):
    def one(axis_at, blocks):
        draws = jax.random.uniform(jax.random.fold_in(jax.random.fold_in(key, 6), axis_at), (blocks,), jnp.float32, low / len(pieces), top_value / len(pieces))
        return jnp.repeat(jnp.exp(draws), shape[axis_at] // blocks).reshape((-1,) + (1,) * (len(shape) - axis_at - 1))

    loudness = one(*pieces[0])
    for cut in pieces[1:]:
        loudness = loudness * one(*cut)
    return loudness


def centred(stream_key, extent, scale, bound, split=(), kind=jnp.bfloat16):
    result = jax.random.normal(stream_key, extent, jnp.float32) * scale
    if len(split) > 0:
        result = block_levels(stream_key, extent, split, -0.22, 0.18) * result
    return jnp.clip(result, min=-bound, max=bound).astype(kind)


def setup_inputs(seed: int = 0) -> dict:
    seeds = jax.random.split(jax.random.key(seed), 19)
    tokens = centred(seeds[0], (SEQS, L, D), 1.0, 6.0, ((0, 8), (1, 4)))
    lengths = draw_lengths(jax.random.fold_in(seeds[18], 71), 0)
    view_masks = set_ends((jax.random.randint(seeds[2], (SEQS, SPR, 2, D), 0, 10) < 9).astype(jnp.int32), jax.random.fold_in(seeds[2], 1), 0, 1)
    w_qkv = centred(seeds[3], (3, D, D), D ** -0.5, 0.21875, ((2, 4),))
    b_qv = centred(seeds[4], (2, D), 0.5, 3.0, ((1, 4),), jnp.float32)
    w_out = centred(seeds[5], (D, D), (D // 8) ** -0.5, 0.625, ((0, 4),))
    b_out = centred(seeds[6], (D,), 0.5, 3.0, (), jnp.float32)
    ln1_gain = jnp.clip(1.0 + 0.1 * jax.random.normal(seeds[7], (D,), jnp.float32), 0.5, 1.5)
    ln1_bias = centred(seeds[8], (D,), 0.3, 2.0, (), jnp.float32)
    w_in = centred(seeds[9], (D, FF), D ** -0.5, 0.21875, ((1, 4),))
    b_in = centred(seeds[10], (FF,), 0.5, 3.0, ((0, 4),), jnp.float32)
    w_back = centred(seeds[11], (FF, D), FF ** -0.5, 0.109375, ((0, 4),))
    b_back = centred(seeds[12], (D,), 0.5, 3.0, (), jnp.float32)
    ln2_gain = jnp.clip(1.0 + 0.1 * jax.random.normal(seeds[13], (D,), jnp.float32), 0.5, 1.5)
    ln2_bias = centred(seeds[14], (D,), 0.3, 2.0, (), jnp.float32)
    w_pool = centred(seeds[15], (D, D), D ** -0.5, 0.21875)
    b_pool = centred(seeds[16], (D,), 0.3, 2.0, (), jnp.float32)
    cotangent = centred(seeds[17], (SEQS, L, D), 1.0, 6.0, ((0, 8), (1, 4)))
    return {"tokens": tokens, "lengths": lengths, "view_masks": view_masks, "w_qkv": w_qkv, "b_qv": b_qv, "w_out": w_out, "b_out": b_out, "ln1_gain": ln1_gain, "ln1_bias": ln1_bias, "w_in": w_in, "b_in": b_in, "w_back": w_back, "b_back": b_back, "ln2_gain": ln2_gain, "ln2_bias": ln2_bias, "w_pool": w_pool, "b_pool": b_pool, "cotangent": cotangent}


@jax.custom_vjp
def low(v):
    return lax.optimization_barrier(v.astype(jnp.bfloat16)).astype(jnp.float32)

@jax.custom_vjp
def low_back(v):
    return v

def low_keep(v):
    return (low(v), None)

def low_pass(kept, grad):
    return (grad,)

def back_keep(v):
    return (v, None)

def back_low(kept, grad):
    return (low(grad),)
low.defvjp(low_keep, low_pass)
low_back.defvjp(back_keep, back_low)

def matmul(left, right):
    return jnp.dot(left, right, precision=lax.Precision.HIGHEST, preferred_element_type=jnp.float32)

def layout(lengths_row):
    sentence_ends = jnp.cumsum(lengths_row, dtype=jnp.int32)
    starts = sentence_ends - lengths_row
    places = jnp.arange(L, dtype=jnp.int32)
    passed = lax.optimization_barrier(jnp.sum((places[:, None] >= sentence_ends[None, :]).astype(jnp.int32), axis=1, dtype=jnp.int32))
    segment = jnp.where(places < sentence_ends[-1], passed, places + SPR)
    return (segment, starts)

def layer_norm(values, gain, shift):
    center = values - lax.optimization_barrier(jnp.mean(values, axis=-1, keepdims=True))
    spread = lax.optimization_barrier(jnp.mean(center * center, axis=-1, keepdims=True))
    return center * lax.rsqrt(spread + 1e-12) * gain + shift

def encode_row(token_row, lengths_row, layer):
    w_qkv, b_qv, w_out, b_out, ln1_gain, ln1_bias, w_in, b_in, w_back, b_back, ln2_gain, ln2_bias = layer
    segment, starts = layout(lengths_row)
    inputs = low(token_row)
    queries = low(low_back(matmul(inputs, w_qkv[0]) + b_qv[0]))
    key_rows = low(low_back(matmul(inputs, w_qkv[1])))
    value_rows = low(low_back(matmul(inputs, w_qkv[2]) + b_qv[1]))
    head_shape = (L, HEADS, HDIM)
    scores = jnp.einsum('qhd,khd->hqk', queries.reshape(head_shape), key_rows.reshape(head_shape), precision=lax.Precision.HIGHEST) * HDIM ** (-0.5)
    scores = low_back(scores)
    allowed = segment[:, None] == segment[None, :]
    scores = jnp.where(allowed[None], scores, -1000000000.0)
    attention = low(jax.nn.softmax(scores, axis=-1))
    context = jnp.einsum('hqk,khd->qhd', attention, value_rows.reshape(head_shape), precision=lax.Precision.HIGHEST).reshape(L, D)
    context = low(low_back(context))
    attended = low_back(matmul(context, w_out))
    normed_one = layer_norm(token_row + attended + b_out, ln1_gain, ln1_bias)
    hidden_units = low_back(matmul(low(normed_one), w_in) + b_in)
    activation = low(jax.nn.gelu(hidden_units, approximate=False))
    returned = low_back(matmul(activation, w_back))
    normed_two = layer_norm(normed_one + returned + b_back, ln2_gain, ln2_bias)
    return (normed_two, normed_two[starts])

def contrast(cls_rows, view_keep, w_pool, b_pool):
    views = low(cls_rows[:, None, :] * view_keep * (1.0 / 0.9))
    before = jnp.einsum('svd,de->sve', views, w_pool, precision=lax.Precision.HIGHEST) + b_pool
    pooled = jnp.tanh(low_back(before))
    unit = pooled * lax.rsqrt(lax.optimization_barrier(jnp.sum(pooled * pooled, axis=-1, keepdims=True)) + 1e-06)
    anchors = low(unit[:, 0])
    targets = low(unit[:, 1])
    logits = low_back(matmul(anchors, targets.T) * 20.0)
    sent_ids = jnp.arange(SENTS, dtype=jnp.int32)
    chosen = lax.optimization_barrier(jnp.sum(jnp.where(sent_ids[None, :] == sent_ids[:, None], logits, 0.0), axis=1))
    return jnp.sum(jax.nn.logsumexp(logits, axis=1) - chosen)

def reference(tokens, lengths, view_masks, w_qkv, b_qv, w_out, b_out, ln1_gain, ln1_bias, w_in, b_in, w_back, b_back, ln2_gain, ln2_bias, w_pool, b_pool, cotangent):
    view_keep = view_masks.astype(jnp.float32).reshape(SENTS, 2, D)

    def forward(token_rows, *weights):
        layer = weights[:12]

        def scan_step(carried, scan_item):
            normed_two, cls_rows = encode_row(scan_item[0], scan_item[1], layer)
            return (carried, (normed_two, cls_rows))
        unused, (hidden_rows, cls_rows) = lax.scan(jax.checkpoint(scan_step), jnp.float32(0.0), (token_rows, lengths))
        loss_total = contrast(cls_rows.reshape(SENTS, D), view_keep, weights[12], weights[13])
        return (hidden_rows, loss_total)
    primals = tuple((member.astype(jnp.float32) for member in (tokens, w_qkv, b_qv, w_out, b_out, ln1_gain, ln1_bias, w_in, b_in, w_back, b_back, ln2_gain, ln2_bias, w_pool, b_pool)))
    (hidden_rows, loss_total), pullback = jax.vjp(forward, *primals)
    gradients = pullback((cotangent.astype(jnp.float32), jnp.float32(1.0)))
    return (hidden_rows.astype(jnp.bfloat16), loss_total / SENTS, gradients[0], gradients[1], gradients[2], gradients[3], gradients[4], gradients[5], gradients[6], gradients[7], gradients[8], gradients[9], gradients[10], gradients[11], gradients[12], gradients[13], gradients[14])
```

```python
import jax
import jax.numpy as jnp
from jax import lax
from jax.experimental import pallas as pl
from jax.experimental.pallas import tpu as pltpu
from jax.sharding import PartitionSpec as P

HDIM = 64
HALO = 32
BLOCK = 64
KEEP_SCALE = 1.0 / 0.9
MASKED = -1000000000.0


def norm_forward(values, gain, shift):
    center = values - jnp.mean(values, axis=-1, keepdims=True)
    inv_dev = lax.rsqrt(jnp.mean(center * center, axis=-1, keepdims=True) + 1e-12)
    normed = center * inv_dev
    return (normed * gain + shift, normed, inv_dev)


def dot32(equation, left, right):
    return jnp.einsum(equation, left, right, preferred_element_type=jnp.float32)


def contrast(cls_rows, view_masks, w_pool, b_pool):
    local_sents = cls_rows.shape[0]
    own_ids = lax.axis_index("dp") * local_sents + jnp.arange(local_sents, dtype=jnp.int32)
    keep_masks = view_masks.astype(jnp.float32).reshape(local_sents, 2, -1)
    views = (cls_rows[:, None, :] * keep_masks * KEEP_SCALE).astype(jnp.bfloat16)
    pooled = jnp.tanh(dot32("svd,de->sve", views, w_pool) + b_pool)
    inv_length = lax.rsqrt(jnp.sum(pooled * pooled, axis=-1, keepdims=True) + 1e-06)
    unit = pooled * inv_length
    unit_low = unit.astype(jnp.bfloat16)
    anchors = unit_low[:, 0]
    every_target = lax.all_gather(unit_low[:, 1], "dp", axis=0, tiled=True)
    logits = dot32("sd,td->st", anchors, every_target) * 20.0
    sent_ids = jnp.arange(every_target.shape[0], dtype=jnp.int32)
    is_partner = sent_ids[None, :] == own_ids[:, None]
    row_peak = jnp.max(logits, axis=1, keepdims=True)
    raised = jnp.exp(logits - row_peak)
    row_total = jnp.sum(raised, axis=1, keepdims=True)
    log_total = row_peak[:, 0] + jnp.log(row_total[:, 0])
    loss_local = jnp.sum(log_total - jnp.sum(jnp.where(is_partner, logits, 0.0), axis=1))
    logit_grad = (raised / row_total - is_partner.astype(jnp.float32)).astype(jnp.bfloat16)
    anchor_grad = dot32("st,td->sd", logit_grad, every_target) * 20.0
    target_terms = dot32("st,sd->td", logit_grad, anchors) * 20.0
    target_grad = lax.psum_scatter(target_terms, "dp", scatter_dimension=0, tiled=True)
    unit_grad = jnp.stack([anchor_grad, target_grad], axis=1)
    pooled_grad = inv_length * (
        unit_grad - unit * jnp.sum(unit_grad * unit, axis=-1, keepdims=True)
    )
    before_grad = (pooled_grad * (1.0 - pooled * pooled)).astype(jnp.bfloat16)
    w_pool_grad = dot32("svd,sve->de", views, before_grad)
    b_pool_grad = jnp.sum(before_grad, axis=(0, 1), dtype=jnp.float32)
    view_grad = dot32("sve,de->svd", before_grad, w_pool)
    cls_grad = jnp.sum(view_grad * keep_masks, axis=1) * KEEP_SCALE
    sums = lax.psum((w_pool_grad, b_pool_grad, loss_local), "dp")
    loss = sums[2] / (local_sents * lax.axis_size("dp"))
    return (loss, sums[0], sums[1], cls_grad)


MESH = pl.DeviceIdType.MESH
UNIT = 192
UNITS = 12


def greet(peers):
    barrier = pltpu.get_barrier_semaphore()
    for peer in peers:
        pl.semaphore_signal(barrier, inc=1, device_id=peer, device_id_type=MESH)
    pl.semaphore_wait(barrier, len(peers))


class Places:
    def __init__(self, dp_size):
        self.dp = lax.axis_index("dp")
        self.mp = lax.axis_index("mp")
        self.core = self.mp % 2
        self.y = self.mp // 2
        self.x = self.dp % 2
        self.z = self.dp // 2
        self.depth = dp_size // 2
        self.across_core = (self.dp, self.y * 2 + (1 - self.core))
        self.across_y = (self.dp, (1 - self.y) * 2 + self.core)
        self.across_both = (self.dp, (1 - self.y) * 2 + (1 - self.core))
        self.across_x = (self.z * 2 + (1 - self.x), self.mp)

    def along_z(self, step):
        return ((self.z + step) % self.depth * 2 + self.x, self.mp)

    def back_z(self, step):
        return (self.z + self.depth - step) % self.depth


def remote(src, dst, send_sem, recv_sem, device):
    return pltpu.make_async_remote_copy(
        src_ref=src,
        dst_ref=dst,
        send_sem=send_sem,
        recv_sem=recv_sem,
        device_id=device,
        device_id_type=MESH,
    )


def norm_tiles(count, tile, body):
    @pl.loop(0, count // tile)
    def _(i):
        body(pl.ds(pl.multiple_of(i * tile, tile), tile))


def row_marks(lengths_ref, local, first, share, region):
    rows, sents = lengths_ref.shape
    row_id = lax.broadcasted_iota(jnp.int32, local.shape, 0)
    places = local + first

    def per_row(values):
        out = jnp.full(local.shape, values[-1], jnp.int32)
        for r in range(rows - 1):
            out = jnp.where(row_id == r, values[r], out)
        return out

    def body(j, carry):
        passed, begun, ends = carry
        ends = tuple(ends[r] + lengths_ref[r, j] for r in range(rows))
        edge = per_row(ends)
        reached = places >= edge
        return (
            passed + reached.astype(jnp.int32),
            jnp.where(reached, edge, begun),
            ends,
        )

    zero = jnp.zeros(local.shape, jnp.int32)
    start = tuple(jnp.int32(0) for _ in range(rows))
    passed, begun, ends = lax.fori_loop(0, sents, body, (zero, zero, start))
    inside = places < per_row(ends)
    here = (local >= 0) & (local < region)
    segment = jnp.where(here, jnp.where(inside, passed, places + sents), -2)
    begins = (begun >= first) & (begun < first + share)
    owned = here & ((inside & begins) | (~inside & (local < share)))
    return (segment, owned)


def start_column(lengths_ref, row, first, slots):
    slot = lax.broadcasted_iota(jnp.int32, (slots, 1), 0)

    def body(j, carry):
        column, begin = carry
        column = jnp.where(slot == j, begin - first, column)
        return (column, begin + lengths_ref[row, j])

    column, _ = lax.fori_loop(
        0, lengths_ref.shape[1], body, (jnp.full((slots, 1), -1, jnp.int32), jnp.int32(0))
    )
    return column


def head_stack(values):
    lane = lax.broadcasted_iota(jnp.int32, values.shape, 1) // HDIM
    zero = jnp.zeros_like(values)
    return jnp.concatenate(
        [jnp.where(lane == h, values, zero) for h in range(values.shape[1] // HDIM)], axis=0
    )


def head_pick(stacked, width):
    heads = width // HDIM
    rows = stacked.shape[0] // heads
    lane = lax.broadcasted_iota(jnp.int32, (rows, width), 1) // HDIM
    out = stacked[:rows]
    for h in range(1, heads):
        out = jnp.where(lane == h, stacked[h * rows : (h + 1) * rows], out)
    return out


def nn(left, right):
    return jnp.dot(left, right, preferred_element_type=jnp.float32)


def nt(left, right):
    return lax.dot_general(
        left, right, (((1,), (1,)), ((), ())), preferred_element_type=jnp.float32
    )


def tn(left, right):
    return lax.dot_general(
        left, right, (((0,), (0,)), ((), ())), preferred_element_type=jnp.float32
    )


def shard_order(at):
    return [
        at.mp,
        at.y * 2 + (1 - at.core),
        (1 - at.y) * 2 + at.core,
        (1 - at.y) * 2 + (1 - at.core),
    ]


def forward_kernel(dp_size, *refs):
    (
        lengths_ref,
        tokens_hbm,
        wq_hbm,
        wo_hbm,
        wi_hbm,
        wb_hbm,
        bq_hbm,
        bi_hbm,
        b_out,
        gain1,
        shift1,
        b_back,
        gain2,
        shift2,
        hidden_hbm,
        cls_ref,
        wq_out,
        wo_out,
        wi_out,
        wb_out,
        tok_out,
        q_out,
        k_out,
        v_out,
        p_out,
        o_out,
        h1_out,
        n1_out,
        r1_out,
        g_out,
        gp_out,
        n2_out,
        r2_out,
        own_out,
        tok,
        wq,
        wo,
        wi,
        wb,
        bq,
        bi,
        q,
        k,
        v,
        probs,
        o,
        h1,
        n1,
        r1,
        g,
        gp,
        n2,
        r2,
        own,
        acc,
        upper,
        seg,
        hid,
        hid_in,
        local_sem,
        halo_sem,
        bias_s,
        bias_r,
        core_s,
        core_r,
        y_s,
        y_r,
        x_s,
        x_r,
        yc_s,
        yc_r,
        xc_s,
        xc_r,
        out_sem,
    ) = refs
    at = Places(dp_size)
    rows, share, width = tokens_hbm.shape
    region = share + HALO
    total = rows * region
    m = at.mp
    first = m * share
    left = (at.dp, (m + 3) % 4)
    right = (at.dp, (m + 1) % 4)
    order = range(4)
    chunks = (
        [(wq, wq_hbm, (t,)) for t in range(3)]
        + [(wo, wo_hbm, ())]
        + [(wi, wi_hbm, (b,)) for b in range(4)]
        + [(wb, wb_hbm, (b,)) for b in range(4)]
    )
    whole = [(wq, wq_hbm), (wo, wo_hbm), (wi, wi_hbm), (wb, wb_hbm)]

    greet([(at.dp, (m + j) % 4) for j in range(1, 4)] + [at.across_x])

    loads = [
        pltpu.make_async_copy(tokens_hbm.at[r], tok.at[pl.ds(r * region, share)], local_sem.at[r])
        for r in range(rows)
    ]
    loads += [
        pltpu.make_async_copy(src, dst.at[0], local_sem.at[rows + i])
        for i, (dst, src) in enumerate(whole + [(bq, bq_hbm), (bi, bi_hbm)])
    ]
    for load in loads:
        load.start()
    halos = [
        remote(
            tokens_hbm.at[r, pl.ds(0, HALO)],
            tok.at[pl.ds(r * region + share, HALO)],
            halo_sem.at[0, r],
            halo_sem.at[1, r],
            left,
        )
        for r in range(rows)
    ]
    for copy in halos:
        copy.start()
    biases = []
    for j, device in enumerate((at.across_core, at.across_y, at.across_both), start=1):
        for i, (dst, src) in enumerate([(bq, bq_hbm), (bi, bi_hbm)]):
            biases.append(
                remote(src, dst.at[j], bias_s.at[j - 1, i], bias_r.at[j - 1, i], device)
            )
    for copy in biases:
        copy.start()

    def core_copy(i):
        dst, src = whole[i]
        return remote(src, dst.at[1], core_s.at[i], core_r.at[i], at.across_core)

    def y_copy(c):
        dst, src, index = chunks[c]
        place = (*index, at.x)
        return remote(src.at[place], dst.at[(2, *place)], y_s.at[c], y_r.at[c], at.across_y)

    def x_copy(c):
        ref = chunks[c][0].at[(2, *chunks[c][2], at.x)]
        return remote(ref, ref, x_s.at[c], x_r.at[c], at.across_x)

    def yc_copy(c):
        ref, _, index = chunks[c]
        place = (*index, at.x)
        return remote(
            ref.at[(2, *place)], ref.at[(3, *place)], yc_s.at[c], yc_r.at[c], at.across_core
        )

    def xc_copy(c):
        ref, _, index = chunks[c]
        place = (*index, 1 - at.x)
        return remote(
            ref.at[(2, *place)], ref.at[(3, *place)], xc_s.at[c], xc_r.at[c], at.across_core
        )

    for c in range(12):
        y_copy(c).start()
    for i in range(4):
        core_copy(i).start()

    def step(c):
        if c < 12:
            y_copy(c).wait_recv()
            x_copy(c).start()
            yc_copy(c).start()
        if c > 0:
            x_copy(c - 1).wait_recv()
            xc_copy(c - 1).start()

    saves = []

    def save(src, dst):
        copy = pltpu.make_async_copy(src, dst, out_sem.at[len(saves)])
        copy.start()
        saves.append(copy)

    lane = lax.broadcasted_iota(jnp.int32, (8, 384), 1)
    segment, owned = row_marks(lengths_ref, lane, first, share, region)
    seg_cols = segment.astype(jnp.float32).T
    own_cols = owned.astype(jnp.float32).T
    for r in range(rows):
        seg[r] = jnp.broadcast_to(seg_cols[: seg.shape[1], r : r + 1], seg.shape[1:])
        own[pl.ds(r * region, region)] = own_cols[:region, r : r + 1]
    save(own, own_out)
    key_rows = []
    for r in range(rows):
        block = lax.broadcasted_iota(jnp.int32, (8, BLOCK + 2 * HALO), 0)
        offset = lax.broadcasted_iota(jnp.int32, (8, BLOCK + 2 * HALO), 1)
        keys, _ = row_marks(
            RowView(lengths_ref, r), block * BLOCK + offset - HALO, first, share, region
        )
        key_rows.append(keys.astype(jnp.float32))
    blocks = q.shape[2] // BLOCK

    q[...] = jnp.zeros_like(q)
    k[...] = jnp.zeros_like(k)
    v[...] = jnp.zeros_like(v)

    for load in loads:
        load.wait()
    for copy in halos:
        copy.wait()
    for copy in biases:
        copy.wait_recv()
    save(tok, tok_out)

    def project(s):
        x = tok[...]
        for t, dst in enumerate((q, k, v)):
            y = nn(x, wq[s, t].reshape(width, -1))
            if t == 0:
                y = (y + bq[s, 0:1]).astype(jnp.bfloat16) * jnp.bfloat16(0.125)
            elif t == 1:
                y = y.astype(jnp.bfloat16)
            else:
                y = (y + bq[s, 1:2]).astype(jnp.bfloat16)
            lead = 0 if t == 0 else HALO
            for r in range(rows):
                dst[s, r, lead : lead + region] = y[r * region : (r + 1) * region]

    def attend(s):
        heads = q.shape[3] // HDIM
        for r in range(rows):
            for b in range(blocks):
                queries = head_stack(q[s, r, b * BLOCK : (b + 1) * BLOCK])
                window = slice(b * BLOCK, b * BLOCK + BLOCK + 2 * HALO)
                scores = nt(queries, k[s, r, window])
                allowed = seg[r, b * BLOCK : (b + 1) * BLOCK] == key_rows[r][b : b + 1]
                scores = jnp.where(jnp.concatenate([allowed] * heads, axis=0), scores, MASKED)
                peak = jnp.max(scores, axis=1, keepdims=True)
                raised = jnp.exp(scores - peak)
                weights = (raised / jnp.sum(raised, axis=1, keepdims=True)).astype(jnp.bfloat16)
                probs[s, r * blocks + b] = weights
                context = nn(weights, v[s, r, window])
                o[s, r, b * BLOCK : (b + 1) * BLOCK] = head_pick(context, heads * HDIM).astype(
                    jnp.bfloat16
                )

    def attention(i):
        s = order[i]
        project(s)
        attend(s)

    attention(0)
    step(0)
    core_copy(0).wait_recv()
    step(1)
    attention(1)
    step(2)
    step(3)
    attention(2)
    step(4)
    for c in range(3):
        yc_copy(c).wait_recv()
        xc_copy(c).wait_recv()
    attention(3)
    step(5)
    save(wq, wq_out)
    save(q, q_out)
    save(k, k_out)
    save(v, v_out)
    save(probs, p_out)
    save(o, o_out)

    core_copy(1).wait_recv()
    yc_copy(3).wait_recv()
    xc_copy(3).wait_recv()
    save(wo, wo_out)
    for r in range(rows):
        part = pl.ds(r * region, region)
        y = nn(o[0, r, :region], wo[0].reshape(-1, width))
        for s in range(1, 4):
            y = y + nn(o[s, r, :region], wo[s].reshape(-1, width))
        acc[part] = y

    def first_norm(part):
        values = tok[part].astype(jnp.float32) + acc[part] + b_out[...]
        normed, unit, inv = norm_forward(values, gain1[...], shift1[...])
        n1[part] = unit
        r1[part] = inv
        h1[part] = normed.astype(jnp.bfloat16)
        acc[part] = normed + b_back[...]

    norm_tiles(total, 96, first_norm)
    save(h1, h1_out)
    save(n1, n1_out)
    save(r1, r1_out)
    step(6)

    def raise_units(s):
        for n in range(3):
            columns = slice(n * 256, n * 256 + 256)
            upper[...] = nn(h1[...], wi[s, :, :, :, columns].reshape(width, 256))

            def activate(part):
                u = upper[part] + bi[s, :, columns]
                cdf = 0.5 * (1.0 + lax.erf(u * 0.7071067811865476))
                g[s, part, columns] = (u * cdf).astype(jnp.bfloat16)
                slope = cdf + u * jnp.exp(-0.5 * u * u) * 0.3989422804014327
                gp[s, part, columns] = slope.astype(jnp.bfloat16)

            norm_tiles(total, 96, activate)

    def lower_units(s):
        for r in range(rows):
            part = pl.ds(r * region, region)
            acc[part] = acc[part] + nn(g[s, part], wb[s].reshape(width, width))

    core_copy(2).wait_recv()
    raise_units(order[0])
    step(7)
    lower_units_early = [order[0], order[1]]
    core_copy(3).wait_recv()
    lower_units(lower_units_early[0])
    step(8)
    raise_units(order[1])
    step(9)
    lower_units(lower_units_early[1])
    for c in range(4, 8):
        yc_copy(c).wait_recv()
        xc_copy(c).wait_recv()
    save(wi, wi_out)
    raise_units(order[2])
    step(10)
    raise_units(order[3])
    save(g, g_out)
    save(gp, gp_out)
    step(11)
    step(12)
    lower_units(order[2])
    for c in range(8, 12):
        yc_copy(c).wait_recv()
        xc_copy(c).wait_recv()
    save(wb, wb_out)
    lower_units(order[3])

    def second_norm(part):
        normed, unit, inv = norm_forward(acc[part], gain2[...], shift2[...])
        n2[part] = unit
        r2[part] = inv
        hid[part] = normed.astype(jnp.bfloat16)

    norm_tiles(total, 96, second_norm)
    save(n2, n2_out)
    save(r2, r2_out)

    slots = cls_ref.shape[0] // rows
    for r in range(rows):
        place = lax.broadcasted_iota(jnp.int32, (slots, share), 1)
        pick = place == start_column(lengths_ref, r, first, slots)
        cls_ref[r * slots : (r + 1) * slots] = nn(
            pick.astype(jnp.bfloat16), hid[r * region : r * region + share]
        ).astype(jnp.bfloat16)

    def mask_hidden(part):
        hid[part] = (hid[part].astype(jnp.float32) * own[part]).astype(jnp.bfloat16)

    norm_tiles(total, 96, mask_hidden)
    settled = [
        remote(
            hid.at[pl.ds(r * region + share, HALO)],
            hid_in.at[r],
            halo_sem.at[2, r],
            halo_sem.at[3, r],
            right,
        )
        for r in range(rows)
    ]
    for copy in settled:
        copy.start()
    for copy in settled:
        copy.wait()
    for r in range(rows):
        head = pl.ds(r * region, HALO)
        hid[head] = hid[head] + hid_in[r]
    for r in range(rows):
        save(hid.at[pl.ds(r * region, share)], hidden_hbm.at[r])

    for copy in saves:
        copy.wait()
    for copy in biases:
        copy.wait_send()
    for i in range(4):
        core_copy(i).wait_send()
    for c in range(12):
        y_copy(c).wait_send()
        x_copy(c).wait_send()
        yc_copy(c).wait_send()
        xc_copy(c).wait_send()


class RowView:
    def __init__(self, ref, row):
        self.ref, self.row = ref, row
        self.shape = (1, ref.shape[1])

    def __getitem__(self, index):
        return self.ref[self.row, index[1]]


def forward(tokens, lengths, w_qkv, b_qv, w_out, b_out, ln1, w_in, b_in, w_back, b_back, ln2, dp_size):
    rows, share, width = tokens.shape
    region = share + HALO
    total = rows * region
    blocks = -(-region // BLOCK)
    padded = blocks * BLOCK
    keyed = padded + 2 * HALO
    low, full = jnp.bfloat16, jnp.float32
    head_cols = w_qkv.shape[2]
    slots = 32
    shape = jax.ShapeDtypeStruct
    saved = [
        ((4, 3, 2, width // 2, head_cols), low),
        ((4, 2, head_cols // 2, width), low),
        ((4, 4, 2, width // 8, width), low),
        ((4, 4, 2, width // 8, width), low),
        ((total, width), low),
        ((4, rows, padded, head_cols), low),
        ((4, rows, keyed, head_cols), low),
        ((4, rows, keyed, head_cols), low),
        ((4, rows * blocks, head_cols // HDIM * BLOCK, BLOCK + 2 * HALO), low),
        ((4, rows, padded, head_cols), low),
        ((total, width), low),
        ((total, width), full),
        ((total, 1), full),
        ((4, total, width), low),
        ((4, total, width), low),
        ((total, width), full),
        ((total, 1), full),
        ((total, 1), full),
    ]
    out_shape = [shape((rows, share, width), low), shape((rows * slots, width), low)]
    out_shape += [shape(*item) for item in saved]
    held = [pltpu.VMEM(*item) for item in saved]
    dma = pltpu.SemaphoreType.DMA
    scratch = [held[4]] + held[:4]
    scratch += [pltpu.VMEM((4, 2, head_cols), full), pltpu.VMEM((4, 1, width), full)]
    scratch += held[5:]
    scratch += [
        pltpu.VMEM((total, width), full),
        pltpu.VMEM((total, 256), full),
        pltpu.VMEM((rows, padded, BLOCK + 2 * HALO), full),
        pltpu.VMEM((total, width), low),
        pltpu.VMEM((rows, HALO, width), low),
        dma((rows + 6,)),
        dma((4, rows)),
        dma((3, 2)),
        dma((3, 2)),
        dma((4,)),
        dma((4,)),
        *[dma((12,))] * 8,
        dma((24,)),
    ]
    anywhere = pl.BlockSpec(memory_space=pl.ANY)
    vmem = pl.BlockSpec(memory_space=pltpu.VMEM)
    row = lambda vector: vector.reshape(1, -1)
    return pl.pallas_call(
        lambda *refs: forward_kernel(dp_size, *refs),
        out_shape=out_shape,
        in_specs=[pl.BlockSpec(memory_space=pltpu.SMEM)] + [anywhere] * 7 + [vmem] * 6,
        out_specs=[anywhere, vmem] + [anywhere] * len(saved),
        scratch_shapes=scratch,
        compiler_params=pltpu.CompilerParams(
            collective_id=2, has_side_effects=True, vmem_limit_bytes=64 * 1024 * 1024 - 65536
        ),
        name="forward",
    )(
        lengths,
        tokens,
        w_qkv.reshape(3, 2, width // 2, head_cols),
        w_out.reshape(2, head_cols // 2, width),
        w_in.reshape(4, 2, width // 8, width),
        w_back.reshape(4, 2, width // 8, width),
        b_qv,
        row(b_in),
        row(b_out),
        row(ln1[0]),
        row(ln1[1]),
        row(b_back),
        row(ln2[0]),
        row(ln2[1]),
    )


class Reducer:
    def __init__(self, at, bufs):
        self.at = at
        self.pieces = pieces_of(at.depth)
        self.plane = self.pieces == at.depth
        self.ready = 0
        (
            self.parts,
            self.core_in,
            self.y_in,
            self.x_in,
            self.z_in,
            self.whole,
            self.done,
            self.core_s,
            self.core_r,
            self.y_s,
            self.y_r,
            self.x_s,
            self.x_r,
            self.z_s,
            self.z_r,
            self.za_s,
            self.za_r,
            self.xa_s,
            self.xa_r,
            self.own_s,
            self.out_s,
        ) = bufs

    def core_copy(self, u):
        at = self.at
        return remote(
            self.parts.at[1, :, u],
            self.core_in.at[:, u],
            self.core_s.at[u],
            self.core_r.at[u],
            at.across_core,
        )

    def y_copy(self, u):
        at = self.at
        return remote(
            self.parts.at[0, 1, u],
            self.y_in.at[u],
            self.y_s.at[u],
            self.y_r.at[u],
            at.across_y,
        )

    def x_copy(self, u):
        return remote(
            self.parts.at[0, 0, u, 1],
            self.x_in.at[u],
            self.x_s.at[u],
            self.x_r.at[u],
            self.at.across_x,
        )

    def z_copy(self, u, step):
        at = self.at
        return remote(
            self.parts.at[0, 0, u, 0, (at.z + step) % at.depth],
            self.z_in.at[u, step - 1],
            self.z_s.at[u, step - 1],
            self.z_r.at[u, step - 1],
            at.along_z(step),
        )

    def za_copy(self, u, step):
        at = self.at
        return remote(
            self.done.at[u],
            self.whole.at[u, 0, at.z],
            self.za_s.at[u, step - 1],
            self.za_r.at[u, step - 1],
            at.along_z(step),
        )

    def own_copy(self, u):
        return pltpu.make_async_copy(
            self.done.at[u], self.whole.at[u, 0, self.at.z], self.own_s.at[u]
        )

    def xa_copy(self, u):
        return remote(
            self.whole.at[u, 0],
            self.whole.at[u, 1],
            self.xa_s.at[u],
            self.xa_r.at[u],
            self.at.across_x,
        )

    def out_copies(self, u, out):
        held = self.whole.at[u] if self.plane else self.parts.at[0, 0, u]
        return [
            pltpu.make_async_copy(held.at[0], out.at[u, self.at.x], self.out_s.at[u, 0]),
            pltpu.make_async_copy(held.at[1], out.at[u, 1 - self.at.x], self.out_s.at[u, 1]),
        ]

    def add(self, place, source, at):
        both = self.parts[place].astype(jnp.float32) + source[at].astype(jnp.float32)
        self.parts[place] = both.astype(jnp.bfloat16)

    def start(self, u):
        self.core_copy(u).start()

    def add_far(self, u):
        self.core_copy(u).wait_recv()
        for half in range(2):
            self.add((0, 1, u, half), self.core_in, (1, u, half))
        self.y_copy(u).start()

    def add_near(self, u):
        for half in range(2):
            self.add((0, 0, u, half), self.core_in, (0, u, half))

    def add_y(self, u):
        self.y_copy(u).wait_recv()
        self.add((0, 0, u, 1), self.y_in, (u, 1))
        if self.plane:
            self.x_copy(u).start()
        self.add((0, 0, u, 0), self.y_in, (u, 0))

    def add_x(self, u):
        self.x_copy(u).wait_recv()
        self.add((0, 0, u, 0), self.x_in, (u,))
        for step in range(1, self.at.depth):
            self.z_copy(u, step).start()

    def add_z(self, u):
        at = self.at
        total = self.parts[0, 0, u, 0, at.z].astype(jnp.float32)
        for step in range(1, at.depth):
            self.z_copy(u, step).wait_recv()
            total = total + self.z_in[u, step - 1].astype(jnp.float32)
        self.done[u] = total.astype(jnp.bfloat16)
        for step in range(1, at.depth):
            self.za_copy(u, step).start()
        self.own_copy(u).start()

    def spread_x(self, u):
        self.own_copy(u).wait()
        for step in range(1, self.at.depth):
            self.za_copy(u, step).wait_recv()
        self.xa_copy(u).start()

    def finish(self, u, out):
        if self.plane:
            self.xa_copy(u).wait_recv()
        for copy in self.out_copies(u, out):
            copy.start()

    def drain(self, u, out):
        self.core_copy(u).wait_send()
        self.y_copy(u).wait_send()
        for copy in self.out_copies(u, out):
            copy.wait()
        if not self.plane:
            return
        self.x_copy(u).wait_send()
        self.xa_copy(u).wait_send()
        for step in range(1, self.at.depth):
            self.z_copy(u, step).wait_send()
            self.za_copy(u, step).wait_send()


def pieces_of(depth):
    return depth if UNIT % (16 * depth) == 0 else 4


def reducer_scratch(depth):
    lanes = max(depth - 1, 1)
    depth = pieces_of(depth)
    rows = UNIT // depth
    dma = pltpu.SemaphoreType.DMA
    low = jnp.bfloat16
    return [
        pltpu.VMEM((2, 2, UNITS, 2, depth, rows, 384), low),
        pltpu.VMEM((2, UNITS, 2, depth, rows, 384), low),
        pltpu.VMEM((UNITS, 2, depth, rows, 384), low),
        pltpu.VMEM((UNITS, depth, rows, 384), low),
        pltpu.VMEM((UNITS, lanes if depth == lanes + 1 else 1, rows, 384), low),
        pltpu.VMEM((UNITS, 2, depth, rows, 384), low),
        pltpu.VMEM((UNITS, rows, 384), low),
        *[dma((UNITS,))] * 6,
        *[dma((UNITS, lanes if depth == lanes + 1 else 1))] * 4,
        *[dma((UNITS,))] * 3,
        dma((UNITS, 2)),
    ]


class Ring:
    def __init__(self, slots, sem, sources):
        self.slots, self.sem, self.sources = slots, sem, sources
        self.count = len(slots)
        self.used = 0
        for i in range(min(self.count, len(sources))):
            self.copy(i).start()

    def copy(self, i):
        return pltpu.make_async_copy(
            self.sources[i], self.slots[i % self.count], self.sem.at[i]
        )

    def take(self):
        self.copy(self.used).wait()
        return self.slots[self.used % self.count]

    def free(self):
        ahead = self.used + self.count
        if ahead < len(self.sources):
            self.copy(ahead).start()
        self.used += 1


def backward_kernel(dp_size, *refs):
    (
        lengths_ref,
        cls_grad,
        gain1,
        gain2,
        cot_hbm,
        wq_hbm,
        wo_hbm,
        wi_hbm,
        wb_hbm,
        tok_hbm,
        q_hbm,
        k_hbm,
        v_hbm,
        p_hbm,
        o_hbm,
        h1_hbm,
        n1_hbm,
        r1_hbm,
        g_hbm,
        gp_hbm,
        n2_hbm,
        r2_hbm,
        own_hbm,
        sums_hbm,
        grad_hbm,
        vec_out,
        own,
        cot,
        unit,
        inv1,
        inv2,
        acc,
        df,
        turned,
        h1,
        tok,
        q,
        k,
        v,
        probs,
        o,
        wo,
        w0,
        w1,
        w2,
        wq0,
        wq1,
        g0,
        g1,
        gp0,
        gp1,
        du,
        do,
        dkv,
        dqkv,
        vec,
        vec_in,
        vec_z,
        halo_in,
        load_sem,
        g_sem,
        w_sem,
        gp_sem,
        wq_sem,
        halo_sem,
        vec_s,
        vec_r,
        *bufs,
    ) = refs
    at = Places(dp_size)
    red = Reducer(at, bufs)
    rows, share, width = cot_hbm.shape
    region = share + HALO
    total = rows * region
    m = at.mp
    first = m * share
    left = (at.dp, (m + 3) % 4)
    right = (at.dp, (m + 1) % 4)
    order = (1, 3, 2, 0)
    true_shard = shard_order(at)

    def loading(i, src, dst):
        return pltpu.make_async_copy(src, dst, load_sem.at[i])

    cots = [
        loading(r, cot_hbm.at[r], cot.at[pl.ds(r * region, share)]) for r in range(rows)
    ]
    early = cots + [
        loading(rows + i, src, dst)
        for i, (src, dst) in enumerate(
            [(own_hbm, own), (n2_hbm, unit), (r2_hbm, inv2), (r1_hbm, inv1)]
        )
    ]
    for copy in early:
        copy.start()
    g_ring = Ring((g0, g1), g_sem, [g_hbm.at[s] for s in order])
    w_sources = [ref.at[s] for s in order for ref in (wb_hbm, wi_hbm)]
    w_ring = Ring((w0, w1, w2), w_sem, w_sources)
    gp_ring = Ring((gp0, gp1), gp_sem, [gp_hbm.at[s] for s in order])
    late = [
        loading(rows + 4 + i, src, dst)
        for i, (src, dst) in enumerate(
            [
                (h1_hbm, h1),
                (tok_hbm, tok),
                (o_hbm, o),
                (wo_hbm, wo),
                (q_hbm, q),
                (k_hbm, k),
                (v_hbm, v),
                (p_hbm, probs),
            ]
        )
    ]
    for copy in late:
        copy.start()
    wq_ring = Ring((wq0, wq1), wq_sem, [wq_hbm.at[s] for s in order])

    peers = [(at.dp, (m + j) % 4) for j in range(1, 4)] + [at.across_x]
    greet(peers + [at.along_z(step) for step in range(1, at.depth)])
    halos = [
        remote(
            cot_hbm.at[r, pl.ds(0, HALO)],
            cot.at[pl.ds(r * region + share, HALO)],
            halo_sem.at[0, r],
            halo_sem.at[1, r],
            left,
        )
        for r in range(rows)
    ]
    for copy in halos:
        copy.start()

    def events():
        lag = 3 if red.plane else 0
        for i in range(UNITS + lag):
            if i < UNITS:
                while i >= red.ready:
                    yield None
                yield lambda: red.add_y(i)
            if i >= lag:
                yield lambda: red.finish(i - lag, sums_hbm)
            if red.plane and 2 <= i < UNITS + 2:
                yield lambda: red.spread_x(i - 2)
            if red.plane and 1 <= i < UNITS + 1:
                yield lambda: red.add_z(i - 1)
            if red.plane and i < UNITS:
                yield lambda: red.add_x(i)

    queue = events()

    def pump(count):
        for _ in range(count):
            event = next(queue, None)
            if event is not None:
                event()

    vec[0] = jnp.zeros(vec.shape[1:], jnp.float32)
    slots = cls_grad.shape[0] // rows
    for copy in early:
        copy.wait()
    for copy in halos:
        copy.wait()

    def norm_back(part, grad, gain, inv, base):
        normed, inv_dev = unit[part], inv[part]
        scaled = grad * gain[...]
        centered = scaled - jnp.mean(scaled, axis=-1, keepdims=True)
        inner = jnp.mean(scaled * normed, axis=-1, keepdims=True)
        grad_in = inv_dev * (centered - normed * inner)
        acc[part] = grad_in
        df[part] = grad_in.astype(jnp.bfloat16)
        vec[0, base : base + 1] += jnp.sum(grad_in, axis=0, keepdims=True)
        vec[0, base + 1 : base + 2] += jnp.sum(grad * normed, axis=0, keepdims=True)
        vec[0, base + 2 : base + 3] += jnp.sum(grad, axis=0, keepdims=True)

    tile = 96
    for r in range(rows):
        starts = start_row(lengths_ref, r, first, slots)
        come = cls_grad[r * slots : (r + 1) * slots]
        terms = []
        for _ in range(3):
            term = come.astype(jnp.bfloat16)
            terms.append(term)
            come = come - term.astype(jnp.float32)

        @pl.loop(0, region // tile)
        def _(i):
            part = pl.ds(pl.multiple_of(r * region + i * tile, 32), tile)
            place = i * tile + lax.broadcasted_iota(jnp.int32, (tile, slots), 0)
            hit = (place == starts) & (place < share)
            pick = jnp.where(hit, 1.0, 0.0).astype(jnp.bfloat16)
            grad = cot[part].astype(jnp.float32)
            for term in terms:
                grad = grad + nn(pick, term)
            norm_back(part, grad * own[part], gain2, inv2, 3)

    first_unit = pltpu.make_async_copy(n1_hbm, unit, load_sem.at[1])
    first_unit.start()

    def put(s, u, half, values):
        low = values.astype(jnp.bfloat16)
        for i in range(values.shape[0] // UNIT):
            red.parts[s % 2, s // 2, u + i, half] = low[i * UNIT : (i + 1) * UNIT].reshape(
                red.pieces, UNIT // red.pieces, 384
            )

    def true_half(half):
        return at.x if half == 0 else 1 - at.x

    def true_columns(half):
        return pl.ds(pl.multiple_of(true_half(half) * 384, 128), 384)

    def sent(i, units):
        if i == 1:
            for u in units:
                red.start(u)
        if i == 2:
            for u in units:
                red.add_far(u)
        if i == 3:
            for u in units:
                red.add_near(u)
            red.ready = units[-1] + 1

    for i in range(4):
        g = g_ring.take()
        turned[...] = g[...].T
        g_ring.free()
        for half in range(2):
            put(order[i], 0, half, nn(turned[...], df[:, true_columns(half)]))
        sent(i, range(4))
    late[0].wait()
    turned[...] = h1[...].T
    for i in range(4):
        s = order[i]
        wb = w_ring.take()
        slope = gp_ring.take()
        for half in range(2):
            columns = true_columns(half)
            rows_here = pl.ds(2 * true_half(half), 2)
            rise = nt(df[...], wb[rows_here].reshape(384, width))
            rise = (rise * slope[:, columns].astype(jnp.float32)).astype(jnp.bfloat16)
            du[:, columns] = rise
            vec[0, pl.ds(6 + true_shard[s], 1), columns] = jnp.sum(
                rise.astype(jnp.float32), axis=0, keepdims=True
            )
            put(s, 4, half, nn(turned[...], rise))
        w_ring.free()
        gp_ring.free()
        wi = w_ring.take()
        sent(i, range(4, 8))
        for r in range(rows):
            part = pl.ds(r * region, region)
            acc[part] = acc[part] + nt(du[part], wi[...].reshape(width, width))
        w_ring.free()
        pump(3)

    first_unit.wait()

    @pl.loop(0, total // tile)
    def _(i):
        part = pl.ds(pl.multiple_of(i * tile, tile), tile)
        norm_back(part, acc[part], gain1, inv1, 0)

    for copy in late[1:]:
        copy.wait()
    pump(2)

    heads = q.shape[3] // HDIM
    cols = heads * HDIM
    blocks = q.shape[2] // BLOCK
    for i in range(4):
        s = order[i]
        flat = jnp.concatenate([o[s, r, :region] for r in range(rows)], axis=0)
        for half in range(2):
            put(s, 8, half, tn(flat, df[:, true_columns(half)]))
        sent(i, [8])
    pump(3)
    do[...] = jnp.zeros_like(do)
    for i in range(4):
        s = order[i]
        back = nt(df[...], wo[s].reshape(cols, width)).astype(jnp.bfloat16)
        for r in range(rows):
            do[r, :region] = back[r * region : (r + 1) * region]
        dkv[...] = jnp.zeros_like(dkv)
        for r in range(rows):
            for b in range(blocks):
                here = slice(b * BLOCK, (b + 1) * BLOCK)
                window = slice(b * BLOCK, b * BLOCK + BLOCK + 2 * HALO)
                grads = head_stack(do[r, here])
                queries = head_stack(q[s, r, here])
                weight = probs[s, r * blocks + b]
                wide = weight.astype(jnp.float32)
                rise = nt(grads, v[s, r, window])
                inner = jnp.sum(wide * rise, axis=1, keepdims=True)
                fall = (wide * (rise - inner)).astype(jnp.bfloat16)
                dq = head_pick(nn(fall, k[s, r, window]), cols) * 0.125
                valid = min(region - b * BLOCK, BLOCK)
                dqkv[0, r * region + b * BLOCK : r * region + b * BLOCK + valid] = dq[
                    :valid
                ].astype(jnp.bfloat16)
                dkv[0, r, window] += tn(fall, queries)
                dkv[1, r, window] += tn(weight, grads)
        for r in range(rows):
            for t in range(2):
                dqkv[1 + t, r * region : (r + 1) * region] = dkv[
                    t, r, HALO : HALO + region
                ].astype(jnp.bfloat16)
        wqs = wq_ring.take()
        for t, lane in ((0, 0), (1, None), (2, 256)):
            part = dqkv[t]
            if lane is not None:
                vec[0, pl.ds(10 + true_shard[s], 1), lane : lane + cols] = jnp.sum(
                    part.astype(jnp.float32), axis=0, keepdims=True
                )
            for half in range(2):
                put(s, 9 + t, half, tn(part, tok[:, true_columns(half)]))
            acc[...] += nt(part, wqs[t].reshape(width, cols))
        wq_ring.free()
        sent(i, range(9, 12))
        pump(5)

    def mask_grad(part):
        acc[part] = acc[part] * own[part]

    norm_tiles(total, tile, mask_grad)
    settled = [
        remote(
            acc.at[pl.ds(r * region + share, HALO)],
            halo_in.at[r],
            halo_sem.at[2, r],
            halo_sem.at[3, r],
            right,
        )
        for r in range(rows)
    ]
    for copy in settled:
        copy.start()

    def vec_copy(i):
        device = (at.across_core, at.across_y, at.across_x)[i]
        return remote(vec.at[i], vec_in.at[i], vec_s.at[i], vec_r.at[i], device)

    def vec_z_copy(step):
        index = 2 + step
        return remote(
            vec.at[3], vec_z.at[step], vec_s.at[index], vec_r.at[index], at.along_z(step)
        )

    vec_copy(0).start()
    pump(2)
    grads = []
    for copy in settled:
        copy.wait()
    for r in range(rows):
        head = pl.ds(r * region, HALO)
        acc[head] = acc[head] + halo_in[r]
    for r in range(rows):
        copy = loading(r, acc.at[pl.ds(r * region, share)], grad_hbm.at[r])
        copy.start()
        grads.append(copy)
    for i in range(3):
        vec_copy(i).wait_recv()
        both = vec[i] + vec_in[i]
        if i < 2:
            vec[i + 1] = both
            vec_copy(i + 1).start()
        else:
            vec[3] = both
            vec_z[0] = both
            for step in range(1, at.depth):
                vec_z_copy(step).start()
        pump(4)
    for step in range(1, at.depth):
        vec_z_copy(step).wait_recv()
    both = vec_z[at.back_z(0)]
    for z in range(1, at.depth):
        both = both + vec_z[at.back_z(z)]
    vec_out[...] = both
    for event in queue:
        event()
    for copy in grads:
        copy.wait()
    for i in range(3):
        vec_copy(i).wait_send()
    for step in range(1, at.depth):
        vec_z_copy(step).wait_send()

    @pl.loop(0, UNITS)
    def _(u):
        red.drain(u, sums_hbm)


def start_row(lengths_ref, row, first, slots):
    slot = lax.broadcasted_iota(jnp.int32, (1, slots), 1)

    def body(j, carry):
        line, begin = carry
        return (jnp.where(slot == j, begin - first, line), begin + lengths_ref[row, j])

    line, _ = lax.fori_loop(
        0, lengths_ref.shape[1], body, (jnp.full((1, slots), -1, jnp.int32), jnp.int32(0))
    )
    return line


def backward(lengths, cls_grad, gain1, gain2, cotangent, saved, dp_size):
    rows, share, width = cotangent.shape
    region = share + HALO
    total = rows * region
    q, k, probs, o = saved[5], saved[6], saved[8], saved[9]
    depth = dp_size // 2
    low, full = jnp.bfloat16, jnp.float32
    cols = q.shape[3]
    dma = pltpu.SemaphoreType.DMA
    vmem = pltpu.VMEM
    scratch = [
        vmem((total, 1), full),
        vmem((total, width), low),
        vmem((total, width), full),
        vmem((total, 1), full),
        vmem((total, 1), full),
        vmem((total, width), full),
        vmem((total, width), low),
        vmem((width, total), low),
        vmem((total, width), low),
        vmem((total, width), low),
        vmem(q.shape, low),
        vmem(k.shape, low),
        vmem(k.shape, low),
        vmem(probs.shape, low),
        vmem(o.shape, low),
        vmem(saved[1].shape, low),
        *[vmem(saved[2].shape[1:], low)] * 3,
        *[vmem(saved[0].shape[1:], low)] * 2,
        *[vmem((total, width), low)] * 4,
        vmem((total, width), low),
        vmem(q.shape[1:], low),
        vmem((2, *k.shape[1:]), full),
        vmem((3, total, cols), low),
        vmem((4, 16, width), full),
        vmem((3, 16, width), full),
        vmem((depth, 16, width), full),
        vmem((rows, HALO, width), full),
        dma((rows + 12,)),
        *[dma((8,))] * 4,
        dma((4, rows)),
        dma((2 + depth,)),
        dma((2 + depth,)),
    ] + reducer_scratch(depth)
    anywhere = pl.BlockSpec(memory_space=pl.ANY)
    in_vmem = pl.BlockSpec(memory_space=pltpu.VMEM)
    shape = jax.ShapeDtypeStruct
    return pl.pallas_call(
        lambda *refs: backward_kernel(dp_size, *refs),
        out_shape=[
            shape((UNITS, 2, pieces_of(depth), UNIT // pieces_of(depth), 384), low),
            shape((rows, share, width), full),
            shape((16, width), full),
        ],
        in_specs=[pl.BlockSpec(memory_space=pltpu.SMEM)] + [in_vmem] * 3 + [anywhere] * 19,
        out_specs=[anywhere, anywhere, in_vmem],
        scratch_shapes=scratch,
        compiler_params=pltpu.CompilerParams(
            collective_id=1, has_side_effects=True, vmem_limit_bytes=64 * 1024 * 1024 - 65536
        ),
        name="backward",
    )(lengths, cls_grad, gain1.reshape(1, -1), gain2.reshape(1, -1), cotangent, *saved)


def shards(
    tokens,
    lengths,
    view_masks,
    w_qkv,
    b_qv,
    w_out,
    b_out,
    ln1_gain,
    ln1_bias,
    w_in,
    b_in,
    w_back,
    b_back,
    ln2_gain,
    ln2_bias,
    w_pool,
    b_pool,
    cotangent,
):
    rows, share, width = tokens.shape
    hidden, cls_part, *saved = forward(
        tokens, lengths, w_qkv, b_qv, w_out, b_out, (ln1_gain, ln1_bias), w_in, b_in, w_back,
        b_back, (ln2_gain, ln2_bias), lax.axis_size("dp"),
    )
    cls_rows = cls_part.reshape(rows, -1, width)[:, : lengths.shape[1]]
    cls_rows = lax.psum(cls_rows, "mp").astype(jnp.float32)
    loss, w_pool_grad, b_pool_grad, cls_grad = contrast(
        cls_rows.reshape(-1, width), view_masks, w_pool, b_pool
    )
    cls_grad = cls_grad.reshape(rows, -1, width)
    cls_grad = jnp.pad(cls_grad, [(0, 0), (0, 32 - cls_grad.shape[1]), (0, 0)])
    ranks = lax.axis_size("dp")
    sums, token_grad, vectors = backward(
        lengths, cls_grad.reshape(-1, width), ln1_gain, ln2_gain, cotangent, saved, ranks
    )
    if pieces_of(ranks // 2) != ranks // 2:
        sums = lax.psum(sums, "dp")
    sums = sums.transpose(0, 2, 3, 1, 4).reshape(UNITS, UNIT, width).astype(jnp.float32)
    own = lax.axis_index("mp")
    cols = b_qv.shape[1]
    own_qv = lax.dynamic_slice_in_dim(vectors, 10 + own, 1, axis=0)
    own_in = lax.dynamic_slice_in_dim(vectors, 6 + own, 1, axis=0)
    return (
        hidden,
        loss,
        token_grad,
        sums[9:12].transpose(0, 2, 1),
        jnp.concatenate([own_qv[:, :cols], own_qv[:, 256 : 256 + cols]], axis=0),
        sums[8],
        vectors[0],
        vectors[1],
        vectors[2],
        sums[4:8].reshape(width, width),
        own_in[0],
        sums[0:4].reshape(width, width),
        vectors[3],
        vectors[4],
        vectors[5],
        w_pool_grad,
        b_pool_grad,
    )


def solution(mesh):
    in_specs = (
        P("dp", "mp", None),
        P("dp", None),
        P("dp", None, None, None),
        P(None, None, "mp"),
        P(None, "mp"),
        P("mp", None),
        P(),
        P(),
        P(),
        P(None, "mp"),
        P("mp"),
        P("mp", None),
        P(),
        P(),
        P(),
        P(),
        P(),
        P("dp", "mp", None),
    )
    out_specs = (
        P("dp", "mp", None),
        P(),
        P("dp", "mp", None),
        P(None, None, "mp"),
        P(None, "mp"),
        P("mp", None),
        P(),
        P(),
        P(),
        P(None, "mp"),
        P("mp"),
        P("mp", None),
        P(),
        P(),
        P(),
        P(),
        P(),
    )
    return jax.shard_map(shards, mesh=mesh, in_specs=in_specs, out_specs=out_specs, check_vma=False)
```

```python
import jax
import jax.numpy as jnp
from jax import lax
from jax.experimental import pallas as pl
from jax.experimental.pallas import tpu as pltpu
from jax.sharding import PartitionSpec as P

HDIM = 64
HALO = 32
BLOCK = 64
KEEP_SCALE = 1.0 / 0.9
MASKED = -1000000000.0


def norm_forward(values, gain, shift):
    center = values - jnp.mean(values, axis=-1, keepdims=True)
    inv_dev = lax.rsqrt(jnp.mean(center * center, axis=-1, keepdims=True) + 1e-12)
    normed = center * inv_dev
    return (normed * gain + shift, normed, inv_dev)


def dot32(equation, left, right):
    return jnp.einsum(equation, left, right, preferred_element_type=jnp.float32)


def contrast(cls_rows, view_masks, w_pool, b_pool):
    local_sents = cls_rows.shape[0]
    own_ids = lax.axis_index("dp") * local_sents + jnp.arange(local_sents, dtype=jnp.int32)
    keep_masks = view_masks.astype(jnp.float32).reshape(local_sents, 2, -1)
    views = (cls_rows[:, None, :] * keep_masks * KEEP_SCALE).astype(jnp.bfloat16)
    pooled = jnp.tanh(dot32("svd,de->sve", views, w_pool) + b_pool)
    inv_length = lax.rsqrt(jnp.sum(pooled * pooled, axis=-1, keepdims=True) + 1e-06)
    unit = pooled * inv_length
    unit_low = unit.astype(jnp.bfloat16)
    anchors = unit_low[:, 0]
    every_target = lax.all_gather(unit_low[:, 1], "dp", axis=0, tiled=True)
    logits = dot32("sd,td->st", anchors, every_target) * 20.0
    sent_ids = jnp.arange(every_target.shape[0], dtype=jnp.int32)
    is_partner = sent_ids[None, :] == own_ids[:, None]
    row_peak = jnp.max(logits, axis=1, keepdims=True)
    raised = jnp.exp(logits - row_peak)
    row_total = jnp.sum(raised, axis=1, keepdims=True)
    log_total = row_peak[:, 0] + jnp.log(row_total[:, 0])
    loss_local = jnp.sum(log_total - jnp.sum(jnp.where(is_partner, logits, 0.0), axis=1))
    logit_grad = (raised / row_total - is_partner.astype(jnp.float32)).astype(jnp.bfloat16)
    anchor_grad = dot32("st,td->sd", logit_grad, every_target) * 20.0
    target_terms = dot32("st,sd->td", logit_grad, anchors) * 20.0
    target_grad = lax.psum_scatter(target_terms, "dp", scatter_dimension=0, tiled=True)
    unit_grad = jnp.stack([anchor_grad, target_grad], axis=1)
    pooled_grad = inv_length * (
        unit_grad - unit * jnp.sum(unit_grad * unit, axis=-1, keepdims=True)
    )
    before_grad = (pooled_grad * (1.0 - pooled * pooled)).astype(jnp.bfloat16)
    w_pool_grad = dot32("svd,sve->de", views, before_grad)
    b_pool_grad = jnp.sum(before_grad, axis=(0, 1), dtype=jnp.float32)
    view_grad = dot32("sve,de->svd", before_grad, w_pool)
    cls_grad = jnp.sum(view_grad * keep_masks, axis=1) * KEEP_SCALE
    sums = lax.psum((w_pool_grad, b_pool_grad, loss_local), "dp")
    loss = sums[2] / (local_sents * lax.axis_size("dp"))
    return (loss, sums[0], sums[1], cls_grad)


MESH = pl.DeviceIdType.MESH
UNIT = 192
UNITS = 12


def greet(peers):
    barrier = pltpu.get_barrier_semaphore()
    for peer in peers:
        pl.semaphore_signal(barrier, inc=1, device_id=peer, device_id_type=MESH)
    pl.semaphore_wait(barrier, len(peers))


class Places:
    def __init__(self, dp_size):
        self.dp = lax.axis_index("dp")
        self.mp = lax.axis_index("mp")
        self.core = self.mp % 2
        self.y = self.mp // 2
        self.x = self.dp % 2
        self.z = self.dp // 2
        self.depth = dp_size // 2
        self.across_core = (self.dp, self.y * 2 + (1 - self.core))
        self.across_y = (self.dp, (1 - self.y) * 2 + self.core)
        self.across_both = (self.dp, (1 - self.y) * 2 + (1 - self.core))
        self.across_x = (self.z * 2 + (1 - self.x), self.mp)

    def along_z(self, step):
        return ((self.z + step) % self.depth * 2 + self.x, self.mp)

    def back_z(self, step):
        return (self.z + self.depth - step) % self.depth


def remote(src, dst, send_sem, recv_sem, device):
    return pltpu.make_async_remote_copy(
        src_ref=src,
        dst_ref=dst,
        send_sem=send_sem,
        recv_sem=recv_sem,
        device_id=device,
        device_id_type=MESH,
    )


def norm_tiles(count, tile, body):
    @pl.loop(0, count // tile)
    def _(i):
        body(pl.ds(pl.multiple_of(i * tile, tile), tile))


def row_marks(lengths_ref, local, first, share, region):
    rows, sents = lengths_ref.shape
    row_id = lax.broadcasted_iota(jnp.int32, local.shape, 0)
    places = local + first

    def per_row(values):
        out = jnp.full(local.shape, values[-1], jnp.int32)
        for r in range(rows - 1):
            out = jnp.where(row_id == r, values[r], out)
        return out

    def body(j, carry):
        passed, begun, ends = carry
        ends = tuple(ends[r] + lengths_ref[r, j] for r in range(rows))
        edge = per_row(ends)
        reached = places >= edge
        return (
            passed + reached.astype(jnp.int32),
            jnp.where(reached, edge, begun),
            ends,
        )

    zero = jnp.zeros(local.shape, jnp.int32)
    start = tuple(jnp.int32(0) for _ in range(rows))
    passed, begun, ends = lax.fori_loop(0, sents, body, (zero, zero, start))
    inside = places < per_row(ends)
    here = (local >= 0) & (local < region)
    segment = jnp.where(here, jnp.where(inside, passed, places + sents), -2)
    begins = (begun >= first) & (begun < first + share)
    owned = here & ((inside & begins) | (~inside & (local < share)))
    return (segment, owned)


def start_column(lengths_ref, row, first, slots):
    slot = lax.broadcasted_iota(jnp.int32, (slots, 1), 0)

    def body(j, carry):
        column, begin = carry
        column = jnp.where(slot == j, begin - first, column)
        return (column, begin + lengths_ref[row, j])

    column, _ = lax.fori_loop(
        0, lengths_ref.shape[1], body, (jnp.full((slots, 1), -1, jnp.int32), jnp.int32(0))
    )
    return column


def head_stack(values):
    lane = lax.broadcasted_iota(jnp.int32, values.shape, 1) // HDIM
    zero = jnp.zeros_like(values)
    return jnp.concatenate(
        [jnp.where(lane == h, values, zero) for h in range(values.shape[1] // HDIM)], axis=0
    )


def head_pick(stacked, width):
    heads = width // HDIM
    rows = stacked.shape[0] // heads
    lane = lax.broadcasted_iota(jnp.int32, (rows, width), 1) // HDIM
    out = stacked[:rows]
    for h in range(1, heads):
        out = jnp.where(lane == h, stacked[h * rows : (h + 1) * rows], out)
    return out


def nn(left, right):
    return jnp.dot(left, right, preferred_element_type=jnp.float32)


def nt(left, right):
    return lax.dot_general(
        left, right, (((1,), (1,)), ((), ())), preferred_element_type=jnp.float32
    )


def tn(left, right):
    return lax.dot_general(
        left, right, (((0,), (0,)), ((), ())), preferred_element_type=jnp.float32
    )


def shard_order(at):
    return [
        at.mp,
        at.y * 2 + (1 - at.core),
        (1 - at.y) * 2 + at.core,
        (1 - at.y) * 2 + (1 - at.core),
    ]


def forward_kernel(dp_size, gathers, *refs):
    (
        lengths_ref,
        tokens_hbm,
        wq_hbm,
        wo_hbm,
        wi_hbm,
        wb_hbm,
        bq_hbm,
        bi_hbm,
        masks_hbm,
        b_out,
        gain1,
        shift1,
        b_back,
        gain2,
        shift2,
        hidden_hbm,
        cls_ref,
        wq_out,
        wo_out,
        wi_out,
        wb_out,
        tok_out,
        q_out,
        k_out,
        v_out,
        p_out,
        o_out,
        h1_out,
        n1_out,
        r1_out,
        g_out,
        gp_out,
        n2_out,
        r2_out,
        own_out,
        masks_out,
        tok,
        wq,
        wo,
        wi,
        wb,
        bq,
        bi,
        q,
        k,
        v,
        probs,
        o,
        h1,
        n1,
        r1,
        g,
        gp,
        n2,
        r2,
        own,
        acc,
        upper,
        seg,
        hid,
        hid_in,
        local_sem,
        halo_sem,
        bias_s,
        bias_r,
        core_s,
        core_r,
        y_s,
        y_r,
        x_s,
        x_r,
        yc_s,
        yc_r,
        xc_s,
        xc_r,
        out_sem,
        mask_s,
        mask_r,
    ) = refs
    at = Places(dp_size)
    rows, share, width = tokens_hbm.shape
    region = share + HALO
    total = rows * region
    m = at.mp
    first = m * share
    left = (at.dp, (m + 3) % 4)
    right = (at.dp, (m + 1) % 4)
    order = range(4)
    chunks = (
        [(wq, wq_hbm, (t,)) for t in range(3)]
        + [(wo, wo_hbm, ())]
        + [(wi, wi_hbm, (b,)) for b in range(4)]
        + [(wb, wb_hbm, (b,)) for b in range(4)]
    )
    whole = [(wq, wq_hbm), (wo, wo_hbm), (wi, wi_hbm), (wb, wb_hbm)]

    peers = [(at.dp, (m + j) % 4) for j in range(1, 4)] + [at.across_x]
    greet(peers + [at.along_z(step) for step in range(1, at.depth if gathers else 1)])

    loads = [
        pltpu.make_async_copy(tokens_hbm.at[r], tok.at[pl.ds(r * region, share)], local_sem.at[r])
        for r in range(rows)
    ]
    loads += [
        pltpu.make_async_copy(src, dst.at[0], local_sem.at[rows + i])
        for i, (dst, src) in enumerate(whole + [(bq, bq_hbm), (bi, bi_hbm)])
    ]
    for load in loads:
        load.start()
    halos = [
        remote(
            tokens_hbm.at[r, pl.ds(0, HALO)],
            tok.at[pl.ds(r * region + share, HALO)],
            halo_sem.at[0, r],
            halo_sem.at[1, r],
            left,
        )
        for r in range(rows)
    ]
    for copy in halos:
        copy.start()
    biases = []
    for j, device in enumerate((at.across_core, at.across_y, at.across_both), start=1):
        for i, (dst, src) in enumerate([(bq, bq_hbm), (bi, bi_hbm)]):
            biases.append(
                remote(src, dst.at[j], bias_s.at[j - 1, i], bias_r.at[j - 1, i], device)
            )
    for copy in biases:
        copy.start()

    def core_copy(i):
        dst, src = whole[i]
        return remote(src, dst.at[1], core_s.at[i], core_r.at[i], at.across_core)

    def y_copy(c):
        dst, src, index = chunks[c]
        place = (*index, at.x)
        return remote(src.at[place], dst.at[(2, *place)], y_s.at[c], y_r.at[c], at.across_y)

    def x_copy(c):
        ref = chunks[c][0].at[(2, *chunks[c][2], at.x)]
        return remote(ref, ref, x_s.at[c], x_r.at[c], at.across_x)

    def yc_copy(c):
        ref, _, index = chunks[c]
        place = (*index, at.x)
        return remote(
            ref.at[(2, *place)], ref.at[(3, *place)], yc_s.at[c], yc_r.at[c], at.across_core
        )

    def xc_copy(c):
        ref, _, index = chunks[c]
        place = (*index, 1 - at.x)
        return remote(
            ref.at[(2, *place)], ref.at[(3, *place)], xc_s.at[c], xc_r.at[c], at.across_core
        )

    mask_hops = []
    if gathers:
        piece = masks_out.at[at.z, at.x, at.core]
        mask_along = [
            remote(
                masks_hbm.at[at.core], piece, mask_s.at[step], mask_r.at[step], at.along_z(step)
            )
            for step in range(1, at.depth)
        ]
        mask_own = pltpu.make_async_copy(masks_hbm.at[at.core], piece, mask_s.at[0])
        mask_own.start()
        for copy in mask_along:
            copy.start()
        for i, (part, device) in enumerate(
            [
                (masks_out.at[:, at.x, at.core], at.across_x),
                (masks_out.at[:, :, at.core], at.across_core),
            ]
        ):
            index = at.depth + i
            mask_hops.append(remote(part, part, mask_s.at[index], mask_r.at[index], device))

    def pass_masks(stage):
        if not gathers:
            return
        if stage == 0:
            mask_own.wait()
            for copy in mask_along:
                copy.wait_recv()
        else:
            mask_hops[stage - 1].wait_recv()
        if stage < 2:
            mask_hops[stage].start()

    for c in range(12):
        y_copy(c).start()
    for i in range(4):
        core_copy(i).start()

    def step(c):
        if c < 12:
            y_copy(c).wait_recv()
            x_copy(c).start()
            yc_copy(c).start()
        if c > 0:
            x_copy(c - 1).wait_recv()
            xc_copy(c - 1).start()

    saves = []

    def save(src, dst):
        copy = pltpu.make_async_copy(src, dst, out_sem.at[len(saves)])
        copy.start()
        saves.append(copy)

    lane = lax.broadcasted_iota(jnp.int32, (8, 384), 1)
    segment, owned = row_marks(lengths_ref, lane, first, share, region)
    seg_cols = segment.astype(jnp.float32).T
    own_cols = owned.astype(jnp.float32).T
    for r in range(rows):
        seg[r] = jnp.broadcast_to(seg_cols[: seg.shape[1], r : r + 1], seg.shape[1:])
        own[pl.ds(r * region, region)] = own_cols[:region, r : r + 1]
    save(own, own_out)
    key_rows = []
    for r in range(rows):
        block = lax.broadcasted_iota(jnp.int32, (8, BLOCK + 2 * HALO), 0)
        offset = lax.broadcasted_iota(jnp.int32, (8, BLOCK + 2 * HALO), 1)
        keys, _ = row_marks(
            RowView(lengths_ref, r), block * BLOCK + offset - HALO, first, share, region
        )
        key_rows.append(keys.astype(jnp.float32))
    blocks = q.shape[2] // BLOCK

    q[...] = jnp.zeros_like(q)
    k[...] = jnp.zeros_like(k)
    v[...] = jnp.zeros_like(v)

    for load in loads:
        load.wait()
    for copy in halos:
        copy.wait()
    for copy in biases:
        copy.wait_recv()
    save(tok, tok_out)

    def project(s):
        x = tok[...]
        for t, dst in enumerate((q, k, v)):
            y = nn(x, wq[s, t].reshape(width, -1))
            if t == 0:
                y = (y + bq[s, 0:1]).astype(jnp.bfloat16) * jnp.bfloat16(0.125)
            elif t == 1:
                y = y.astype(jnp.bfloat16)
            else:
                y = (y + bq[s, 1:2]).astype(jnp.bfloat16)
            lead = 0 if t == 0 else HALO
            for r in range(rows):
                dst[s, r, lead : lead + region] = y[r * region : (r + 1) * region]

    def attend(s):
        heads = q.shape[3] // HDIM
        for r in range(rows):
            for b in range(blocks):
                queries = head_stack(q[s, r, b * BLOCK : (b + 1) * BLOCK])
                window = slice(b * BLOCK, b * BLOCK + BLOCK + 2 * HALO)
                scores = nt(queries, k[s, r, window])
                allowed = seg[r, b * BLOCK : (b + 1) * BLOCK] == key_rows[r][b : b + 1]
                scores = jnp.where(jnp.concatenate([allowed] * heads, axis=0), scores, MASKED)
                peak = jnp.max(scores, axis=1, keepdims=True)
                raised = jnp.exp(scores - peak)
                weights = (raised / jnp.sum(raised, axis=1, keepdims=True)).astype(jnp.bfloat16)
                probs[s, r * blocks + b] = weights
                context = nn(weights, v[s, r, window])
                o[s, r, b * BLOCK : (b + 1) * BLOCK] = head_pick(context, heads * HDIM).astype(
                    jnp.bfloat16
                )

    def attention(i):
        s = order[i]
        project(s)
        attend(s)

    attention(0)
    step(0)
    core_copy(0).wait_recv()
    step(1)
    attention(1)
    step(2)
    step(3)
    attention(2)
    step(4)
    pass_masks(0)
    for c in range(3):
        yc_copy(c).wait_recv()
        xc_copy(c).wait_recv()
    attention(3)
    step(5)
    save(wq, wq_out)
    save(q, q_out)
    save(k, k_out)
    save(v, v_out)
    save(probs, p_out)
    save(o, o_out)

    core_copy(1).wait_recv()
    yc_copy(3).wait_recv()
    xc_copy(3).wait_recv()
    save(wo, wo_out)
    for r in range(rows):
        part = pl.ds(r * region, region)
        y = nn(o[0, r, :region], wo[0].reshape(-1, width))
        for s in range(1, 4):
            y = y + nn(o[s, r, :region], wo[s].reshape(-1, width))
        acc[part] = y

    def first_norm(part):
        values = tok[part].astype(jnp.float32) + acc[part] + b_out[...]
        normed, unit, inv = norm_forward(values, gain1[...], shift1[...])
        n1[part] = unit
        r1[part] = inv
        h1[part] = normed.astype(jnp.bfloat16)
        acc[part] = normed + b_back[...]

    norm_tiles(total, 96, first_norm)
    save(h1, h1_out)
    save(n1, n1_out)
    save(r1, r1_out)
    step(6)

    def raise_units(s):
        for n in range(3):
            columns = slice(n * 256, n * 256 + 256)
            upper[...] = nn(h1[...], wi[s, :, :, :, columns].reshape(width, 256))

            def activate(part):
                u = upper[part] + bi[s, :, columns]
                cdf = 0.5 * (1.0 + lax.erf(u * 0.7071067811865476))
                g[s, part, columns] = (u * cdf).astype(jnp.bfloat16)
                slope = cdf + u * jnp.exp(-0.5 * u * u) * 0.3989422804014327
                gp[s, part, columns] = slope.astype(jnp.bfloat16)

            norm_tiles(total, 96, activate)

    def lower_units(s):
        for r in range(rows):
            part = pl.ds(r * region, region)
            acc[part] = acc[part] + nn(g[s, part], wb[s].reshape(width, width))

    core_copy(2).wait_recv()
    raise_units(order[0])
    step(7)
    lower_units_early = [order[0], order[1]]
    core_copy(3).wait_recv()
    lower_units(lower_units_early[0])
    step(8)
    pass_masks(1)
    raise_units(order[1])
    step(9)
    lower_units(lower_units_early[1])
    for c in range(4, 8):
        yc_copy(c).wait_recv()
        xc_copy(c).wait_recv()
    save(wi, wi_out)
    raise_units(order[2])
    step(10)
    raise_units(order[3])
    save(g, g_out)
    save(gp, gp_out)
    step(11)
    step(12)
    lower_units(order[2])
    pass_masks(2)
    for c in range(8, 12):
        yc_copy(c).wait_recv()
        xc_copy(c).wait_recv()
    save(wb, wb_out)
    lower_units(order[3])

    def second_norm(part):
        normed, unit, inv = norm_forward(acc[part], gain2[...], shift2[...])
        n2[part] = unit
        r2[part] = inv
        hid[part] = normed.astype(jnp.bfloat16)

    norm_tiles(total, 96, second_norm)
    save(n2, n2_out)
    save(r2, r2_out)

    slots = cls_ref.shape[0] // rows
    for r in range(rows):
        place = lax.broadcasted_iota(jnp.int32, (slots, share), 1)
        pick = place == start_column(lengths_ref, r, first, slots)
        cls_ref[r * slots : (r + 1) * slots] = nn(
            pick.astype(jnp.bfloat16), hid[r * region : r * region + share]
        ).astype(jnp.bfloat16)

    def mask_hidden(part):
        hid[part] = (hid[part].astype(jnp.float32) * own[part]).astype(jnp.bfloat16)

    norm_tiles(total, 96, mask_hidden)
    settled = [
        remote(
            hid.at[pl.ds(r * region + share, HALO)],
            hid_in.at[r],
            halo_sem.at[2, r],
            halo_sem.at[3, r],
            right,
        )
        for r in range(rows)
    ]
    for copy in settled:
        copy.start()
    for copy in settled:
        copy.wait()
    for r in range(rows):
        head = pl.ds(r * region, HALO)
        hid[head] = hid[head] + hid_in[r]
    for r in range(rows):
        save(hid.at[pl.ds(r * region, share)], hidden_hbm.at[r])

    for copy in saves:
        copy.wait()
    for copy in biases + mask_hops + (mask_along if gathers else []):
        copy.wait_send()
    for i in range(4):
        core_copy(i).wait_send()
    for c in range(12):
        y_copy(c).wait_send()
        x_copy(c).wait_send()
        yc_copy(c).wait_send()
        xc_copy(c).wait_send()


class RowView:
    def __init__(self, ref, row):
        self.ref, self.row = ref, row
        self.shape = (1, ref.shape[1])

    def __getitem__(self, index):
        return self.ref[self.row, index[1]]


def forward(tokens, lengths, w_qkv, b_qv, w_out, b_out, ln1, w_in, b_in, w_back, b_back, ln2, masks,
            dp_size, gathers):
    rows, share, width = tokens.shape
    region = share + HALO
    total = rows * region
    blocks = -(-region // BLOCK)
    padded = blocks * BLOCK
    keyed = padded + 2 * HALO
    low, full = jnp.bfloat16, jnp.float32
    head_cols = w_qkv.shape[2]
    slots = 32
    shape = jax.ShapeDtypeStruct
    saved = [
        ((4, 3, 2, width // 2, head_cols), low),
        ((4, 2, head_cols // 2, width), low),
        ((4, 4, 2, width // 8, width), low),
        ((4, 4, 2, width // 8, width), low),
        ((total, width), low),
        ((4, rows, padded, head_cols), low),
        ((4, rows, keyed, head_cols), low),
        ((4, rows, keyed, head_cols), low),
        ((4, rows * blocks, head_cols // HDIM * BLOCK, BLOCK + 2 * HALO), low),
        ((4, rows, padded, head_cols), low),
        ((total, width), low),
        ((total, width), full),
        ((total, 1), full),
        ((4, total, width), low),
        ((4, total, width), low),
        ((total, width), full),
        ((total, 1), full),
        ((total, 1), full),
    ]
    out_shape = [shape((rows, share, width), low), shape((rows * slots, width), low)]
    out_shape += [shape(*item) for item in saved]
    out_shape += [shape((dp_size // 2, 2, *masks.shape) if gathers else (8, 128), low)]
    held = [pltpu.VMEM(*item) for item in saved]
    dma = pltpu.SemaphoreType.DMA
    scratch = [held[4]] + held[:4]
    scratch += [pltpu.VMEM((4, 2, head_cols), full), pltpu.VMEM((4, 1, width), full)]
    scratch += held[5:]
    scratch += [
        pltpu.VMEM((total, width), full),
        pltpu.VMEM((total, 256), full),
        pltpu.VMEM((rows, padded, BLOCK + 2 * HALO), full),
        pltpu.VMEM((total, width), low),
        pltpu.VMEM((rows, HALO, width), low),
        dma((rows + 6,)),
        dma((4, rows)),
        dma((3, 2)),
        dma((3, 2)),
        dma((4,)),
        dma((4,)),
        *[dma((12,))] * 8,
        dma((24,)),
        dma((dp_size // 2 + 2,)),
        dma((dp_size // 2 + 2,)),
    ]
    anywhere = pl.BlockSpec(memory_space=pl.ANY)
    vmem = pl.BlockSpec(memory_space=pltpu.VMEM)
    row = lambda vector: vector.reshape(1, -1)
    return pl.pallas_call(
        lambda *refs: forward_kernel(dp_size, gathers, *refs),
        out_shape=out_shape,
        in_specs=[pl.BlockSpec(memory_space=pltpu.SMEM)] + [anywhere] * 8 + [vmem] * 6,
        out_specs=[anywhere, vmem] + [anywhere] * (len(saved) + 1),
        scratch_shapes=scratch,
        compiler_params=pltpu.CompilerParams(
            collective_id=2, has_side_effects=True, vmem_limit_bytes=64 * 1024 * 1024 - 65536
        ),
        name="forward",
    )(
        lengths,
        tokens,
        w_qkv.reshape(3, 2, width // 2, head_cols),
        w_out.reshape(2, head_cols // 2, width),
        w_in.reshape(4, 2, width // 8, width),
        w_back.reshape(4, 2, width // 8, width),
        b_qv,
        row(b_in),
        masks,
        row(b_out),
        row(ln1[0]),
        row(ln1[1]),
        row(b_back),
        row(ln2[0]),
        row(ln2[1]),
    )


class Reducer:
    def __init__(self, at, bufs):
        self.at = at
        self.pieces = pieces_of(at.depth)
        self.plane = self.pieces == at.depth
        self.ready = 0
        (
            self.parts,
            self.core_in,
            self.y_in,
            self.x_in,
            self.z_in,
            self.whole,
            self.done,
            self.core_s,
            self.core_r,
            self.y_s,
            self.y_r,
            self.x_s,
            self.x_r,
            self.z_s,
            self.z_r,
            self.za_s,
            self.za_r,
            self.xa_s,
            self.xa_r,
            self.own_s,
            self.out_s,
        ) = bufs

    def core_copy(self, u):
        at = self.at
        return remote(
            self.parts.at[1, :, u],
            self.core_in.at[:, u],
            self.core_s.at[u],
            self.core_r.at[u],
            at.across_core,
        )

    def y_copy(self, u):
        at = self.at
        return remote(
            self.parts.at[0, 1, u],
            self.y_in.at[u],
            self.y_s.at[u],
            self.y_r.at[u],
            at.across_y,
        )

    def x_copy(self, u):
        return remote(
            self.parts.at[0, 0, u, 1],
            self.x_in.at[u],
            self.x_s.at[u],
            self.x_r.at[u],
            self.at.across_x,
        )

    def z_copy(self, u, step):
        at = self.at
        return remote(
            self.parts.at[0, 0, u, 0, (at.z + step) % at.depth],
            self.z_in.at[u, step - 1],
            self.z_s.at[u, step - 1],
            self.z_r.at[u, step - 1],
            at.along_z(step),
        )

    def za_copy(self, u, step):
        at = self.at
        return remote(
            self.done.at[u],
            self.whole.at[u, 0, at.z],
            self.za_s.at[u, step - 1],
            self.za_r.at[u, step - 1],
            at.along_z(step),
        )

    def own_copy(self, u):
        return pltpu.make_async_copy(
            self.done.at[u], self.whole.at[u, 0, self.at.z], self.own_s.at[u]
        )

    def xa_copy(self, u):
        return remote(
            self.whole.at[u, 0],
            self.whole.at[u, 1],
            self.xa_s.at[u],
            self.xa_r.at[u],
            self.at.across_x,
        )

    def out_copies(self, u, out):
        held = self.whole.at[u] if self.plane else self.parts.at[0, 0, u]
        return [
            pltpu.make_async_copy(
                held.at[half],
                out.at[u, :, :, pl.ds(pl.multiple_of(side * 384, 128), 384)],
                self.out_s.at[u, half],
            )
            for half, side in ((0, self.at.x), (1, 1 - self.at.x))
        ]

    def add(self, place, source, at):
        both = self.parts[place].astype(jnp.float32) + source[at].astype(jnp.float32)
        self.parts[place] = both.astype(jnp.bfloat16)

    def start(self, u):
        self.core_copy(u).start()

    def add_far(self, u):
        self.core_copy(u).wait_recv()
        for half in range(2):
            self.add((0, 1, u, half), self.core_in, (1, u, half))
        self.y_copy(u).start()

    def add_near(self, u):
        for half in range(2):
            self.add((0, 0, u, half), self.core_in, (0, u, half))

    def add_y(self, u):
        self.y_copy(u).wait_recv()
        self.add((0, 0, u, 1), self.y_in, (u, 1))
        if self.plane:
            self.x_copy(u).start()
        self.add((0, 0, u, 0), self.y_in, (u, 0))

    def add_x(self, u):
        self.x_copy(u).wait_recv()
        self.add((0, 0, u, 0), self.x_in, (u,))
        for step in range(1, self.at.depth):
            self.z_copy(u, step).start()

    def add_z(self, u):
        at = self.at
        total = self.parts[0, 0, u, 0, at.z].astype(jnp.float32)
        for step in range(1, at.depth):
            self.z_copy(u, step).wait_recv()
            total = total + self.z_in[u, step - 1].astype(jnp.float32)
        self.done[u] = total.astype(jnp.bfloat16)
        for step in range(1, at.depth):
            self.za_copy(u, step).start()
        self.own_copy(u).start()

    def spread_x(self, u):
        self.own_copy(u).wait()
        for step in range(1, self.at.depth):
            self.za_copy(u, step).wait_recv()
        self.xa_copy(u).start()

    def finish(self, u, out):
        if self.plane:
            self.xa_copy(u).wait_recv()
        for copy in self.out_copies(u, out):
            copy.start()

    def drain(self, u, out):
        self.core_copy(u).wait_send()
        self.y_copy(u).wait_send()
        for copy in self.out_copies(u, out):
            copy.wait()
        if not self.plane:
            return
        self.x_copy(u).wait_send()
        self.xa_copy(u).wait_send()
        for step in range(1, self.at.depth):
            self.z_copy(u, step).wait_send()
            self.za_copy(u, step).wait_send()


def pieces_of(depth):
    return depth if UNIT % (16 * depth) == 0 else 4


def reducer_scratch(depth):
    lanes = max(depth - 1, 1)
    depth = pieces_of(depth)
    rows = UNIT // depth
    dma = pltpu.SemaphoreType.DMA
    low = jnp.bfloat16
    return [
        pltpu.VMEM((2, 2, UNITS, 2, depth, rows, 384), low),
        pltpu.VMEM((2, UNITS, 2, depth, rows, 384), low),
        pltpu.VMEM((UNITS, 2, depth, rows, 384), low),
        pltpu.VMEM((UNITS, depth, rows, 384), low),
        pltpu.VMEM((UNITS, lanes if depth == lanes + 1 else 1, rows, 384), low),
        pltpu.VMEM((UNITS, 2, depth, rows, 384), low),
        pltpu.VMEM((UNITS, rows, 384), low),
        *[dma((UNITS,))] * 6,
        *[dma((UNITS, lanes if depth == lanes + 1 else 1))] * 4,
        *[dma((UNITS,))] * 3,
        dma((UNITS, 2)),
    ]


class Ring:
    def __init__(self, slots, sem, sources):
        self.slots, self.sem, self.sources = slots, sem, sources
        self.count = len(slots)
        self.used = 0
        for i in range(min(self.count, len(sources))):
            self.copy(i).start()

    def copy(self, i):
        return pltpu.make_async_copy(
            self.sources[i], self.slots[i % self.count], self.sem.at[i]
        )

    def take(self):
        self.copy(self.used).wait()
        return self.slots[self.used % self.count]

    def free(self):
        ahead = self.used + self.count
        if ahead < len(self.sources):
            self.copy(ahead).start()
        self.used += 1


def backward_kernel(dp_size, *refs):
    (
        lengths_ref,
        cls_grad,
        gain1,
        gain2,
        cot_hbm,
        wq_hbm,
        wo_hbm,
        wi_hbm,
        wb_hbm,
        tok_hbm,
        q_hbm,
        k_hbm,
        v_hbm,
        p_hbm,
        o_hbm,
        h1_hbm,
        n1_hbm,
        r1_hbm,
        g_hbm,
        gp_hbm,
        n2_hbm,
        r2_hbm,
        own_hbm,
        sums_hbm,
        grad_hbm,
        vec_out,
        own,
        cot,
        unit,
        inv1,
        inv2,
        acc,
        df,
        turned,
        h1,
        tok,
        q,
        k,
        v,
        probs,
        o,
        wo,
        w0,
        w1,
        w2,
        wq0,
        wq1,
        g0,
        g1,
        gp0,
        gp1,
        du,
        do,
        dkv,
        dqkv,
        vec,
        vec_in,
        vec_z,
        halo_in,
        load_sem,
        g_sem,
        w_sem,
        gp_sem,
        wq_sem,
        halo_sem,
        vec_s,
        vec_r,
        *bufs,
    ) = refs
    at = Places(dp_size)
    red = Reducer(at, bufs)
    rows, share, width = cot_hbm.shape
    region = share + HALO
    total = rows * region
    m = at.mp
    first = m * share
    left = (at.dp, (m + 3) % 4)
    right = (at.dp, (m + 1) % 4)
    order = (1, 3, 2, 0)
    true_shard = shard_order(at)

    def loading(i, src, dst):
        return pltpu.make_async_copy(src, dst, load_sem.at[i])

    cots = [
        loading(r, cot_hbm.at[r], cot.at[pl.ds(r * region, share)]) for r in range(rows)
    ]
    early = cots + [
        loading(rows + i, src, dst)
        for i, (src, dst) in enumerate(
            [(own_hbm, own), (n2_hbm, unit), (r2_hbm, inv2), (r1_hbm, inv1)]
        )
    ]
    for copy in early:
        copy.start()
    g_ring = Ring((g0, g1), g_sem, [g_hbm.at[s] for s in order])
    w_sources = [ref.at[s] for s in order for ref in (wb_hbm, wi_hbm)]
    w_ring = Ring((w0, w1, w2), w_sem, w_sources)
    gp_ring = Ring((gp0, gp1), gp_sem, [gp_hbm.at[s] for s in order])
    late = [
        loading(rows + 4 + i, src, dst)
        for i, (src, dst) in enumerate(
            [
                (h1_hbm, h1),
                (tok_hbm, tok),
                (o_hbm, o),
                (wo_hbm, wo),
                (q_hbm, q),
                (k_hbm, k),
                (v_hbm, v),
                (p_hbm, probs),
            ]
        )
    ]
    for copy in late:
        copy.start()
    wq_ring = Ring((wq0, wq1), wq_sem, [wq_hbm.at[s] for s in order])

    peers = [(at.dp, (m + j) % 4) for j in range(1, 4)] + [at.across_x]
    greet(peers + [at.along_z(step) for step in range(1, at.depth)])
    halos = [
        remote(
            cot_hbm.at[r, pl.ds(0, HALO)],
            cot.at[pl.ds(r * region + share, HALO)],
            halo_sem.at[0, r],
            halo_sem.at[1, r],
            left,
        )
        for r in range(rows)
    ]
    for copy in halos:
        copy.start()

    def events():
        lag = 3 if red.plane else 0
        for i in range(UNITS + lag):
            if i < UNITS:
                while i >= red.ready:
                    yield None
                yield lambda: red.add_y(i)
            if i >= lag:
                yield lambda: red.finish(i - lag, sums_hbm)
            if red.plane and 2 <= i < UNITS + 2:
                yield lambda: red.spread_x(i - 2)
            if red.plane and 1 <= i < UNITS + 1:
                yield lambda: red.add_z(i - 1)
            if red.plane and i < UNITS:
                yield lambda: red.add_x(i)

    queue = events()

    def pump(count):
        for _ in range(count):
            event = next(queue, None)
            if event is not None:
                event()

    vec[0] = jnp.zeros(vec.shape[1:], jnp.float32)
    slots = cls_grad.shape[0] // rows
    for copy in early:
        copy.wait()
    for copy in halos:
        copy.wait()

    def norm_back(part, grad, gain, inv, base):
        normed, inv_dev = unit[part], inv[part]
        scaled = grad * gain[...]
        centered = scaled - jnp.mean(scaled, axis=-1, keepdims=True)
        inner = jnp.mean(scaled * normed, axis=-1, keepdims=True)
        grad_in = inv_dev * (centered - normed * inner)
        acc[part] = grad_in
        df[part] = grad_in.astype(jnp.bfloat16)
        vec[0, base : base + 1] += jnp.sum(grad_in, axis=0, keepdims=True)
        vec[0, base + 1 : base + 2] += jnp.sum(grad * normed, axis=0, keepdims=True)
        vec[0, base + 2 : base + 3] += jnp.sum(grad, axis=0, keepdims=True)

    tile = 96
    for r in range(rows):
        starts = start_row(lengths_ref, r, first, slots)
        come = cls_grad[r * slots : (r + 1) * slots]
        terms = []
        for _ in range(3):
            term = come.astype(jnp.bfloat16)
            terms.append(term)
            come = come - term.astype(jnp.float32)

        @pl.loop(0, region // tile)
        def _(i):
            part = pl.ds(pl.multiple_of(r * region + i * tile, 32), tile)
            place = i * tile + lax.broadcasted_iota(jnp.int32, (tile, slots), 0)
            hit = (place == starts) & (place < share)
            pick = jnp.where(hit, 1.0, 0.0).astype(jnp.bfloat16)
            grad = cot[part].astype(jnp.float32)
            for term in terms:
                grad = grad + nn(pick, term)
            norm_back(part, grad * own[part], gain2, inv2, 3)

    first_unit = pltpu.make_async_copy(n1_hbm, unit, load_sem.at[1])
    first_unit.start()

    def put(s, u, half, values):
        low = values.astype(jnp.bfloat16)
        for i in range(values.shape[0] // UNIT):
            red.parts[s % 2, s // 2, u + i, half] = low[i * UNIT : (i + 1) * UNIT].reshape(
                red.pieces, UNIT // red.pieces, 384
            )

    def true_half(half):
        return at.x if half == 0 else 1 - at.x

    def true_columns(half):
        return pl.ds(pl.multiple_of(true_half(half) * 384, 128), 384)

    def sent(i, units):
        if i == 1:
            for u in units:
                red.start(u)
        if i == 2:
            for u in units:
                red.add_far(u)
        if i == 3:
            for u in units:
                red.add_near(u)
            red.ready = units[-1] + 1

    for i in range(4):
        g = g_ring.take()
        turned[...] = g[...].T
        g_ring.free()
        for half in range(2):
            put(order[i], 0, half, nn(turned[...], df[:, true_columns(half)]))
        sent(i, range(4))
    late[0].wait()
    turned[...] = h1[...].T
    for i in range(4):
        s = order[i]
        wb = w_ring.take()
        slope = gp_ring.take()
        for half in range(2):
            columns = true_columns(half)
            rows_here = pl.ds(2 * true_half(half), 2)
            rise = nt(df[...], wb[rows_here].reshape(384, width))
            rise = (rise * slope[:, columns].astype(jnp.float32)).astype(jnp.bfloat16)
            du[:, columns] = rise
            vec[0, pl.ds(6 + true_shard[s], 1), columns] = jnp.sum(
                rise.astype(jnp.float32), axis=0, keepdims=True
            )
            put(s, 4, half, nn(turned[...], rise))
        w_ring.free()
        gp_ring.free()
        wi = w_ring.take()
        sent(i, range(4, 8))
        for r in range(rows):
            part = pl.ds(r * region, region)
            acc[part] = acc[part] + nt(du[part], wi[...].reshape(width, width))
        w_ring.free()
        pump(3)

    first_unit.wait()

    @pl.loop(0, total // tile)
    def _(i):
        part = pl.ds(pl.multiple_of(i * tile, tile), tile)
        norm_back(part, acc[part], gain1, inv1, 0)

    for copy in late[1:]:
        copy.wait()
    pump(2)

    heads = q.shape[3] // HDIM
    cols = heads * HDIM
    blocks = q.shape[2] // BLOCK
    for i in range(4):
        s = order[i]
        flat = jnp.concatenate([o[s, r, :region] for r in range(rows)], axis=0)
        for half in range(2):
            put(s, 8, half, tn(flat, df[:, true_columns(half)]))
        sent(i, [8])
    pump(3)
    do[...] = jnp.zeros_like(do)
    for i in range(4):
        s = order[i]
        back = nt(df[...], wo[s].reshape(cols, width)).astype(jnp.bfloat16)
        for r in range(rows):
            do[r, :region] = back[r * region : (r + 1) * region]
        dkv[...] = jnp.zeros_like(dkv)
        for r in range(rows):
            for b in range(blocks):
                here = slice(b * BLOCK, (b + 1) * BLOCK)
                window = slice(b * BLOCK, b * BLOCK + BLOCK + 2 * HALO)
                grads = head_stack(do[r, here])
                queries = head_stack(q[s, r, here])
                weight = probs[s, r * blocks + b]
                wide = weight.astype(jnp.float32)
                rise = nt(grads, v[s, r, window])
                inner = jnp.sum(wide * rise, axis=1, keepdims=True)
                fall = (wide * (rise - inner)).astype(jnp.bfloat16)
                dq = head_pick(nn(fall, k[s, r, window]), cols) * 0.125
                valid = min(region - b * BLOCK, BLOCK)
                dqkv[0, r * region + b * BLOCK : r * region + b * BLOCK + valid] = dq[
                    :valid
                ].astype(jnp.bfloat16)
                dkv[0, r, window] += tn(fall, queries)
                dkv[1, r, window] += tn(weight, grads)
        for r in range(rows):
            for t in range(2):
                dqkv[1 + t, r * region : (r + 1) * region] = dkv[
                    t, r, HALO : HALO + region
                ].astype(jnp.bfloat16)
        wqs = wq_ring.take()
        for t, lane in ((0, 0), (1, None), (2, 256)):
            part = dqkv[t]
            if lane is not None:
                vec[0, pl.ds(10 + true_shard[s], 1), lane : lane + cols] = jnp.sum(
                    part.astype(jnp.float32), axis=0, keepdims=True
                )
            for half in range(2):
                put(s, 9 + t, half, tn(part, tok[:, true_columns(half)]))
            acc[...] += nt(part, wqs[t].reshape(width, cols))
        wq_ring.free()
        sent(i, range(9, 12))
        pump(5)

    def mask_grad(part):
        acc[part] = acc[part] * own[part]

    norm_tiles(total, tile, mask_grad)
    settled = [
        remote(
            acc.at[pl.ds(r * region + share, HALO)],
            halo_in.at[r],
            halo_sem.at[2, r],
            halo_sem.at[3, r],
            right,
        )
        for r in range(rows)
    ]
    for copy in settled:
        copy.start()

    def vec_copy(i):
        device = (at.across_core, at.across_y, at.across_x)[i]
        return remote(vec.at[i], vec_in.at[i], vec_s.at[i], vec_r.at[i], device)

    def vec_z_copy(step):
        index = 2 + step
        return remote(
            vec.at[3], vec_z.at[step], vec_s.at[index], vec_r.at[index], at.along_z(step)
        )

    vec_copy(0).start()
    pump(2)
    grads = []
    for copy in settled:
        copy.wait()
    for r in range(rows):
        head = pl.ds(r * region, HALO)
        acc[head] = acc[head] + halo_in[r]
    for r in range(rows):
        copy = loading(r, acc.at[pl.ds(r * region, share)], grad_hbm.at[r])
        copy.start()
        grads.append(copy)
    for i in range(3):
        vec_copy(i).wait_recv()
        both = vec[i] + vec_in[i]
        if i < 2:
            vec[i + 1] = both
            vec_copy(i + 1).start()
        else:
            vec[3] = both
            vec_z[0] = both
            for step in range(1, at.depth):
                vec_z_copy(step).start()
        pump(4)
    for step in range(1, at.depth):
        vec_z_copy(step).wait_recv()
    both = vec_z[at.back_z(0)]
    for z in range(1, at.depth):
        both = both + vec_z[at.back_z(z)]
    vec_out[...] = both
    for event in queue:
        event()
    for copy in grads:
        copy.wait()
    for i in range(3):
        vec_copy(i).wait_send()
    for step in range(1, at.depth):
        vec_z_copy(step).wait_send()

    @pl.loop(0, UNITS)
    def _(u):
        red.drain(u, sums_hbm)


def start_row(lengths_ref, row, first, slots):
    slot = lax.broadcasted_iota(jnp.int32, (1, slots), 1)

    def body(j, carry):
        line, begin = carry
        return (jnp.where(slot == j, begin - first, line), begin + lengths_ref[row, j])

    line, _ = lax.fori_loop(
        0, lengths_ref.shape[1], body, (jnp.full((1, slots), -1, jnp.int32), jnp.int32(0))
    )
    return line


def backward(lengths, cls_grad, gain1, gain2, cotangent, saved, dp_size):
    rows, share, width = cotangent.shape
    region = share + HALO
    total = rows * region
    q, k, probs, o = saved[5], saved[6], saved[8], saved[9]
    depth = dp_size // 2
    low, full = jnp.bfloat16, jnp.float32
    cols = q.shape[3]
    dma = pltpu.SemaphoreType.DMA
    vmem = pltpu.VMEM
    scratch = [
        vmem((total, 1), full),
        vmem((total, width), low),
        vmem((total, width), full),
        vmem((total, 1), full),
        vmem((total, 1), full),
        vmem((total, width), full),
        vmem((total, width), low),
        vmem((width, total), low),
        vmem((total, width), low),
        vmem((total, width), low),
        vmem(q.shape, low),
        vmem(k.shape, low),
        vmem(k.shape, low),
        vmem(probs.shape, low),
        vmem(o.shape, low),
        vmem(saved[1].shape, low),
        *[vmem(saved[2].shape[1:], low)] * 3,
        *[vmem(saved[0].shape[1:], low)] * 2,
        *[vmem((total, width), low)] * 4,
        vmem((total, width), low),
        vmem(q.shape[1:], low),
        vmem((2, *k.shape[1:]), full),
        vmem((3, total, cols), low),
        vmem((4, 16, width), full),
        vmem((3, 16, width), full),
        vmem((depth, 16, width), full),
        vmem((rows, HALO, width), full),
        dma((rows + 12,)),
        *[dma((8,))] * 4,
        dma((4, rows)),
        dma((2 + depth,)),
        dma((2 + depth,)),
    ] + reducer_scratch(depth)
    anywhere = pl.BlockSpec(memory_space=pl.ANY)
    in_vmem = pl.BlockSpec(memory_space=pltpu.VMEM)
    shape = jax.ShapeDtypeStruct
    return pl.pallas_call(
        lambda *refs: backward_kernel(dp_size, *refs),
        out_shape=[
            shape((UNITS, pieces_of(depth), UNIT // pieces_of(depth), width), low),
            shape((rows, share, width), full),
            shape((16, width), full),
        ],
        in_specs=[pl.BlockSpec(memory_space=pltpu.SMEM)] + [in_vmem] * 3 + [anywhere] * 19,
        out_specs=[anywhere, anywhere, in_vmem],
        scratch_shapes=scratch,
        compiler_params=pltpu.CompilerParams(
            collective_id=1, has_side_effects=True, vmem_limit_bytes=64 * 1024 * 1024 - 65536
        ),
        name="backward",
    )(lengths, cls_grad, gain1.reshape(1, -1), gain2.reshape(1, -1), cotangent, *saved)


def contrast_kernel(dp_size, sents, *refs):
    (
        cls_ref,
        b_pool,
        w_hbm,
        masks_hbm,
        loss_ref,
        w_grad,
        b_grad,
        cls_grad,
        w_pool,
        masks,
        rows_in,
        mine,
        every,
        views,
        pooled,
        units,
        inverse,
        logit_grad,
        lowered,
        load_sem,
        rs_s,
        rs_r,
        own_sem,
        z_s,
        z_r,
        hop_s,
        hop_r,
    ) = refs
    at = Places(dp_size)
    width = w_pool.shape[0]
    slots = views.shape[1]
    group = slots // dp_size
    share = group // 4
    loads = [
        pltpu.make_async_copy(w_hbm, w_pool, load_sem.at[0]),
        pltpu.make_async_copy(masks_hbm, masks, load_sem.at[1]),
    ]
    for load in loads:
        load.start()
    others = [(at.dp, (at.mp + j) % 4) for j in range(1, 4)]
    greet(others + [at.across_x] + [at.along_z(step) for step in range(1, at.depth)])

    quarters = [
        remote(
            cls_ref.at[(at.mp + j) % 4],
            rows_in.at[j - 1],
            rs_s.at[j - 1],
            rs_r.at[j - 1],
            others[j - 1],
        )
        for j in range(1, 4)
    ]
    for copy in quarters:
        copy.start()
    total = cls_ref[at.mp].astype(jnp.float32)
    for j, copy in enumerate(quarters):
        copy.wait_recv()
        total = total + rows_in[j].astype(jnp.float32)
    mine[...] = total.astype(jnp.bfloat16)

    place = every.at[at.z, at.x, at.y, at.core]
    own = pltpu.make_async_copy(mine, place, own_sem)
    own.start()
    along = [
        remote(mine, place, z_s.at[step - 1], z_r.at[step - 1], at.along_z(step))
        for step in range(1, at.depth)
    ]
    for copy in along:
        copy.start()
    own.wait()
    for copy in along:
        copy.wait_recv()
    hops = []
    for i, (part, device) in enumerate(
        [
            (every.at[:, at.x, at.y, at.core], at.across_x),
            (every.at[:, :, at.y, at.core], at.across_y),
            (every.at[:, :, :, at.core], at.across_core),
        ]
    ):
        hop = remote(part, part, hop_s.at[i], hop_r.at[i], device)
        hop.start()
        hop.wait_recv()
        hops.append(hop)
    for load in loads:
        load.wait()

    per_z = slots // at.depth
    for t in range(2):
        for z in range(at.depth):
            part = slice(z * per_z, (z + 1) * per_z)
            cls_rows = every[z].reshape(per_z, width).astype(jnp.float32)
            keep = masks[z, :, t].reshape(per_z, width).astype(jnp.float32)
            view = (cls_rows * keep * KEEP_SCALE).astype(jnp.bfloat16)
            views[t, part] = view
            unit = jnp.tanh(nn(view, w_pool[...]) + b_pool[...])
            pooled[t, part] = unit
            inv = lax.rsqrt(jnp.sum(unit * unit, axis=-1, keepdims=True) + 1e-06)
            inverse[t, part] = inv
            units[t, part] = (unit * inv).astype(jnp.bfloat16)

    def real(index):
        return index % 32 < sents

    loss = jnp.zeros((1, 1), jnp.float32)
    for z in range(at.depth):
        part = slice(z * per_z, (z + 1) * per_z)
        logits = nt(units[0, part], units[1]) * 20.0
        line = z * per_z + lax.broadcasted_iota(jnp.int32, logits.shape, 0)
        column = lax.broadcasted_iota(jnp.int32, logits.shape, 1)
        logits = jnp.where(real(column), logits, MASKED)
        peak = jnp.max(logits, axis=1, keepdims=True)
        raised = jnp.exp(logits - peak)
        row_total = jnp.sum(raised, axis=1, keepdims=True)
        partner = line == column
        chosen = jnp.sum(jnp.where(partner, logits, 0.0), axis=1, keepdims=True)
        row_loss = peak + jnp.log(row_total) - chosen
        row_loss = jnp.where(real(line[:, :1]), row_loss, 0.0)
        loss = loss + jnp.sum(row_loss, axis=0, keepdims=True)
        grad = raised / row_total - jnp.where(partner, 1.0, 0.0)
        logit_grad[part] = jnp.where(real(line), grad, 0.0).astype(jnp.bfloat16)
    count = slots // 32 * sents
    loss_ref[...] = jnp.broadcast_to(loss / count, loss_ref.shape)

    bias = jnp.zeros((1, width), jnp.float32)
    for t in range(2):
        for z in range(at.depth):
            part = slice(z * per_z, (z + 1) * per_z)
            if t == 0:
                unit_grad = nn(logit_grad[part], units[1]) * 20.0
            else:
                unit_grad = tn(logit_grad[:, part], units[0]) * 20.0
            before = pooled[t, part]
            inv = inverse[t, part]
            unit = before * inv
            inner = jnp.sum(unit_grad * unit, axis=-1, keepdims=True)
            grad = inv * (unit_grad - unit * inner) * (1.0 - before * before)
            low = grad.astype(jnp.bfloat16)
            lowered[t, part] = low
            bias = bias + jnp.sum(low.astype(jnp.float32), axis=0, keepdims=True)
    b_grad[...] = bias

    here = pl.ds(pl.multiple_of(at.dp * group, group), group)
    back = jnp.zeros((group, width), jnp.float32)
    for t in range(2):
        keep = masks[at.z, at.x, t].astype(jnp.float32)
        back = back + nt(lowered[t, here], w_pool[...]) * keep
    cls_grad[...] = back * KEEP_SCALE
    for half in range(2):
        columns = slice(half * width // 2, (half + 1) * width // 2)
        w_grad[:, columns] = tn(views[0], lowered[0, :, columns]) + tn(
            views[1], lowered[1, :, columns]
        )
    for copy in quarters + along + hops:
        copy.wait_send()


def contrast_whole(cls_part, masks, w_pool, b_pool, dp_size, sents):
    group, width = cls_part.shape
    slots = group * dp_size
    depth = dp_size // 2
    share = group // 4
    low, full = jnp.bfloat16, jnp.float32
    dma = pltpu.SemaphoreType.DMA
    vmem = pltpu.VMEM
    anywhere = pl.BlockSpec(memory_space=pl.ANY)
    in_vmem = pl.BlockSpec(memory_space=pltpu.VMEM)
    shape = jax.ShapeDtypeStruct
    return pl.pallas_call(
        lambda *refs: contrast_kernel(dp_size, sents, *refs),
        out_shape=[
            shape((8, 128), full),
            shape((width, width), full),
            shape((1, width), full),
            shape((group, width), full),
        ],
        in_specs=[in_vmem, in_vmem, anywhere, anywhere],
        out_specs=[in_vmem] * 4,
        scratch_shapes=[
            vmem((width, width), low),
            vmem(masks.shape, low),
            vmem((3, share, width), low),
            vmem((share, width), low),
            vmem((depth, 2, 2, 2, share, width), low),
            vmem((2, slots, width), low),
            vmem((2, slots, width), full),
            vmem((2, slots, width), low),
            vmem((2, slots, 1), full),
            vmem((slots, slots), low),
            vmem((2, slots, width), low),
            dma((2,)),
            dma((3,)),
            dma((3,)),
            dma,
            dma((max(depth - 1, 1),)),
            dma((max(depth - 1, 1),)),
            dma((3,)),
            dma((3,)),
        ],
        compiler_params=pltpu.CompilerParams(
            collective_id=3, has_side_effects=True, vmem_limit_bytes=60 * 1024 * 1024
        ),
        name="contrast",
    )(cls_part.reshape(4, share, width), b_pool.reshape(1, -1), w_pool, masks)


def shards(
    tokens,
    lengths,
    view_masks,
    w_qkv,
    b_qv,
    w_out,
    b_out,
    ln1_gain,
    ln1_bias,
    w_in,
    b_in,
    w_back,
    b_back,
    ln2_gain,
    ln2_bias,
    w_pool,
    b_pool,
    cotangent,
):
    rows, share, width = tokens.shape
    ranks = lax.axis_size("dp")
    sents = lengths.shape[1]
    gathers = ranks * rows * 32 <= 1024
    masks = jnp.pad(view_masks, [(0, 0), (0, 32 - sents), (0, 0), (0, 0)]).astype(jnp.bfloat16)
    masks = masks.transpose(2, 0, 1, 3).reshape(2, rows * 32, width)
    hidden, cls_part, *saved, masks = forward(
        tokens, lengths, w_qkv, b_qv, w_out, b_out, (ln1_gain, ln1_bias), w_in, b_in, w_back,
        b_back, (ln2_gain, ln2_bias), masks, ranks, gathers,
    )
    if gathers:
        loss, w_pool_grad, b_pool_grad, cls_grad = contrast_whole(
            cls_part, masks, w_pool, b_pool, ranks, sents
        )
        loss, b_pool_grad = loss[0, 0], b_pool_grad[0]
    else:
        cls_rows = cls_part.reshape(rows, -1, width)[:, :sents]
        cls_rows = lax.psum(cls_rows, "mp").astype(jnp.float32)
        loss, w_pool_grad, b_pool_grad, cls_grad = contrast(
            cls_rows.reshape(-1, width), view_masks, w_pool, b_pool
        )
        cls_grad = cls_grad.reshape(rows, -1, width)
        cls_grad = jnp.pad(cls_grad, [(0, 0), (0, 32 - sents), (0, 0)]).reshape(-1, width)
    sums, token_grad, vectors = backward(
        lengths, cls_grad, ln1_gain, ln2_gain, cotangent, saved, ranks
    )
    if pieces_of(ranks // 2) != ranks // 2:
        sums = lax.psum(sums, "dp")
    sums = sums.reshape(UNITS, UNIT, width).astype(jnp.float32)
    own = lax.axis_index("mp")
    cols = b_qv.shape[1]
    own_qv = lax.dynamic_slice_in_dim(vectors, 10 + own, 1, axis=0)
    own_in = lax.dynamic_slice_in_dim(vectors, 6 + own, 1, axis=0)
    return (
        hidden,
        loss,
        token_grad,
        sums[9:12].transpose(0, 2, 1),
        jnp.concatenate([own_qv[:, :cols], own_qv[:, 256 : 256 + cols]], axis=0),
        sums[8],
        vectors[0],
        vectors[1],
        vectors[2],
        sums[4:8].reshape(width, width),
        own_in[0],
        sums[0:4].reshape(width, width),
        vectors[3],
        vectors[4],
        vectors[5],
        w_pool_grad,
        b_pool_grad,
    )


def solution(mesh):
    in_specs = (
        P("dp", "mp", None),
        P("dp", None),
        P("dp", None, None, None),
        P(None, None, "mp"),
        P(None, "mp"),
        P("mp", None),
        P(),
        P(),
        P(),
        P(None, "mp"),
        P("mp"),
        P("mp", None),
        P(),
        P(),
        P(),
        P(),
        P(),
        P("dp", "mp", None),
    )
    out_specs = (
        P("dp", "mp", None),
        P(),
        P("dp", "mp", None),
        P(None, None, "mp"),
        P(None, "mp"),
        P("mp", None),
        P(),
        P(),
        P(),
        P(None, "mp"),
        P("mp"),
        P("mp", None),
        P(),
        P(),
        P(),
        P(),
        P(),
    )
    return jax.shard_map(shards, mesh=mesh, in_specs=in_specs, out_specs=out_specs, check_vma=False)
```

```python
import jax
import jax.numpy as jnp
from jax import lax
from jax.experimental import pallas as pl
from jax.experimental.pallas import tpu as pltpu
from jax.sharding import PartitionSpec as P

HDIM = 64
HALO = 32
BLOCK = 64
KEEP_SCALE = 1.0 / 0.9
MASKED = -1000000000.0


def norm_forward(values, gain, shift):
    center = values - jnp.mean(values, axis=-1, keepdims=True)
    inv_dev = lax.rsqrt(jnp.mean(center * center, axis=-1, keepdims=True) + 1e-12)
    normed = center * inv_dev
    return (normed * gain + shift, normed, inv_dev)


def dot32(equation, left, right):
    return jnp.einsum(equation, left, right, preferred_element_type=jnp.float32)


def contrast(cls_rows, view_masks, w_pool, b_pool):
    local_sents = cls_rows.shape[0]
    own_ids = lax.axis_index("dp") * local_sents + jnp.arange(local_sents, dtype=jnp.int32)
    keep_masks = view_masks.astype(jnp.float32).reshape(local_sents, 2, -1)
    views = (cls_rows[:, None, :] * keep_masks * KEEP_SCALE).astype(jnp.bfloat16)
    pooled = jnp.tanh(dot32("svd,de->sve", views, w_pool) + b_pool)
    inv_length = lax.rsqrt(jnp.sum(pooled * pooled, axis=-1, keepdims=True) + 1e-06)
    unit = pooled * inv_length
    unit_low = unit.astype(jnp.bfloat16)
    anchors = unit_low[:, 0]
    every_target = lax.all_gather(unit_low[:, 1], "dp", axis=0, tiled=True)
    logits = dot32("sd,td->st", anchors, every_target) * 20.0
    sent_ids = jnp.arange(every_target.shape[0], dtype=jnp.int32)
    is_partner = sent_ids[None, :] == own_ids[:, None]
    row_peak = jnp.max(logits, axis=1, keepdims=True)
    raised = jnp.exp(logits - row_peak)
    row_total = jnp.sum(raised, axis=1, keepdims=True)
    log_total = row_peak[:, 0] + jnp.log(row_total[:, 0])
    loss_local = jnp.sum(log_total - jnp.sum(jnp.where(is_partner, logits, 0.0), axis=1))
    logit_grad = (raised / row_total - is_partner.astype(jnp.float32)).astype(jnp.bfloat16)
    anchor_grad = dot32("st,td->sd", logit_grad, every_target) * 20.0
    target_terms = dot32("st,sd->td", logit_grad, anchors) * 20.0
    target_grad = lax.psum_scatter(target_terms, "dp", scatter_dimension=0, tiled=True)
    unit_grad = jnp.stack([anchor_grad, target_grad], axis=1)
    pooled_grad = inv_length * (
        unit_grad - unit * jnp.sum(unit_grad * unit, axis=-1, keepdims=True)
    )
    before_grad = (pooled_grad * (1.0 - pooled * pooled)).astype(jnp.bfloat16)
    w_pool_grad = dot32("svd,sve->de", views, before_grad)
    b_pool_grad = jnp.sum(before_grad, axis=(0, 1), dtype=jnp.float32)
    view_grad = dot32("sve,de->svd", before_grad, w_pool)
    cls_grad = jnp.sum(view_grad * keep_masks, axis=1) * KEEP_SCALE
    sums = lax.psum((w_pool_grad, b_pool_grad, loss_local), "dp")
    loss = sums[2] / (local_sents * lax.axis_size("dp"))
    return (loss, sums[0], sums[1], cls_grad)


MESH = pl.DeviceIdType.MESH
UNIT = 192
UNITS = 12


def greet(peers):
    barrier = pltpu.get_barrier_semaphore()
    for peer in peers:
        pl.semaphore_signal(barrier, inc=1, device_id=peer, device_id_type=MESH)
    pl.semaphore_wait(barrier, len(peers))


class Places:
    def __init__(self, dp_size):
        self.dp = lax.axis_index("dp")
        self.mp = lax.axis_index("mp")
        self.core = self.mp % 2
        self.y = self.mp // 2
        self.x = self.dp % 2
        self.z = self.dp // 2
        self.depth = dp_size // 2
        self.across_core = (self.dp, self.y * 2 + (1 - self.core))
        self.across_y = (self.dp, (1 - self.y) * 2 + self.core)
        self.across_both = (self.dp, (1 - self.y) * 2 + (1 - self.core))
        self.across_x = (self.z * 2 + (1 - self.x), self.mp)

    def along_z(self, step):
        return ((self.z + step) % self.depth * 2 + self.x, self.mp)

    def back_z(self, step):
        return (self.z + self.depth - step) % self.depth


def remote(src, dst, send_sem, recv_sem, device):
    return pltpu.make_async_remote_copy(
        src_ref=src,
        dst_ref=dst,
        send_sem=send_sem,
        recv_sem=recv_sem,
        device_id=device,
        device_id_type=MESH,
    )


def norm_tiles(count, tile, body):
    @pl.loop(0, count // tile)
    def _(i):
        body(pl.ds(pl.multiple_of(i * tile, tile), tile))


def row_marks(lengths_ref, local, first, share, region):
    rows, sents = lengths_ref.shape
    row_id = lax.broadcasted_iota(jnp.int32, local.shape, 0)
    places = local + first

    def per_row(values):
        out = jnp.full(local.shape, values[-1], jnp.int32)
        for r in range(rows - 1):
            out = jnp.where(row_id == r, values[r], out)
        return out

    def body(j, carry):
        passed, begun, ends = carry
        ends = tuple(ends[r] + lengths_ref[r, j] for r in range(rows))
        edge = per_row(ends)
        reached = places >= edge
        return (
            passed + reached.astype(jnp.int32),
            jnp.where(reached, edge, begun),
            ends,
        )

    zero = jnp.zeros(local.shape, jnp.int32)
    start = tuple(jnp.int32(0) for _ in range(rows))
    passed, begun, ends = lax.fori_loop(0, sents, body, (zero, zero, start))
    inside = places < per_row(ends)
    here = (local >= 0) & (local < region)
    segment = jnp.where(here, jnp.where(inside, passed, places + sents), -2)
    begins = (begun >= first) & (begun < first + share)
    owned = here & ((inside & begins) | (~inside & (local < share)))
    return (segment, owned)


def start_column(lengths_ref, row, first, slots):
    slot = lax.broadcasted_iota(jnp.int32, (slots, 1), 0)

    def body(j, carry):
        column, begin = carry
        column = jnp.where(slot == j, begin - first, column)
        return (column, begin + lengths_ref[row, j])

    column, _ = lax.fori_loop(
        0, lengths_ref.shape[1], body, (jnp.full((slots, 1), -1, jnp.int32), jnp.int32(0))
    )
    return column


def head_stack(values):
    lane = lax.broadcasted_iota(jnp.int32, values.shape, 1) // HDIM
    zero = jnp.zeros_like(values)
    return jnp.concatenate(
        [jnp.where(lane == h, values, zero) for h in range(values.shape[1] // HDIM)], axis=0
    )


def head_pick(stacked, width):
    heads = width // HDIM
    rows = stacked.shape[0] // heads
    lane = lax.broadcasted_iota(jnp.int32, (rows, width), 1) // HDIM
    out = stacked[:rows]
    for h in range(1, heads):
        out = jnp.where(lane == h, stacked[h * rows : (h + 1) * rows], out)
    return out


def nn(left, right):
    return jnp.dot(left, right, preferred_element_type=jnp.float32)


def nt(left, right):
    return lax.dot_general(
        left, right, (((1,), (1,)), ((), ())), preferred_element_type=jnp.float32
    )


def tn(left, right):
    return lax.dot_general(
        left, right, (((0,), (0,)), ((), ())), preferred_element_type=jnp.float32
    )


def shard_order(at):
    return [
        at.mp,
        at.y * 2 + (1 - at.core),
        (1 - at.y) * 2 + at.core,
        (1 - at.y) * 2 + (1 - at.core),
    ]


def forward_kernel(dp_size, gathers, *refs):
    (
        lengths_ref,
        tokens_hbm,
        wq_hbm,
        wo_hbm,
        wi_hbm,
        wb_hbm,
        bq_hbm,
        bi_hbm,
        masks_hbm,
        b_out,
        gain1,
        shift1,
        b_back,
        gain2,
        shift2,
        hidden_hbm,
        cls_ref,
        wq_out,
        wo_out,
        wi_out,
        wb_out,
        tok_out,
        q_out,
        k_out,
        v_out,
        p_out,
        o_out,
        h1_out,
        n1_out,
        r1_out,
        g_out,
        gp_out,
        n2_out,
        r2_out,
        own_out,
        masks_out,
        tok,
        wq,
        wo,
        wi,
        wb,
        bq,
        bi,
        q,
        k,
        v,
        probs,
        o,
        h1,
        n1,
        r1,
        g,
        gp,
        n2,
        r2,
        own,
        acc,
        upper,
        seg,
        key_seg,
        hid,
        hid_in,
        local_sem,
        halo_sem,
        bias_s,
        bias_r,
        core_s,
        core_r,
        y_s,
        y_r,
        x_s,
        x_r,
        yc_s,
        yc_r,
        xc_s,
        xc_r,
        out_sem,
        mask_s,
        mask_r,
    ) = refs
    at = Places(dp_size)
    rows, share, width = tokens_hbm.shape
    region = share + HALO
    total = rows * region
    m = at.mp
    first = m * share
    left = (at.dp, (m + 3) % 4)
    right = (at.dp, (m + 1) % 4)
    order = range(4)
    chunks = (
        [(wq, wq_hbm, (t,)) for t in range(3)]
        + [(wo, wo_hbm, ())]
        + [(wi, wi_hbm, (b,)) for b in range(4)]
        + [(wb, wb_hbm, (b,)) for b in range(4)]
    )
    whole = [(wq, wq_hbm), (wo, wo_hbm), (wi, wi_hbm), (wb, wb_hbm)]

    peers = [(at.dp, (m + j) % 4) for j in range(1, 4)] + [at.across_x]
    greet(peers + [at.along_z(step) for step in range(1, at.depth if gathers else 1)])

    loads = [
        pltpu.make_async_copy(tokens_hbm.at[r], tok.at[pl.ds(r * region, share)], local_sem.at[r])
        for r in range(rows)
    ]
    loads += [
        pltpu.make_async_copy(src, dst.at[0], local_sem.at[rows + i])
        for i, (dst, src) in enumerate(whole + [(bq, bq_hbm), (bi, bi_hbm)])
    ]
    for load in loads:
        load.start()
    halos = [
        remote(
            tokens_hbm.at[r, pl.ds(0, HALO)],
            tok.at[pl.ds(r * region + share, HALO)],
            halo_sem.at[0, r],
            halo_sem.at[1, r],
            left,
        )
        for r in range(rows)
    ]
    for copy in halos:
        copy.start()
    biases = []
    for j, device in enumerate((at.across_core, at.across_y, at.across_both), start=1):
        for i, (dst, src) in enumerate([(bq, bq_hbm), (bi, bi_hbm)]):
            biases.append(
                remote(src, dst.at[j], bias_s.at[j - 1, i], bias_r.at[j - 1, i], device)
            )
    for copy in biases:
        copy.start()

    def core_copy(i):
        dst, src = whole[i]
        return remote(src, dst.at[1], core_s.at[i], core_r.at[i], at.across_core)

    def y_copy(c):
        dst, src, index = chunks[c]
        place = (*index, at.x)
        return remote(src.at[place], dst.at[(2, *place)], y_s.at[c], y_r.at[c], at.across_y)

    def x_copy(c):
        ref = chunks[c][0].at[(2, *chunks[c][2], at.x)]
        return remote(ref, ref, x_s.at[c], x_r.at[c], at.across_x)

    def yc_copy(c):
        ref, _, index = chunks[c]
        place = (*index, at.x)
        return remote(
            ref.at[(2, *place)], ref.at[(3, *place)], yc_s.at[c], yc_r.at[c], at.across_core
        )

    def xc_copy(c):
        ref, _, index = chunks[c]
        place = (*index, 1 - at.x)
        return remote(
            ref.at[(2, *place)], ref.at[(3, *place)], xc_s.at[c], xc_r.at[c], at.across_core
        )

    mask_hops = []
    if gathers:
        mask_own = pltpu.make_async_copy(
            masks_hbm.at[at.core], masks_out.at[at.z, at.x, at.core], mask_s.at[0]
        )
        mask_own.start()
        mask_hops = [
            remote(
                masks_hbm.at[at.core],
                masks_out.at[at.z, at.x, at.core],
                mask_s.at[at.depth],
                mask_r.at[at.depth],
                at.across_x,
            )
        ]
        for step in range(1, at.depth):
            pair = masks_out.at[at.z, :, at.core]
            mask_hops.append(
                remote(pair, pair, mask_s.at[step], mask_r.at[step], at.along_z(step))
            )
        view = masks_out.at[:, :, at.core]
        index = at.depth + 1
        mask_hops.append(
            remote(view, view, mask_s.at[index], mask_r.at[index], at.across_core)
        )
        mask_hops[0].start()

    def pass_masks(stage):
        if not gathers:
            return
        come = [mask_hops[:1], mask_hops[1:-1], mask_hops[-1:]]
        if stage == 0:
            mask_own.wait()
        for hop in come[stage]:
            hop.wait_recv()
        if stage < 2:
            for hop in come[stage + 1]:
                hop.start()

    for c in range(12):
        y_copy(c).start()
    for i in range(4):
        core_copy(i).start()

    def step(c):
        if c < 12:
            y_copy(c).wait_recv()
            x_copy(c).start()
            yc_copy(c).start()
        if c > 0:
            x_copy(c - 1).wait_recv()
            xc_copy(c - 1).start()

    saves = []

    def save(src, dst):
        copy = pltpu.make_async_copy(src, dst, out_sem.at[len(saves)])
        copy.start()
        saves.append(copy)

    lane = lax.broadcasted_iota(jnp.int32, (8, 384), 1)
    segment, owned = row_marks(lengths_ref, lane, first, share, region)
    seg_cols = segment.astype(jnp.float32).T
    own_cols = owned.astype(jnp.float32).T
    for r in range(rows):
        seg[r] = jnp.broadcast_to(seg_cols[: seg.shape[1], r : r + 1], seg.shape[1:])
        own[pl.ds(r * region, region)] = own_cols[:region, r : r + 1]
    save(own, own_out)
    for r in range(rows):
        block = lax.broadcasted_iota(jnp.int32, (8, BLOCK + 2 * HALO), 0)
        offset = lax.broadcasted_iota(jnp.int32, (8, BLOCK + 2 * HALO), 1)
        keys, _ = row_marks(
            RowView(lengths_ref, r), block * BLOCK + offset - HALO, first, share, region
        )
        key_seg[r] = keys.astype(jnp.float32)
    blocks = q.shape[2] // BLOCK

    q[...] = jnp.zeros_like(q)
    k[...] = jnp.zeros_like(k)
    v[...] = jnp.zeros_like(v)

    for load in loads:
        load.wait()
    for copy in halos:
        copy.wait()
    for copy in biases:
        copy.wait_recv()
    save(tok, tok_out)

    def project(s):
        x = tok[...]
        for t, dst in enumerate((q, k, v)):
            y = nn(x, wq[s, t].reshape(width, -1))
            if t == 0:
                y = (y + bq[s, 0:1]).astype(jnp.bfloat16) * jnp.bfloat16(0.125)
            elif t == 1:
                y = y.astype(jnp.bfloat16)
            else:
                y = (y + bq[s, 1:2]).astype(jnp.bfloat16)
            lead = 0 if t == 0 else HALO
            for r in range(rows):
                dst[s, r, lead : lead + region] = y[r * region : (r + 1) * region]

    def attend(s):
        heads = q.shape[3] // HDIM

        @pl.loop(0, rows)
        def _(r):
            for b in range(blocks):
                queries = head_stack(q[s, r, b * BLOCK : (b + 1) * BLOCK])
                window = slice(b * BLOCK, b * BLOCK + BLOCK + 2 * HALO)
                scores = nt(queries, k[s, r, window])
                allowed = seg[r, b * BLOCK : (b + 1) * BLOCK] == key_seg[r, b : b + 1]
                scores = jnp.where(jnp.concatenate([allowed] * heads, axis=0), scores, MASKED)
                peak = jnp.max(scores, axis=1, keepdims=True)
                raised = jnp.exp(scores - peak)
                weights = (raised / jnp.sum(raised, axis=1, keepdims=True)).astype(jnp.bfloat16)
                probs[s, r * blocks + b] = weights
                context = nn(weights, v[s, r, window])
                o[s, r, b * BLOCK : (b + 1) * BLOCK] = head_pick(context, heads * HDIM).astype(
                    jnp.bfloat16
                )

    def attention(i):
        s = order[i]
        project(s)
        attend(s)

    attention(0)
    step(0)
    core_copy(0).wait_recv()
    step(1)
    pass_masks(0)
    attention(1)
    step(2)
    step(3)
    attention(2)
    step(4)
    for c in range(3):
        yc_copy(c).wait_recv()
        xc_copy(c).wait_recv()
    attention(3)
    step(5)
    save(wq, wq_out)
    save(q, q_out)
    save(k, k_out)
    save(v, v_out)
    save(probs, p_out)
    save(o, o_out)

    core_copy(1).wait_recv()
    yc_copy(3).wait_recv()
    xc_copy(3).wait_recv()
    save(wo, wo_out)
    for r in range(rows):
        part = pl.ds(r * region, region)
        y = nn(o[0, r, :region], wo[0].reshape(-1, width))
        for s in range(1, 4):
            y = y + nn(o[s, r, :region], wo[s].reshape(-1, width))
        acc[part] = y

    def first_norm(part):
        values = tok[part].astype(jnp.float32) + acc[part] + b_out[...]
        normed, unit, inv = norm_forward(values, gain1[...], shift1[...])
        n1[part] = unit
        r1[part] = inv
        h1[part] = normed.astype(jnp.bfloat16)
        acc[part] = normed + b_back[...]

    norm_tiles(total, 96, first_norm)
    save(h1, h1_out)
    save(n1, n1_out)
    save(r1, r1_out)
    step(6)

    def raise_units(s):
        @pl.loop(0, 3)
        def _(n):
            columns = pl.ds(pl.multiple_of(n * 256, 256), 256)
            upper[...] = nn(h1[...], wi[s, :, :, :, columns].reshape(width, 256))

            def activate(part):
                u = upper[part] + bi[s, :, columns]
                cdf = 0.5 * (1.0 + lax.erf(u * 0.7071067811865476))
                g[s, part, columns] = (u * cdf).astype(jnp.bfloat16)
                slope = cdf + u * jnp.exp(-0.5 * u * u) * 0.3989422804014327
                gp[s, part, columns] = slope.astype(jnp.bfloat16)

            norm_tiles(total, 96, activate)

    def lower_units(s):
        @pl.loop(0, rows)
        def _(r):
            part = pl.ds(pl.multiple_of(r * region, 32), region)
            acc[part] = acc[part] + nn(g[s, part], wb[s].reshape(width, width))

    core_copy(2).wait_recv()
    raise_units(order[0])
    step(7)
    lower_units_early = [order[0], order[1]]
    core_copy(3).wait_recv()
    lower_units(lower_units_early[0])
    step(8)
    pass_masks(1)
    raise_units(order[1])
    step(9)
    lower_units(lower_units_early[1])
    for c in range(4, 8):
        yc_copy(c).wait_recv()
        xc_copy(c).wait_recv()
    save(wi, wi_out)
    raise_units(order[2])
    step(10)
    raise_units(order[3])
    save(g, g_out)
    save(gp, gp_out)
    step(11)
    step(12)
    lower_units(order[2])
    pass_masks(2)
    for c in range(8, 12):
        yc_copy(c).wait_recv()
        xc_copy(c).wait_recv()
    save(wb, wb_out)
    lower_units(order[3])

    def second_norm(part):
        normed, unit, inv = norm_forward(acc[part], gain2[...], shift2[...])
        n2[part] = unit
        r2[part] = inv
        hid[part] = normed.astype(jnp.bfloat16)

    norm_tiles(total, 96, second_norm)
    save(n2, n2_out)
    save(r2, r2_out)

    slots = cls_ref.shape[0] // rows
    for r in range(rows):
        place = lax.broadcasted_iota(jnp.int32, (slots, share), 1)
        pick = place == start_column(lengths_ref, r, first, slots)
        cls_ref[r * slots : (r + 1) * slots] = nn(
            pick.astype(jnp.bfloat16), hid[r * region : r * region + share]
        ).astype(jnp.bfloat16)

    def mask_hidden(part):
        hid[part] = (hid[part].astype(jnp.float32) * own[part]).astype(jnp.bfloat16)

    norm_tiles(total, 96, mask_hidden)
    settled = [
        remote(
            hid.at[pl.ds(r * region + share, HALO)],
            hid_in.at[r],
            halo_sem.at[2, r],
            halo_sem.at[3, r],
            right,
        )
        for r in range(rows)
    ]
    for copy in settled:
        copy.start()
    for copy in settled:
        copy.wait()
    for r in range(rows):
        head = pl.ds(r * region, HALO)
        hid[head] = hid[head] + hid_in[r]
    for r in range(rows):
        save(hid.at[pl.ds(r * region, share)], hidden_hbm.at[r])

    for copy in saves:
        copy.wait()
    for copy in biases + mask_hops:
        copy.wait_send()
    for i in range(4):
        core_copy(i).wait_send()
    for c in range(12):
        y_copy(c).wait_send()
        x_copy(c).wait_send()
        yc_copy(c).wait_send()
        xc_copy(c).wait_send()


class RowView:
    def __init__(self, ref, row):
        self.ref, self.row = ref, row
        self.shape = (1, ref.shape[1])

    def __getitem__(self, index):
        return self.ref[self.row, index[1]]


def forward(tokens, lengths, w_qkv, b_qv, w_out, b_out, ln1, w_in, b_in, w_back, b_back, ln2, masks,
            dp_size, gathers):
    rows, share, width = tokens.shape
    region = share + HALO
    total = rows * region
    blocks = -(-region // BLOCK)
    padded = blocks * BLOCK
    keyed = padded + 2 * HALO
    low, full = jnp.bfloat16, jnp.float32
    head_cols = w_qkv.shape[2]
    slots = 32
    shape = jax.ShapeDtypeStruct
    saved = [
        ((4, 3, 2, width // 2, head_cols), low),
        ((4, 2, head_cols // 2, width), low),
        ((4, 4, 2, width // 8, width), low),
        ((4, 4, 2, width // 8, width), low),
        ((total, width), low),
        ((4, rows, padded, head_cols), low),
        ((4, rows, keyed, head_cols), low),
        ((4, rows, keyed, head_cols), low),
        ((4, rows * blocks, head_cols // HDIM * BLOCK, BLOCK + 2 * HALO), low),
        ((4, rows, padded, head_cols), low),
        ((total, width), low),
        ((total, width), full),
        ((total, 1), full),
        ((4, total, width), low),
        ((4, total, width), low),
        ((total, width), full),
        ((total, 1), full),
        ((total, 1), full),
    ]
    out_shape = [shape((rows, share, width), low), shape((rows * slots, width), low)]
    out_shape += [shape(*item) for item in saved]
    out_shape += [shape((dp_size // 2, 2, *masks.shape) if gathers else (8, 128), low)]
    held = [pltpu.VMEM(*item) for item in saved]
    dma = pltpu.SemaphoreType.DMA
    scratch = [held[4]] + held[:4]
    scratch += [pltpu.VMEM((4, 2, head_cols), full), pltpu.VMEM((4, 1, width), full)]
    scratch += held[5:]
    scratch += [
        pltpu.VMEM((total, width), full),
        pltpu.VMEM((total, 256), full),
        pltpu.VMEM((rows, padded, BLOCK + 2 * HALO), full),
        pltpu.VMEM((rows, 8, BLOCK + 2 * HALO), full),
        pltpu.VMEM((total, width), low),
        pltpu.VMEM((rows, HALO, width), low),
        dma((rows + 6,)),
        dma((4, rows)),
        dma((3, 2)),
        dma((3, 2)),
        dma((4,)),
        dma((4,)),
        *[dma((12,))] * 8,
        dma((24,)),
        dma((dp_size // 2 + 2,)),
        dma((dp_size // 2 + 2,)),
    ]
    anywhere = pl.BlockSpec(memory_space=pl.ANY)
    vmem = pl.BlockSpec(memory_space=pltpu.VMEM)
    row = lambda vector: vector.reshape(1, -1)
    return pl.pallas_call(
        lambda *refs: forward_kernel(dp_size, gathers, *refs),
        out_shape=out_shape,
        in_specs=[pl.BlockSpec(memory_space=pltpu.SMEM)] + [anywhere] * 8 + [vmem] * 6,
        out_specs=[anywhere, vmem] + [anywhere] * (len(saved) + 1),
        scratch_shapes=scratch,
        compiler_params=pltpu.CompilerParams(
            collective_id=2, has_side_effects=True, vmem_limit_bytes=64 * 1024 * 1024 - 65536
        ),
        name="forward",
    )(
        lengths,
        tokens,
        w_qkv.reshape(3, 2, width // 2, head_cols),
        w_out.reshape(2, head_cols // 2, width),
        w_in.reshape(4, 2, width // 8, width),
        w_back.reshape(4, 2, width // 8, width),
        b_qv,
        row(b_in),
        masks,
        row(b_out),
        row(ln1[0]),
        row(ln1[1]),
        row(b_back),
        row(ln2[0]),
        row(ln2[1]),
    )


class Reducer:
    def __init__(self, at, bufs):
        self.at = at
        self.pieces = pieces_of(at.depth)
        self.plane = self.pieces == at.depth
        self.ready = 0
        (
            self.parts,
            self.core_in,
            self.y_in,
            self.x_in,
            self.z_in,
            self.whole,
            self.done,
            self.core_s,
            self.core_r,
            self.y_s,
            self.y_r,
            self.x_s,
            self.x_r,
            self.z_s,
            self.z_r,
            self.za_s,
            self.za_r,
            self.xa_s,
            self.xa_r,
            self.own_s,
            self.out_s,
        ) = bufs

    def core_copy(self, u):
        at = self.at
        return remote(
            self.parts.at[1, :, u],
            self.core_in.at[:, u],
            self.core_s.at[u],
            self.core_r.at[u],
            at.across_core,
        )

    def y_copy(self, u):
        at = self.at
        return remote(
            self.parts.at[0, 1, u],
            self.y_in.at[u],
            self.y_s.at[u],
            self.y_r.at[u],
            at.across_y,
        )

    def x_copy(self, u):
        return remote(
            self.parts.at[0, 0, u, 1],
            self.x_in.at[u],
            self.x_s.at[u],
            self.x_r.at[u],
            self.at.across_x,
        )

    def z_copy(self, u, step):
        at = self.at
        return remote(
            self.parts.at[0, 0, u, 0, (at.z + step) % at.depth],
            self.z_in.at[u, step - 1],
            self.z_s.at[u, step - 1],
            self.z_r.at[u, step - 1],
            at.along_z(step),
        )

    def za_copy(self, u, step):
        at = self.at
        return remote(
            self.done.at[u],
            self.whole.at[u, 0, at.z],
            self.za_s.at[u, step - 1],
            self.za_r.at[u, step - 1],
            at.along_z(step),
        )

    def own_copy(self, u):
        return pltpu.make_async_copy(
            self.done.at[u], self.whole.at[u, 0, self.at.z], self.own_s.at[u]
        )

    def xa_copy(self, u):
        return remote(
            self.whole.at[u, 0],
            self.whole.at[u, 1],
            self.xa_s.at[u],
            self.xa_r.at[u],
            self.at.across_x,
        )

    def out_copies(self, u, out):
        held = self.whole.at[u] if self.plane else self.parts.at[0, 0, u]
        return [
            pltpu.make_async_copy(
                held.at[half],
                out.at[u, :, :, pl.ds(pl.multiple_of(side * 384, 128), 384)],
                self.out_s.at[u, half],
            )
            for half, side in ((0, self.at.x), (1, 1 - self.at.x))
        ]

    def add(self, place, source, at):
        @pl.loop(0, self.pieces)
        def _(p):
            mine = self.parts[(*place, p)].astype(jnp.float32)
            both = mine + source[(*at, p)].astype(jnp.float32)
            self.parts[(*place, p)] = both.astype(jnp.bfloat16)

    def start(self, u):
        self.core_copy(u).start()

    def add_far(self, u):
        self.core_copy(u).wait_recv()
        for half in range(2):
            self.add((0, 1, u, half), self.core_in, (1, u, half))
        self.y_copy(u).start()

    def add_near(self, u):
        for half in range(2):
            self.add((0, 0, u, half), self.core_in, (0, u, half))

    def add_y(self, u):
        self.y_copy(u).wait_recv()
        self.add((0, 0, u, 1), self.y_in, (u, 1))
        if self.plane:
            self.x_copy(u).start()
        self.add((0, 0, u, 0), self.y_in, (u, 0))

    def add_x(self, u):
        self.x_copy(u).wait_recv()
        self.add((0, 0, u, 0), self.x_in, (u,))
        for step in range(1, self.at.depth):
            self.z_copy(u, step).start()

    def add_z(self, u):
        at = self.at
        total = self.parts[0, 0, u, 0, at.z].astype(jnp.float32)
        for step in range(1, at.depth):
            self.z_copy(u, step).wait_recv()
            total = total + self.z_in[u, step - 1].astype(jnp.float32)
        self.done[u] = total.astype(jnp.bfloat16)
        for step in range(1, at.depth):
            self.za_copy(u, step).start()
        self.own_copy(u).start()

    def spread_x(self, u):
        self.own_copy(u).wait()
        for step in range(1, self.at.depth):
            self.za_copy(u, step).wait_recv()
        self.xa_copy(u).start()

    def finish(self, u, out):
        if self.plane:
            self.xa_copy(u).wait_recv()
        for copy in self.out_copies(u, out):
            copy.start()

    def drain(self, u, out):
        self.core_copy(u).wait_send()
        self.y_copy(u).wait_send()
        for copy in self.out_copies(u, out):
            copy.wait()
        if not self.plane:
            return
        self.x_copy(u).wait_send()
        self.xa_copy(u).wait_send()
        for step in range(1, self.at.depth):
            self.z_copy(u, step).wait_send()
            self.za_copy(u, step).wait_send()


def pieces_of(depth):
    return depth if UNIT % (16 * depth) == 0 else 4


def reducer_scratch(depth):
    lanes = max(depth - 1, 1)
    depth = pieces_of(depth)
    rows = UNIT // depth
    dma = pltpu.SemaphoreType.DMA
    low = jnp.bfloat16
    return [
        pltpu.VMEM((2, 2, UNITS, 2, depth, rows, 384), low),
        pltpu.VMEM((2, UNITS, 2, depth, rows, 384), low),
        pltpu.VMEM((UNITS, 2, depth, rows, 384), low),
        pltpu.VMEM((UNITS, depth, rows, 384), low),
        pltpu.VMEM((UNITS, lanes if depth == lanes + 1 else 1, rows, 384), low),
        pltpu.VMEM((UNITS, 2, depth, rows, 384), low),
        pltpu.VMEM((UNITS, rows, 384), low),
        *[dma((UNITS,))] * 6,
        *[dma((UNITS, lanes if depth == lanes + 1 else 1))] * 4,
        *[dma((UNITS,))] * 3,
        dma((UNITS, 2)),
    ]


class Ring:
    def __init__(self, slots, sem, sources):
        self.slots, self.sem, self.sources = slots, sem, sources
        self.count = len(slots)
        self.used = 0
        for i in range(min(self.count, len(sources))):
            self.copy(i).start()

    def copy(self, i):
        return pltpu.make_async_copy(
            self.sources[i], self.slots[i % self.count], self.sem.at[i]
        )

    def take(self):
        self.copy(self.used).wait()
        return self.slots[self.used % self.count]

    def free(self):
        ahead = self.used + self.count
        if ahead < len(self.sources):
            self.copy(ahead).start()
        self.used += 1


def backward_kernel(dp_size, *refs):
    (
        lengths_ref,
        cls_grad,
        gain1,
        gain2,
        cot_hbm,
        wq_hbm,
        wo_hbm,
        wi_hbm,
        wb_hbm,
        tok_hbm,
        q_hbm,
        k_hbm,
        v_hbm,
        p_hbm,
        o_hbm,
        h1_hbm,
        n1_hbm,
        r1_hbm,
        g_hbm,
        gp_hbm,
        n2_hbm,
        r2_hbm,
        own_hbm,
        sums_hbm,
        grad_hbm,
        vec_out,
        own,
        cot,
        unit,
        inv1,
        inv2,
        acc,
        df,
        turned,
        h1,
        tok,
        q,
        k,
        v,
        probs,
        o,
        wo,
        w0,
        w1,
        w2,
        wq0,
        wq1,
        g0,
        g1,
        gp0,
        gp1,
        du,
        do,
        dq_pad,
        dkv,
        dqkv,
        vec,
        vec_in,
        vec_z,
        halo_in,
        load_sem,
        g_sem,
        w_sem,
        gp_sem,
        wq_sem,
        halo_sem,
        vec_s,
        vec_r,
        *bufs,
    ) = refs
    at = Places(dp_size)
    red = Reducer(at, bufs)
    rows, share, width = cot_hbm.shape
    region = share + HALO
    total = rows * region
    m = at.mp
    first = m * share
    left = (at.dp, (m + 3) % 4)
    right = (at.dp, (m + 1) % 4)
    order = (1, 3, 2, 0)
    true_shard = shard_order(at)

    def loading(i, src, dst):
        return pltpu.make_async_copy(src, dst, load_sem.at[i])

    cots = [
        loading(r, cot_hbm.at[r], cot.at[pl.ds(r * region, share)]) for r in range(rows)
    ]
    early = cots + [
        loading(rows + i, src, dst)
        for i, (src, dst) in enumerate(
            [(own_hbm, own), (n2_hbm, unit), (r2_hbm, inv2), (r1_hbm, inv1)]
        )
    ]
    for copy in early:
        copy.start()
    g_ring = Ring((g0, g1), g_sem, [g_hbm.at[s] for s in order])
    w_sources = [ref.at[s] for s in order for ref in (wb_hbm, wi_hbm)]
    w_ring = Ring((w0, w1, w2), w_sem, w_sources)
    gp_ring = Ring((gp0, gp1), gp_sem, [gp_hbm.at[s] for s in order])
    late = [
        loading(rows + 4 + i, src, dst)
        for i, (src, dst) in enumerate(
            [
                (h1_hbm, h1),
                (tok_hbm, tok),
                (o_hbm, o),
                (wo_hbm, wo),
                (q_hbm, q),
                (k_hbm, k),
                (v_hbm, v),
                (p_hbm, probs),
            ]
        )
    ]
    for copy in late:
        copy.start()
    wq_ring = Ring((wq0, wq1), wq_sem, [wq_hbm.at[s] for s in order])

    peers = [(at.dp, (m + j) % 4) for j in range(1, 4)] + [at.across_x]
    greet(peers + [at.along_z(step) for step in range(1, at.depth)])
    halos = [
        remote(
            cot_hbm.at[r, pl.ds(0, HALO)],
            cot.at[pl.ds(r * region + share, HALO)],
            halo_sem.at[0, r],
            halo_sem.at[1, r],
            left,
        )
        for r in range(rows)
    ]
    for copy in halos:
        copy.start()

    expected = []
    for u in range(UNITS):
        arrives = 11.5 + 6.3 * (u + 1)
        expected.append((arrives, u, red.add_y))
        if red.plane:
            expected.append((arrives + 5.0, u, red.add_x))
            expected.append((arrives + 11.0, u, red.add_z))
            expected.append((arrives + 17.0, u, red.spread_x))
        expected.append((arrives + 22.0, u, lambda u: red.finish(u, sums_hbm)))
    expected.sort(key=lambda event: event[0])

    def pump(until):
        while expected and expected[0][0] <= until and expected[0][1] < red.ready:
            _, u, event = expected.pop(0)
            event(u)

    vec[0] = jnp.zeros(vec.shape[1:], jnp.float32)
    slots = cls_grad.shape[0] // rows
    for copy in early:
        copy.wait()
    for copy in halos:
        copy.wait()

    def norm_back(part, grad, gain, inv, base):
        normed, inv_dev = unit[part], inv[part]
        scaled = grad * gain[...]
        centered = scaled - jnp.mean(scaled, axis=-1, keepdims=True)
        inner = jnp.mean(scaled * normed, axis=-1, keepdims=True)
        grad_in = inv_dev * (centered - normed * inner)
        acc[part] = grad_in
        df[part] = grad_in.astype(jnp.bfloat16)
        vec[0, base : base + 1] += jnp.sum(grad_in, axis=0, keepdims=True)
        vec[0, base + 1 : base + 2] += jnp.sum(grad * normed, axis=0, keepdims=True)
        vec[0, base + 2 : base + 3] += jnp.sum(grad, axis=0, keepdims=True)

    tile = 96
    for r in range(rows):
        starts = start_row(lengths_ref, r, first, slots)
        come = cls_grad[r * slots : (r + 1) * slots]
        terms = []
        for _ in range(3):
            term = come.astype(jnp.bfloat16)
            terms.append(term)
            come = come - term.astype(jnp.float32)

        @pl.loop(0, region // tile)
        def _(i):
            part = pl.ds(pl.multiple_of(r * region + i * tile, 32), tile)
            place = i * tile + lax.broadcasted_iota(jnp.int32, (tile, slots), 0)
            hit = (place == starts) & (place < share)
            pick = jnp.where(hit, 1.0, 0.0).astype(jnp.bfloat16)
            grad = cot[part].astype(jnp.float32)
            for term in terms:
                grad = grad + nn(pick, term)
            norm_back(part, grad * own[part], gain2, inv2, 3)

    first_unit = pltpu.make_async_copy(n1_hbm, unit, load_sem.at[1])
    first_unit.start()

    def put(s, u, half, values):
        low = values.astype(jnp.bfloat16)
        for i in range(values.shape[0] // UNIT):
            red.parts[s % 2, s // 2, u + i, half] = low[i * UNIT : (i + 1) * UNIT].reshape(
                red.pieces, UNIT // red.pieces, 384
            )

    def true_half(half):
        return (at.x + half) % 2

    def true_columns(half):
        return pl.ds(pl.multiple_of(true_half(half) * 384, 128), 384)

    def sent(i, units):
        if i == 1:
            for u in units:
                red.start(u)
        if i == 2:
            for u in units:
                red.add_far(u)
        if i == 3:
            for u in units:
                red.add_near(u)
            red.ready = units[-1] + 1

    for i in range(4):
        g = g_ring.take()
        turned[...] = g[...].T
        g_ring.free()

        @pl.loop(0, 2)
        def _(half):
            put(order[i], 0, half, nn(turned[...], df[:, true_columns(half)]))

        sent(i, range(4))
    late[0].wait()
    turned[...] = h1[...].T
    for i in range(4):
        s = order[i]
        wb = w_ring.take()
        slope = gp_ring.take()

        @pl.loop(0, 2)
        def _(half):
            columns = true_columns(half)
            rows_here = pl.ds(2 * true_half(half), 2)
            rise = nt(df[...], wb[rows_here].reshape(384, width))
            rise = (rise * slope[:, columns].astype(jnp.float32)).astype(jnp.bfloat16)
            du[:, columns] = rise
            vec[0, pl.ds(6 + true_shard[s], 1), columns] = jnp.sum(
                rise.astype(jnp.float32), axis=0, keepdims=True
            )
            put(s, 4, half, nn(turned[...], rise))

        w_ring.free()
        gp_ring.free()
        wi = w_ring.take()
        sent(i, range(4, 8))

        @pl.loop(0, rows)
        def _(r):
            part = pl.ds(pl.multiple_of(r * region, 32), region)
            acc[part] = acc[part] + nt(du[part], wi[...].reshape(width, width))

        w_ring.free()
        pump(20.0 + 7.5 * i)

    first_unit.wait()

    @pl.loop(0, total // tile)
    def _(i):
        part = pl.ds(pl.multiple_of(i * tile, tile), tile)
        norm_back(part, acc[part], gain1, inv1, 0)

    for copy in late[1:]:
        copy.wait()
    pump(46.0)

    heads = q.shape[3] // HDIM
    cols = heads * HDIM
    blocks = q.shape[2] // BLOCK
    for i in range(4):
        s = order[i]
        flat = jnp.concatenate([o[s, r, :region] for r in range(rows)], axis=0)
        for half in range(2):
            put(s, 8, half, tn(flat, df[:, true_columns(half)]))
        sent(i, [8])
    pump(50.0)
    do[...] = jnp.zeros_like(do)
    for i in range(4):
        s = order[i]
        back = nt(df[...], wo[s].reshape(cols, width)).astype(jnp.bfloat16)
        for r in range(rows):
            do[r, :region] = back[r * region : (r + 1) * region]
        dkv[...] = jnp.zeros_like(dkv)
        @pl.loop(0, blocks)
        def _(b):
            here = pl.ds(pl.multiple_of(b * BLOCK, BLOCK), BLOCK)
            window = pl.ds(pl.multiple_of(b * BLOCK, BLOCK), BLOCK + 2 * HALO)
            for r in range(rows):
                grads = head_stack(do[r, here])
                queries = head_stack(q[s, r, here])
                weight = probs[s, r * blocks + b]
                wide = weight.astype(jnp.float32)
                rise = nt(grads, v[s, r, window])
                inner = jnp.sum(wide * rise, axis=1, keepdims=True)
                fall = (wide * (rise - inner)).astype(jnp.bfloat16)
                dq = head_pick(nn(fall, k[s, r, window]), cols) * 0.125
                dq_pad[r, here] = dq.astype(jnp.bfloat16)
                dkv[0, r, window] += tn(fall, queries)
                dkv[1, r, window] += tn(weight, grads)

        for r in range(rows):
            dqkv[0, r * region : (r + 1) * region] = dq_pad[r, :region]
            for t in range(2):
                dqkv[1 + t, r * region : (r + 1) * region] = dkv[
                    t, r, HALO : HALO + region
                ].astype(jnp.bfloat16)
        wqs = wq_ring.take()
        for t, lane in ((0, 0), (1, None), (2, 256)):
            part = dqkv[t]
            if lane is not None:
                vec[0, pl.ds(10 + true_shard[s], 1), lane : lane + cols] = jnp.sum(
                    part.astype(jnp.float32), axis=0, keepdims=True
                )
            for half in range(2):
                put(s, 9 + t, half, tn(part, tok[:, true_columns(half)]))
            acc[...] += nt(part, wqs[t].reshape(width, cols))
        wq_ring.free()
        sent(i, range(9, 12))
        pump(59.0 + 10.0 * i)

    def mask_grad(part):
        acc[part] = acc[part] * own[part]

    norm_tiles(total, tile, mask_grad)
    settled = [
        remote(
            acc.at[pl.ds(r * region + share, HALO)],
            halo_in.at[r],
            halo_sem.at[2, r],
            halo_sem.at[3, r],
            right,
        )
        for r in range(rows)
    ]
    for copy in settled:
        copy.start()

    def vec_copy(i):
        device = (at.across_core, at.across_y, at.across_x)[i]
        return remote(vec.at[i], vec_in.at[i], vec_s.at[i], vec_r.at[i], device)

    def vec_z_copy(step):
        index = 2 + step
        return remote(
            vec.at[3], vec_z.at[step], vec_s.at[index], vec_r.at[index], at.along_z(step)
        )

    vec_copy(0).start()
    pump(94.0)
    grads = []
    for copy in settled:
        copy.wait()
    for r in range(rows):
        head = pl.ds(r * region, HALO)
        acc[head] = acc[head] + halo_in[r]
    for r in range(rows):
        copy = loading(r, acc.at[pl.ds(r * region, share)], grad_hbm.at[r])
        copy.start()
        grads.append(copy)
    for i in range(3):
        vec_copy(i).wait_recv()
        both = vec[i] + vec_in[i]
        if i < 2:
            vec[i + 1] = both
            vec_copy(i + 1).start()
        else:
            vec[3] = both
            vec_z[0] = both
            for step in range(1, at.depth):
                vec_z_copy(step).start()
        pump(97.0 + 4.0 * i)
    for step in range(1, at.depth):
        vec_z_copy(step).wait_recv()
    both = vec_z[at.back_z(0)]
    for z in range(1, at.depth):
        both = both + vec_z[at.back_z(z)]
    vec_out[...] = both
    pump(1000.0)
    for copy in grads:
        copy.wait()
    for i in range(3):
        vec_copy(i).wait_send()
    for step in range(1, at.depth):
        vec_z_copy(step).wait_send()

    @pl.loop(0, UNITS)
    def _(u):
        red.drain(u, sums_hbm)


def start_row(lengths_ref, row, first, slots):
    slot = lax.broadcasted_iota(jnp.int32, (1, slots), 1)

    def body(j, carry):
        line, begin = carry
        return (jnp.where(slot == j, begin - first, line), begin + lengths_ref[row, j])

    line, _ = lax.fori_loop(
        0, lengths_ref.shape[1], body, (jnp.full((1, slots), -1, jnp.int32), jnp.int32(0))
    )
    return line


def backward(lengths, cls_grad, gain1, gain2, cotangent, saved, dp_size):
    rows, share, width = cotangent.shape
    region = share + HALO
    total = rows * region
    q, k, probs, o = saved[5], saved[6], saved[8], saved[9]
    depth = dp_size // 2
    low, full = jnp.bfloat16, jnp.float32
    cols = q.shape[3]
    dma = pltpu.SemaphoreType.DMA
    vmem = pltpu.VMEM
    scratch = [
        vmem((total, 1), full),
        vmem((total, width), low),
        vmem((total, width), full),
        vmem((total, 1), full),
        vmem((total, 1), full),
        vmem((total, width), full),
        vmem((total, width), low),
        vmem((width, total), low),
        vmem((total, width), low),
        vmem((total, width), low),
        vmem(q.shape, low),
        vmem(k.shape, low),
        vmem(k.shape, low),
        vmem(probs.shape, low),
        vmem(o.shape, low),
        vmem(saved[1].shape, low),
        *[vmem(saved[2].shape[1:], low)] * 3,
        *[vmem(saved[0].shape[1:], low)] * 2,
        *[vmem((total, width), low)] * 4,
        vmem((total, width), low),
        vmem(q.shape[1:], low),
        vmem(q.shape[1:], low),
        vmem((2, *k.shape[1:]), full),
        vmem((3, total, cols), low),
        vmem((4, 16, width), full),
        vmem((3, 16, width), full),
        vmem((depth, 16, width), full),
        vmem((rows, HALO, width), full),
        dma((rows + 12,)),
        *[dma((8,))] * 4,
        dma((4, rows)),
        dma((2 + depth,)),
        dma((2 + depth,)),
    ] + reducer_scratch(depth)
    anywhere = pl.BlockSpec(memory_space=pl.ANY)
    in_vmem = pl.BlockSpec(memory_space=pltpu.VMEM)
    shape = jax.ShapeDtypeStruct
    return pl.pallas_call(
        lambda *refs: backward_kernel(dp_size, *refs),
        out_shape=[
            shape((UNITS, pieces_of(depth), UNIT // pieces_of(depth), width), low),
            shape((rows, share, width), full),
            shape((16, width), full),
        ],
        in_specs=[pl.BlockSpec(memory_space=pltpu.SMEM)] + [in_vmem] * 3 + [anywhere] * 19,
        out_specs=[anywhere, anywhere, in_vmem],
        scratch_shapes=scratch,
        compiler_params=pltpu.CompilerParams(
            collective_id=1, has_side_effects=True, vmem_limit_bytes=64 * 1024 * 1024 - 65536
        ),
        name="backward",
    )(lengths, cls_grad, gain1.reshape(1, -1), gain2.reshape(1, -1), cotangent, *saved)


def contrast_kernel(dp_size, sents, *refs):
    (
        cls_ref,
        b_pool,
        w_hbm,
        masks_hbm,
        loss_ref,
        w_grad,
        b_grad,
        cls_grad,
        w_pool,
        masks,
        rows_in,
        mine,
        every,
        views,
        pooled,
        units,
        inverse,
        logit_grad,
        lowered,
        load_sem,
        rs_s,
        rs_r,
        own_sem,
        z_s,
        z_r,
        hop_s,
        hop_r,
    ) = refs
    at = Places(dp_size)
    width = w_pool.shape[0]
    slots = views.shape[1]
    group = slots // dp_size
    share = group // 4
    loads = [
        pltpu.make_async_copy(w_hbm, w_pool, load_sem.at[0]),
        pltpu.make_async_copy(masks_hbm, masks, load_sem.at[1]),
    ]
    for load in loads:
        load.start()
    others = [(at.dp, (at.mp + j) % 4) for j in range(1, 4)]
    greet(others + [at.across_x] + [at.along_z(step) for step in range(1, at.depth)])

    quarters = [
        remote(
            cls_ref.at[(at.mp + j) % 4],
            rows_in.at[j - 1],
            rs_s.at[j - 1],
            rs_r.at[j - 1],
            others[j - 1],
        )
        for j in range(1, 4)
    ]
    for copy in quarters:
        copy.start()
    total = cls_ref[at.mp].astype(jnp.float32)
    for j, copy in enumerate(quarters):
        copy.wait_recv()
        total = total + rows_in[j].astype(jnp.float32)
    mine[...] = total.astype(jnp.bfloat16)

    place = every.at[at.z, at.x, at.y, at.core]
    own = pltpu.make_async_copy(mine, place, own_sem)
    own.start()
    along = [
        remote(mine, place, z_s.at[step - 1], z_r.at[step - 1], at.along_z(step))
        for step in range(1, at.depth)
    ]
    for copy in along:
        copy.start()
    own.wait()
    for copy in along:
        copy.wait_recv()
    hops = []
    for i, (part, device) in enumerate(
        [
            (every.at[:, at.x, at.y, at.core], at.across_x),
            (every.at[:, :, at.y, at.core], at.across_y),
            (every.at[:, :, :, at.core], at.across_core),
        ]
    ):
        hop = remote(part, part, hop_s.at[i], hop_r.at[i], device)
        hop.start()
        hop.wait_recv()
        hops.append(hop)
    for load in loads:
        load.wait()

    per_z = slots // at.depth
    for t in range(2):
        for z in range(at.depth):
            part = slice(z * per_z, (z + 1) * per_z)
            cls_rows = every[z].reshape(per_z, width).astype(jnp.float32)
            keep = masks[z, :, t].reshape(per_z, width).astype(jnp.float32)
            view = (cls_rows * keep * KEEP_SCALE).astype(jnp.bfloat16)
            views[t, part] = view
            unit = jnp.tanh(nn(view, w_pool[...]) + b_pool[...])
            pooled[t, part] = unit
            inv = lax.rsqrt(jnp.sum(unit * unit, axis=-1, keepdims=True) + 1e-06)
            inverse[t, part] = inv
            units[t, part] = (unit * inv).astype(jnp.bfloat16)

    def real(index):
        return index % 32 < sents

    loss = jnp.zeros((1, 1), jnp.float32)
    for z in range(at.depth):
        part = slice(z * per_z, (z + 1) * per_z)
        logits = nt(units[0, part], units[1]) * 20.0
        line = z * per_z + lax.broadcasted_iota(jnp.int32, logits.shape, 0)
        column = lax.broadcasted_iota(jnp.int32, logits.shape, 1)
        logits = jnp.where(real(column), logits, MASKED)
        peak = jnp.max(logits, axis=1, keepdims=True)
        raised = jnp.exp(logits - peak)
        row_total = jnp.sum(raised, axis=1, keepdims=True)
        partner = line == column
        chosen = jnp.sum(jnp.where(partner, logits, 0.0), axis=1, keepdims=True)
        row_loss = peak + jnp.log(row_total) - chosen
        row_loss = jnp.where(real(line[:, :1]), row_loss, 0.0)
        loss = loss + jnp.sum(row_loss, axis=0, keepdims=True)
        grad = raised / row_total - jnp.where(partner, 1.0, 0.0)
        logit_grad[part] = jnp.where(real(line), grad, 0.0).astype(jnp.bfloat16)
    count = slots // 32 * sents
    loss_ref[...] = jnp.broadcast_to(loss / count, loss_ref.shape)

    bias = jnp.zeros((1, width), jnp.float32)
    for t in range(2):
        for z in range(at.depth):
            part = slice(z * per_z, (z + 1) * per_z)
            if t == 0:
                unit_grad = nn(logit_grad[part], units[1]) * 20.0
            else:
                unit_grad = tn(logit_grad[:, part], units[0]) * 20.0
            before = pooled[t, part]
            inv = inverse[t, part]
            unit = before * inv
            inner = jnp.sum(unit_grad * unit, axis=-1, keepdims=True)
            grad = inv * (unit_grad - unit * inner) * (1.0 - before * before)
            low = grad.astype(jnp.bfloat16)
            lowered[t, part] = low
            bias = bias + jnp.sum(low.astype(jnp.float32), axis=0, keepdims=True)
    b_grad[...] = bias

    here = pl.ds(pl.multiple_of(at.dp * group, group), group)
    back = jnp.zeros((group, width), jnp.float32)
    for t in range(2):
        keep = masks[at.z, at.x, t].astype(jnp.float32)
        back = back + nt(lowered[t, here], w_pool[...]) * keep
    cls_grad[...] = back * KEEP_SCALE
    for half in range(2):
        columns = slice(half * width // 2, (half + 1) * width // 2)
        w_grad[:, columns] = tn(views[0], lowered[0, :, columns]) + tn(
            views[1], lowered[1, :, columns]
        )
    for copy in quarters + along + hops:
        copy.wait_send()


def contrast_whole(cls_part, masks, w_pool, b_pool, dp_size, sents):
    group, width = cls_part.shape
    slots = group * dp_size
    depth = dp_size // 2
    share = group // 4
    low, full = jnp.bfloat16, jnp.float32
    dma = pltpu.SemaphoreType.DMA
    vmem = pltpu.VMEM
    anywhere = pl.BlockSpec(memory_space=pl.ANY)
    in_vmem = pl.BlockSpec(memory_space=pltpu.VMEM)
    shape = jax.ShapeDtypeStruct
    return pl.pallas_call(
        lambda *refs: contrast_kernel(dp_size, sents, *refs),
        out_shape=[
            shape((8, 128), full),
            shape((width, width), full),
            shape((1, width), full),
            shape((group, width), full),
        ],
        in_specs=[in_vmem, in_vmem, anywhere, anywhere],
        out_specs=[in_vmem] * 4,
        scratch_shapes=[
            vmem((width, width), low),
            vmem(masks.shape, low),
            vmem((3, share, width), low),
            vmem((share, width), low),
            vmem((depth, 2, 2, 2, share, width), low),
            vmem((2, slots, width), low),
            vmem((2, slots, width), full),
            vmem((2, slots, width), low),
            vmem((2, slots, 1), full),
            vmem((slots, slots), low),
            vmem((2, slots, width), low),
            dma((2,)),
            dma((3,)),
            dma((3,)),
            dma,
            dma((max(depth - 1, 1),)),
            dma((max(depth - 1, 1),)),
            dma((3,)),
            dma((3,)),
        ],
        compiler_params=pltpu.CompilerParams(
            collective_id=3, has_side_effects=True, vmem_limit_bytes=60 * 1024 * 1024
        ),
        name="contrast",
    )(cls_part.reshape(4, share, width), b_pool.reshape(1, -1), w_pool, masks)


def shards(
    tokens,
    lengths,
    view_masks,
    w_qkv,
    b_qv,
    w_out,
    b_out,
    ln1_gain,
    ln1_bias,
    w_in,
    b_in,
    w_back,
    b_back,
    ln2_gain,
    ln2_bias,
    w_pool,
    b_pool,
    cotangent,
):
    rows, share, width = tokens.shape
    ranks = lax.axis_size("dp")
    sents = lengths.shape[1]
    gathers = ranks * rows * 32 <= 1024
    masks = jnp.pad(view_masks, [(0, 0), (0, 32 - sents), (0, 0), (0, 0)]).astype(jnp.bfloat16)
    masks = masks.transpose(2, 0, 1, 3).reshape(2, rows * 32, width)
    hidden, cls_part, *saved, masks = forward(
        tokens, lengths, w_qkv, b_qv, w_out, b_out, (ln1_gain, ln1_bias), w_in, b_in, w_back,
        b_back, (ln2_gain, ln2_bias), masks, ranks, gathers,
    )
    if gathers:
        loss, w_pool_grad, b_pool_grad, cls_grad = contrast_whole(
            cls_part, masks, w_pool, b_pool, ranks, sents
        )
        loss, b_pool_grad = loss[0, 0], b_pool_grad[0]
    else:
        cls_rows = cls_part.reshape(rows, -1, width)[:, :sents]
        cls_rows = lax.psum(cls_rows, "mp").astype(jnp.float32)
        loss, w_pool_grad, b_pool_grad, cls_grad = contrast(
            cls_rows.reshape(-1, width), view_masks, w_pool, b_pool
        )
        cls_grad = cls_grad.reshape(rows, -1, width)
        cls_grad = jnp.pad(cls_grad, [(0, 0), (0, 32 - sents), (0, 0)]).reshape(-1, width)
    sums, token_grad, vectors = backward(
        lengths, cls_grad, ln1_gain, ln2_gain, cotangent, saved, ranks
    )
    if pieces_of(ranks // 2) != ranks // 2:
        sums = lax.psum(sums, "dp")
    sums = sums.reshape(UNITS, UNIT, width).astype(jnp.float32)
    own = lax.axis_index("mp")
    cols = b_qv.shape[1]
    own_qv = lax.dynamic_slice_in_dim(vectors, 10 + own, 1, axis=0)
    own_in = lax.dynamic_slice_in_dim(vectors, 6 + own, 1, axis=0)
    return (
        hidden,
        loss,
        token_grad,
        sums[9:12].transpose(0, 2, 1),
        jnp.concatenate([own_qv[:, :cols], own_qv[:, 256 : 256 + cols]], axis=0),
        sums[8],
        vectors[0],
        vectors[1],
        vectors[2],
        sums[4:8].reshape(width, width),
        own_in[0],
        sums[0:4].reshape(width, width),
        vectors[3],
        vectors[4],
        vectors[5],
        w_pool_grad,
        b_pool_grad,
    )


def solution(mesh):
    in_specs = (
        P("dp", "mp", None),
        P("dp", None),
        P("dp", None, None, None),
        P(None, None, "mp"),
        P(None, "mp"),
        P("mp", None),
        P(),
        P(),
        P(),
        P(None, "mp"),
        P("mp"),
        P("mp", None),
        P(),
        P(),
        P(),
        P(),
        P(),
        P("dp", "mp", None),
    )
    out_specs = (
        P("dp", "mp", None),
        P(),
        P("dp", "mp", None),
        P(None, None, "mp"),
        P(None, "mp"),
        P("mp", None),
        P(),
        P(),
        P(),
        P(None, "mp"),
        P("mp"),
        P("mp", None),
        P(),
        P(),
        P(),
        P(),
        P(),
    )
    return jax.shard_map(shards, mesh=mesh, in_specs=in_specs, out_specs=out_specs, check_vma=False)
```

```python
import jax
import jax.numpy as jnp
from jax import lax
from jax.experimental import pallas as pl
from jax.experimental.pallas import tpu as pltpu
from jax.sharding import PartitionSpec as P

HDIM = 64
HALO = 32
BLOCK = 64
KEEP_SCALE = 1.0 / 0.9
MASKED = -1000000000.0


def norm_forward(values, gain, shift):
    center = values - jnp.mean(values, axis=-1, keepdims=True)
    inv_dev = lax.rsqrt(jnp.mean(center * center, axis=-1, keepdims=True) + 1e-12)
    normed = center * inv_dev
    return (normed * gain + shift, normed, inv_dev)


def dot32(equation, left, right):
    return jnp.einsum(equation, left, right, preferred_element_type=jnp.float32)


def contrast(cls_rows, view_masks, w_pool, b_pool):
    local_sents = cls_rows.shape[0]
    own_ids = lax.axis_index("dp") * local_sents + jnp.arange(local_sents, dtype=jnp.int32)
    keep_masks = view_masks.astype(jnp.float32).reshape(local_sents, 2, -1)
    views = (cls_rows[:, None, :] * keep_masks * KEEP_SCALE).astype(jnp.bfloat16)
    pooled = jnp.tanh(dot32("svd,de->sve", views, w_pool) + b_pool)
    inv_length = lax.rsqrt(jnp.sum(pooled * pooled, axis=-1, keepdims=True) + 1e-06)
    unit = pooled * inv_length
    unit_low = unit.astype(jnp.bfloat16)
    anchors = unit_low[:, 0]
    every_target = lax.all_gather(unit_low[:, 1], "dp", axis=0, tiled=True)
    logits = dot32("sd,td->st", anchors, every_target) * 20.0
    sent_ids = jnp.arange(every_target.shape[0], dtype=jnp.int32)
    is_partner = sent_ids[None, :] == own_ids[:, None]
    row_peak = jnp.max(logits, axis=1, keepdims=True)
    raised = jnp.exp(logits - row_peak)
    row_total = jnp.sum(raised, axis=1, keepdims=True)
    log_total = row_peak[:, 0] + jnp.log(row_total[:, 0])
    loss_local = jnp.sum(log_total - jnp.sum(jnp.where(is_partner, logits, 0.0), axis=1))
    logit_grad = (raised / row_total - is_partner.astype(jnp.float32)).astype(jnp.bfloat16)
    anchor_grad = dot32("st,td->sd", logit_grad, every_target) * 20.0
    target_terms = dot32("st,sd->td", logit_grad, anchors) * 20.0
    target_grad = lax.psum_scatter(target_terms, "dp", scatter_dimension=0, tiled=True)
    unit_grad = jnp.stack([anchor_grad, target_grad], axis=1)
    pooled_grad = inv_length * (
        unit_grad - unit * jnp.sum(unit_grad * unit, axis=-1, keepdims=True)
    )
    before_grad = (pooled_grad * (1.0 - pooled * pooled)).astype(jnp.bfloat16)
    w_pool_grad = dot32("svd,sve->de", views, before_grad)
    b_pool_grad = jnp.sum(before_grad, axis=(0, 1), dtype=jnp.float32)
    view_grad = dot32("sve,de->svd", before_grad, w_pool)
    cls_grad = jnp.sum(view_grad * keep_masks, axis=1) * KEEP_SCALE
    sums = lax.psum((w_pool_grad, b_pool_grad, loss_local), "dp")
    loss = sums[2] / (local_sents * lax.axis_size("dp"))
    return (loss, sums[0], sums[1], cls_grad)


MESH = pl.DeviceIdType.MESH
UNIT = 192
UNITS = 12


def greet(peers):
    barrier = pltpu.get_barrier_semaphore()
    for peer in peers:
        pl.semaphore_signal(barrier, inc=1, device_id=peer, device_id_type=MESH)
    pl.semaphore_wait(barrier, len(peers))


class Places:
    def __init__(self, dp_size):
        self.dp = lax.axis_index("dp")
        self.mp = lax.axis_index("mp")
        self.core = self.mp % 2
        self.y = self.mp // 2
        self.x = self.dp % 2
        self.z = self.dp // 2
        self.depth = dp_size // 2
        self.across_core = (self.dp, self.y * 2 + (1 - self.core))
        self.across_y = (self.dp, (1 - self.y) * 2 + self.core)
        self.across_both = (self.dp, (1 - self.y) * 2 + (1 - self.core))
        self.across_x = (self.z * 2 + (1 - self.x), self.mp)

    def along_z(self, step):
        return ((self.z + step) % self.depth * 2 + self.x, self.mp)

    def back_z(self, step):
        return (self.z + self.depth - step) % self.depth


def remote(src, dst, send_sem, recv_sem, device):
    return pltpu.make_async_remote_copy(
        src_ref=src,
        dst_ref=dst,
        send_sem=send_sem,
        recv_sem=recv_sem,
        device_id=device,
        device_id_type=MESH,
    )


def norm_tiles(count, tile, body):
    @pl.loop(0, count // tile)
    def _(i):
        body(pl.ds(pl.multiple_of(i * tile, tile), tile))


def row_marks(lengths_ref, local, first, share, region):
    rows, sents = lengths_ref.shape
    row_id = lax.broadcasted_iota(jnp.int32, local.shape, 0)
    places = local + first

    def per_row(values):
        out = jnp.full(local.shape, values[-1], jnp.int32)
        for r in range(rows - 1):
            out = jnp.where(row_id == r, values[r], out)
        return out

    def body(j, carry):
        passed, begun, ends = carry
        ends = tuple(ends[r] + lengths_ref[r, j] for r in range(rows))
        edge = per_row(ends)
        reached = places >= edge
        return (
            passed + reached.astype(jnp.int32),
            jnp.where(reached, edge, begun),
            ends,
        )

    zero = jnp.zeros(local.shape, jnp.int32)
    start = tuple(jnp.int32(0) for _ in range(rows))
    passed, begun, ends = lax.fori_loop(0, sents, body, (zero, zero, start))
    inside = places < per_row(ends)
    here = (local >= 0) & (local < region)
    segment = jnp.where(here, jnp.where(inside, passed, places + sents), -2)
    begins = (begun >= first) & (begun < first + share)
    owned = here & ((inside & begins) | (~inside & (local < share)))
    return (segment, owned)


def start_column(lengths_ref, row, first, slots):
    slot = lax.broadcasted_iota(jnp.int32, (slots, 1), 0)

    def body(j, carry):
        column, begin = carry
        column = jnp.where(slot == j, begin - first, column)
        return (column, begin + lengths_ref[row, j])

    column, _ = lax.fori_loop(
        0, lengths_ref.shape[1], body, (jnp.full((slots, 1), -1, jnp.int32), jnp.int32(0))
    )
    return column


def head_stack(values):
    lane = lax.broadcasted_iota(jnp.int32, values.shape, 1) // HDIM
    zero = jnp.zeros_like(values)
    return jnp.concatenate(
        [jnp.where(lane == h, values, zero) for h in range(values.shape[1] // HDIM)], axis=0
    )


def head_pick(stacked, width):
    heads = width // HDIM
    rows = stacked.shape[0] // heads
    lane = lax.broadcasted_iota(jnp.int32, (rows, width), 1) // HDIM
    out = stacked[:rows]
    for h in range(1, heads):
        out = jnp.where(lane == h, stacked[h * rows : (h + 1) * rows], out)
    return out


def nn(left, right):
    return jnp.dot(left, right, preferred_element_type=jnp.float32)


def nt(left, right):
    return lax.dot_general(
        left, right, (((1,), (1,)), ((), ())), preferred_element_type=jnp.float32
    )


def tn(left, right):
    return lax.dot_general(
        left, right, (((0,), (0,)), ((), ())), preferred_element_type=jnp.float32
    )


def shard_order(at):
    return [
        at.mp,
        at.y * 2 + (1 - at.core),
        (1 - at.y) * 2 + at.core,
        (1 - at.y) * 2 + (1 - at.core),
    ]


def forward_kernel(dp_size, gathers, *refs):
    (
        lengths_ref,
        tokens_hbm,
        wq_hbm,
        wo_hbm,
        wi_hbm,
        wb_hbm,
        bq_hbm,
        bi_hbm,
        masks_hbm,
        vectors,
        hidden_hbm,
        cls_ref,
        wq_out,
        wo_out,
        wi_out,
        wb_out,
        tok_out,
        q_out,
        k_out,
        v_out,
        p_out,
        o_out,
        h1_out,
        n1_out,
        r1_out,
        g_out,
        gp_out,
        n2_out,
        r2_out,
        own_out,
        masks_out,
        tok,
        wq,
        wo,
        wi,
        wb,
        bq,
        bi,
        q,
        k,
        v,
        probs,
        o,
        h1,
        n1,
        r1,
        g,
        gp,
        n2,
        r2,
        own,
        acc,
        upper,
        seg,
        key_seg,
        hid,
        hid_in,
        local_sem,
        halo_sem,
        bias_s,
        bias_r,
        core_s,
        core_r,
        y_s,
        y_r,
        x_s,
        x_r,
        yc_s,
        yc_r,
        xc_s,
        xc_r,
        out_sem,
        mask_s,
        mask_r,
    ) = refs
    at = Places(dp_size)
    rows, share, width = tokens_hbm.shape
    region = share + HALO
    total = rows * region
    m = at.mp
    b_out, gain1, shift1, b_back, gain2, shift2 = (vectors[i : i + 1] for i in range(6))
    first = m * share
    left = (at.dp, (m + 3) % 4)
    right = (at.dp, (m + 1) % 4)
    order = range(4)
    chunks = (
        [(wq, wq_hbm, (t,)) for t in range(3)]
        + [(wo, wo_hbm, ())]
        + [(wi, wi_hbm, (b,)) for b in range(4)]
        + [(wb, wb_hbm, (b,)) for b in range(4)]
    )
    whole = [(wq, wq_hbm), (wo, wo_hbm), (wi, wi_hbm), (wb, wb_hbm)]

    peers = [(at.dp, (m + j) % 4) for j in range(1, 4)] + [at.across_x]
    greet(peers + [at.along_z(step) for step in range(1, at.depth if gathers else 1)])

    loads = [
        pltpu.make_async_copy(tokens_hbm.at[r], tok.at[pl.ds(r * region, share)], local_sem.at[r])
        for r in range(rows)
    ]
    loads += [
        pltpu.make_async_copy(src, dst.at[0], local_sem.at[rows + i])
        for i, (dst, src) in enumerate(whole + [(bq, bq_hbm), (bi, bi_hbm)])
    ]
    for load in loads:
        load.start()
    halos = [
        remote(
            tokens_hbm.at[r, pl.ds(0, HALO)],
            tok.at[pl.ds(r * region + share, HALO)],
            halo_sem.at[0, r],
            halo_sem.at[1, r],
            left,
        )
        for r in range(rows)
    ]
    for copy in halos:
        copy.start()
    biases = []
    for j, device in enumerate((at.across_core, at.across_y, at.across_both), start=1):
        for i, (dst, src) in enumerate([(bq, bq_hbm), (bi, bi_hbm)]):
            biases.append(
                remote(src, dst.at[j], bias_s.at[j - 1, i], bias_r.at[j - 1, i], device)
            )
    for copy in biases:
        copy.start()

    def core_copy(i):
        dst, src = whole[i]
        return remote(src, dst.at[1], core_s.at[i], core_r.at[i], at.across_core)

    def y_copy(c):
        dst, src, index = chunks[c]
        place = (*index, at.x)
        return remote(src.at[place], dst.at[(2, *place)], y_s.at[c], y_r.at[c], at.across_y)

    def x_copy(c):
        ref = chunks[c][0].at[(2, *chunks[c][2], at.x)]
        return remote(ref, ref, x_s.at[c], x_r.at[c], at.across_x)

    def yc_copy(c):
        ref, _, index = chunks[c]
        place = (*index, at.x)
        return remote(
            ref.at[(2, *place)], ref.at[(3, *place)], yc_s.at[c], yc_r.at[c], at.across_core
        )

    def xc_copy(c):
        ref, _, index = chunks[c]
        place = (*index, 1 - at.x)
        return remote(
            ref.at[(2, *place)], ref.at[(3, *place)], xc_s.at[c], xc_r.at[c], at.across_core
        )

    mask_hops = []
    if gathers:
        mask_own = pltpu.make_async_copy(
            masks_hbm.at[at.core], masks_out.at[at.z, at.x, at.core], mask_s.at[0]
        )
        mask_own.start()
        mask_hops = [
            remote(
                masks_hbm.at[at.core],
                masks_out.at[at.z, at.x, at.core],
                mask_s.at[at.depth],
                mask_r.at[at.depth],
                at.across_x,
            )
        ]
        for step in range(1, at.depth):
            pair = masks_out.at[at.z, :, at.core]
            mask_hops.append(
                remote(pair, pair, mask_s.at[step], mask_r.at[step], at.along_z(step))
            )
        view = masks_out.at[:, :, at.core]
        index = at.depth + 1
        mask_hops.append(
            remote(view, view, mask_s.at[index], mask_r.at[index], at.across_core)
        )
        mask_hops[0].start()

    def pass_masks(stage):
        if not gathers:
            return
        come = [mask_hops[:1], mask_hops[1:-1], mask_hops[-1:]]
        if stage == 0:
            mask_own.wait()
        for hop in come[stage]:
            hop.wait_recv()
        if stage < 2:
            for hop in come[stage + 1]:
                hop.start()

    for c in range(12):
        y_copy(c).start()
    for i in range(4):
        core_copy(i).start()

    def step(c):
        if c < 12:
            y_copy(c).wait_recv()
            x_copy(c).start()
            yc_copy(c).start()
        if c > 0:
            x_copy(c - 1).wait_recv()
            xc_copy(c - 1).start()

    saves = []

    def save(src, dst):
        copy = pltpu.make_async_copy(src, dst, out_sem.at[len(saves)])
        copy.start()
        saves.append(copy)

    lane = lax.broadcasted_iota(jnp.int32, (8, 384), 1)
    segment, owned = row_marks(lengths_ref, lane, first, share, region)
    seg_cols = segment.astype(jnp.float32).T
    own_cols = owned.astype(jnp.float32).T
    for r in range(rows):
        seg[r] = jnp.broadcast_to(seg_cols[: seg.shape[1], r : r + 1], seg.shape[1:])
        own[pl.ds(r * region, region)] = own_cols[:region, r : r + 1]
    save(own, own_out)
    for r in range(rows):
        block = lax.broadcasted_iota(jnp.int32, (8, BLOCK + 2 * HALO), 0)
        offset = lax.broadcasted_iota(jnp.int32, (8, BLOCK + 2 * HALO), 1)
        keys, _ = row_marks(
            RowView(lengths_ref, r), block * BLOCK + offset - HALO, first, share, region
        )
        key_seg[r] = keys.astype(jnp.float32)
    blocks = q.shape[2] // BLOCK

    q[...] = jnp.zeros_like(q)
    k[...] = jnp.zeros_like(k)
    v[...] = jnp.zeros_like(v)

    for load in loads:
        load.wait()
    for copy in halos:
        copy.wait()
    for copy in biases:
        copy.wait_recv()
    save(tok, tok_out)

    def project(s):
        @pl.loop(0, rows)
        def _(r):
            x = tok[pl.ds(pl.multiple_of(r * region, 32), region)]
            for t, dst in enumerate((q, k, v)):
                y = nn(x, wq[s, t].reshape(width, -1))
                if t == 0:
                    y = (y + bq[s, 0:1]).astype(jnp.bfloat16) * jnp.bfloat16(0.125)
                elif t == 1:
                    y = y.astype(jnp.bfloat16)
                else:
                    y = (y + bq[s, 1:2]).astype(jnp.bfloat16)
                lead = 0 if t == 0 else HALO
                dst[s, r, lead : lead + region] = y

    def attend(s):
        heads = q.shape[3] // HDIM

        @pl.loop(0, rows)
        def _(r):
            for b in range(blocks):
                queries = head_stack(q[s, r, b * BLOCK : (b + 1) * BLOCK])
                window = slice(b * BLOCK, b * BLOCK + BLOCK + 2 * HALO)
                scores = nt(queries, k[s, r, window])
                allowed = seg[r, b * BLOCK : (b + 1) * BLOCK] == key_seg[r, b : b + 1]
                scores = jnp.where(jnp.concatenate([allowed] * heads, axis=0), scores, MASKED)
                peak = jnp.max(scores, axis=1, keepdims=True)
                raised = jnp.exp(scores - peak)
                weights = (raised / jnp.sum(raised, axis=1, keepdims=True)).astype(jnp.bfloat16)
                probs[s, r * blocks + b] = weights
                context = nn(weights, v[s, r, window])
                o[s, r, b * BLOCK : (b + 1) * BLOCK] = head_pick(context, heads * HDIM).astype(
                    jnp.bfloat16
                )

    def attention(i):
        s = order[i]
        project(s)
        attend(s)

    attention(0)
    step(0)
    core_copy(0).wait_recv()
    step(1)
    pass_masks(0)
    attention(1)
    step(2)
    step(3)
    attention(2)
    step(4)
    for c in range(3):
        yc_copy(c).wait_recv()
        xc_copy(c).wait_recv()
    attention(3)
    step(5)
    save(wq, wq_out)
    save(q, q_out)
    save(k, k_out)
    save(v, v_out)
    save(probs, p_out)
    save(o, o_out)

    core_copy(1).wait_recv()
    yc_copy(3).wait_recv()
    xc_copy(3).wait_recv()
    save(wo, wo_out)

    @pl.loop(0, rows)
    def _(r):
        y = nn(o[0, r, :region], wo[0].reshape(-1, width))
        for s in range(1, 4):
            y = y + nn(o[s, r, :region], wo[s].reshape(-1, width))
        acc[pl.ds(pl.multiple_of(r * region, 32), region)] = y


    def first_norm(part):
        values = tok[part].astype(jnp.float32) + acc[part] + b_out
        normed, unit, inv = norm_forward(values, gain1, shift1)
        n1[part] = unit
        r1[part] = inv
        h1[part] = normed.astype(jnp.bfloat16)
        acc[part] = normed + b_back

    norm_tiles(total, 96, first_norm)
    save(h1, h1_out)
    save(n1, n1_out)
    save(r1, r1_out)
    step(6)

    def raise_units(s):
        @pl.loop(0, 3)
        def _(n):
            columns = pl.ds(pl.multiple_of(n * 256, 256), 256)
            upper[...] = nn(h1[...], wi[s, :, :, :, columns].reshape(width, 256))

            def activate(part):
                u = upper[part] + bi[s, :, columns]
                cdf = 0.5 * (1.0 + lax.erf(u * 0.7071067811865476))
                g[s, part, columns] = (u * cdf).astype(jnp.bfloat16)
                slope = cdf + u * jnp.exp(-0.5 * u * u) * 0.3989422804014327
                gp[s, part, columns] = slope.astype(jnp.bfloat16)

            norm_tiles(total, 96, activate)

    def lower_units(s):
        @pl.loop(0, rows)
        def _(r):
            part = pl.ds(pl.multiple_of(r * region, 32), region)
            acc[part] = acc[part] + nn(g[s, part], wb[s].reshape(width, width))

    core_copy(2).wait_recv()
    raise_units(order[0])
    step(7)
    lower_units_early = [order[0], order[1]]
    core_copy(3).wait_recv()
    lower_units(lower_units_early[0])
    step(8)
    pass_masks(1)
    raise_units(order[1])
    step(9)
    lower_units(lower_units_early[1])
    for c in range(4, 8):
        yc_copy(c).wait_recv()
        xc_copy(c).wait_recv()
    save(wi, wi_out)
    raise_units(order[2])
    step(10)
    raise_units(order[3])
    save(g, g_out)
    save(gp, gp_out)
    step(11)
    step(12)
    lower_units(order[2])
    pass_masks(2)
    for c in range(8, 12):
        yc_copy(c).wait_recv()
        xc_copy(c).wait_recv()
    save(wb, wb_out)
    lower_units(order[3])

    def second_norm(part):
        normed, unit, inv = norm_forward(acc[part], gain2, shift2)
        n2[part] = unit
        r2[part] = inv
        hid[part] = normed.astype(jnp.bfloat16)

    norm_tiles(total, 96, second_norm)
    save(n2, n2_out)
    save(r2, r2_out)

    slots = cls_ref.shape[0] // rows
    for r in range(rows):
        place = lax.broadcasted_iota(jnp.int32, (slots, share), 1)
        pick = place == start_column(lengths_ref, r, first, slots)
        cls_ref[r * slots : (r + 1) * slots] = nn(
            pick.astype(jnp.bfloat16), hid[r * region : r * region + share]
        ).astype(jnp.bfloat16)

    def mask_hidden(part):
        hid[part] = (hid[part].astype(jnp.float32) * own[part]).astype(jnp.bfloat16)

    norm_tiles(total, 96, mask_hidden)
    settled = [
        remote(
            hid.at[pl.ds(r * region + share, HALO)],
            hid_in.at[r],
            halo_sem.at[2, r],
            halo_sem.at[3, r],
            right,
        )
        for r in range(rows)
    ]
    for copy in settled:
        copy.start()
    for copy in settled:
        copy.wait()
    for r in range(rows):
        head = pl.ds(r * region, HALO)
        hid[head] = hid[head] + hid_in[r]
    for r in range(rows):
        save(hid.at[pl.ds(r * region, share)], hidden_hbm.at[r])

    for copy in saves:
        copy.wait()
    for copy in biases + mask_hops:
        copy.wait_send()
    for i in range(4):
        core_copy(i).wait_send()
    for c in range(12):
        y_copy(c).wait_send()
        x_copy(c).wait_send()
        yc_copy(c).wait_send()
        xc_copy(c).wait_send()


class RowView:
    def __init__(self, ref, row):
        self.ref, self.row = ref, row
        self.shape = (1, ref.shape[1])

    def __getitem__(self, index):
        return self.ref[self.row, index[1]]


def forward(tokens, lengths, w_qkv, b_qv, w_out, w_in, b_in, w_back, vectors, masks, dp_size, gathers):
    rows, share, width = tokens.shape
    region = share + HALO
    total = rows * region
    blocks = -(-region // BLOCK)
    padded = blocks * BLOCK
    keyed = padded + 2 * HALO
    low, full = jnp.bfloat16, jnp.float32
    head_cols = w_qkv.shape[2]
    slots = 32
    shape = jax.ShapeDtypeStruct
    saved = [
        ((4, 3, 2, width // 2, head_cols), low),
        ((4, 2, head_cols // 2, width), low),
        ((4, 4, 2, width // 8, width), low),
        ((4, 4, 2, width // 8, width), low),
        ((total, width), low),
        ((4, rows, padded, head_cols), low),
        ((4, rows, keyed, head_cols), low),
        ((4, rows, keyed, head_cols), low),
        ((4, rows * blocks, head_cols // HDIM * BLOCK, BLOCK + 2 * HALO), low),
        ((4, rows, padded, head_cols), low),
        ((total, width), low),
        ((total, width), full),
        ((total, 1), full),
        ((4, total, width), low),
        ((4, total, width), low),
        ((total, width), full),
        ((total, 1), full),
        ((total, 1), full),
    ]
    out_shape = [shape((rows, share, width), low), shape((rows * slots, width), low)]
    out_shape += [shape(*item) for item in saved]
    out_shape += [shape((dp_size // 2, 2, *masks.shape) if gathers else (8, 128), low)]
    held = [pltpu.VMEM(*item) for item in saved]
    dma = pltpu.SemaphoreType.DMA
    scratch = [held[4]] + held[:4]
    scratch += [pltpu.VMEM((4, 2, head_cols), full), pltpu.VMEM((4, 1, width), full)]
    scratch += held[5:]
    scratch += [
        pltpu.VMEM((total, width), full),
        pltpu.VMEM((total, 256), full),
        pltpu.VMEM((rows, padded, BLOCK + 2 * HALO), full),
        pltpu.VMEM((rows, 8, BLOCK + 2 * HALO), full),
        pltpu.VMEM((total, width), low),
        pltpu.VMEM((rows, HALO, width), low),
        dma((rows + 6,)),
        dma((4, rows)),
        dma((3, 2)),
        dma((3, 2)),
        dma((4,)),
        dma((4,)),
        *[dma((12,))] * 8,
        dma((24,)),
        dma((dp_size // 2 + 2,)),
        dma((dp_size // 2 + 2,)),
    ]
    anywhere = pl.BlockSpec(memory_space=pl.ANY)
    vmem = pl.BlockSpec(memory_space=pltpu.VMEM)
    row = lambda vector: vector.reshape(1, -1)
    return pl.pallas_call(
        lambda *refs: forward_kernel(dp_size, gathers, *refs),
        out_shape=out_shape,
        in_specs=[pl.BlockSpec(memory_space=pltpu.SMEM)] + [anywhere] * 8 + [vmem],
        out_specs=[anywhere, vmem] + [anywhere] * (len(saved) + 1),
        scratch_shapes=scratch,
        compiler_params=pltpu.CompilerParams(
            collective_id=2, has_side_effects=True, vmem_limit_bytes=64 * 1024 * 1024 - 65536
        ),
        name="forward",
    )(
        lengths,
        tokens,
        w_qkv.reshape(3, 2, width // 2, head_cols),
        w_out.reshape(2, head_cols // 2, width),
        w_in.reshape(4, 2, width // 8, width),
        w_back.reshape(4, 2, width // 8, width),
        b_qv,
        row(b_in),
        masks,
        vectors,
    )


class Reducer:
    def __init__(self, at, bufs):
        self.at = at
        self.pieces = pieces_of(at.depth)
        self.plane = self.pieces == at.depth
        self.ready = 0
        (
            self.parts,
            self.core_in,
            self.y_in,
            self.x_in,
            self.z_in,
            self.whole,
            self.done,
            self.core_s,
            self.core_r,
            self.y_s,
            self.y_r,
            self.x_s,
            self.x_r,
            self.z_s,
            self.z_r,
            self.za_s,
            self.za_r,
            self.xa_s,
            self.xa_r,
            self.own_s,
            self.out_s,
        ) = bufs

    def core_copy(self, u):
        at = self.at
        return remote(
            self.parts.at[1, :, u],
            self.core_in.at[:, u],
            self.core_s.at[u],
            self.core_r.at[u],
            at.across_core,
        )

    def y_copy(self, u):
        at = self.at
        return remote(
            self.parts.at[0, 1, u],
            self.y_in.at[u],
            self.y_s.at[u],
            self.y_r.at[u],
            at.across_y,
        )

    def x_copy(self, u):
        return remote(
            self.parts.at[0, 0, u, 1],
            self.x_in.at[u],
            self.x_s.at[u],
            self.x_r.at[u],
            self.at.across_x,
        )

    def z_copy(self, u, step):
        at = self.at
        return remote(
            self.parts.at[0, 0, u, 0, (at.z + step) % at.depth],
            self.z_in.at[u, step - 1],
            self.z_s.at[u, step - 1],
            self.z_r.at[u, step - 1],
            at.along_z(step),
        )

    def za_copy(self, u, step):
        at = self.at
        return remote(
            self.done.at[u],
            self.whole.at[u, 0, at.z],
            self.za_s.at[u, step - 1],
            self.za_r.at[u, step - 1],
            at.along_z(step),
        )

    def own_copy(self, u):
        return pltpu.make_async_copy(
            self.done.at[u], self.whole.at[u, 0, self.at.z], self.own_s.at[u]
        )

    def xa_copy(self, u):
        return remote(
            self.whole.at[u, 0],
            self.whole.at[u, 1],
            self.xa_s.at[u],
            self.xa_r.at[u],
            self.at.across_x,
        )

    def out_copies(self, u, out):
        held = self.whole.at[u] if self.plane else self.parts.at[0, 0, u]
        return [
            pltpu.make_async_copy(
                held.at[half],
                out.at[u, :, :, pl.ds(pl.multiple_of(side * 384, 128), 384)],
                self.out_s.at[u, half],
            )
            for half, side in ((0, self.at.x), (1, 1 - self.at.x))
        ]

    def add(self, place, source, at):
        @pl.loop(0, self.pieces)
        def _(p):
            mine = self.parts[(*place, p)].astype(jnp.float32)
            both = mine + source[(*at, p)].astype(jnp.float32)
            self.parts[(*place, p)] = both.astype(jnp.bfloat16)

    def start(self, u):
        self.core_copy(u).start()

    def add_far(self, u):
        self.core_copy(u).wait_recv()
        for half in range(2):
            self.add((0, 1, u, half), self.core_in, (1, u, half))
        self.y_copy(u).start()

    def add_near(self, u):
        for half in range(2):
            self.add((0, 0, u, half), self.core_in, (0, u, half))

    def add_y(self, u):
        self.y_copy(u).wait_recv()
        self.add((0, 0, u, 1), self.y_in, (u, 1))
        if self.plane:
            self.x_copy(u).start()
        self.add((0, 0, u, 0), self.y_in, (u, 0))

    def add_x(self, u):
        self.x_copy(u).wait_recv()
        self.add((0, 0, u, 0), self.x_in, (u,))
        for step in range(1, self.at.depth):
            self.z_copy(u, step).start()

    def add_z(self, u):
        at = self.at
        total = self.parts[0, 0, u, 0, at.z].astype(jnp.float32)
        for step in range(1, at.depth):
            self.z_copy(u, step).wait_recv()
            total = total + self.z_in[u, step - 1].astype(jnp.float32)
        self.done[u] = total.astype(jnp.bfloat16)
        for step in range(1, at.depth):
            self.za_copy(u, step).start()
        self.own_copy(u).start()

    def spread_x(self, u):
        self.own_copy(u).wait()
        for step in range(1, self.at.depth):
            self.za_copy(u, step).wait_recv()
        self.xa_copy(u).start()

    def finish(self, u, out):
        if self.plane:
            self.xa_copy(u).wait_recv()
        for copy in self.out_copies(u, out):
            copy.start()

    def drain(self, u, out):
        self.core_copy(u).wait_send()
        self.y_copy(u).wait_send()
        for copy in self.out_copies(u, out):
            copy.wait()
        if not self.plane:
            return
        self.x_copy(u).wait_send()
        self.xa_copy(u).wait_send()
        for step in range(1, self.at.depth):
            self.z_copy(u, step).wait_send()
            self.za_copy(u, step).wait_send()


def pieces_of(depth):
    return depth if UNIT % (16 * depth) == 0 else 4


def reducer_scratch(depth):
    lanes = max(depth - 1, 1)
    depth = pieces_of(depth)
    rows = UNIT // depth
    dma = pltpu.SemaphoreType.DMA
    low = jnp.bfloat16
    return [
        pltpu.VMEM((2, 2, UNITS, 2, depth, rows, 384), low),
        pltpu.VMEM((2, UNITS, 2, depth, rows, 384), low),
        pltpu.VMEM((UNITS, 2, depth, rows, 384), low),
        pltpu.VMEM((UNITS, depth, rows, 384), low),
        pltpu.VMEM((UNITS, lanes if depth == lanes + 1 else 1, rows, 384), low),
        pltpu.VMEM((UNITS, 2, depth, rows, 384), low),
        pltpu.VMEM((UNITS, rows, 384), low),
        *[dma((UNITS,))] * 6,
        *[dma((UNITS, lanes if depth == lanes + 1 else 1))] * 4,
        *[dma((UNITS,))] * 3,
        dma((UNITS, 2)),
    ]


class Ring:
    def __init__(self, slots, sem, sources):
        self.slots, self.sem, self.sources = slots, sem, sources
        self.count = len(slots)
        self.used = 0
        for i in range(min(self.count, len(sources))):
            self.copy(i).start()

    def copy(self, i):
        return pltpu.make_async_copy(
            self.sources[i], self.slots[i % self.count], self.sem.at[i]
        )

    def take(self):
        self.copy(self.used).wait()
        return self.slots[self.used % self.count]

    def free(self):
        ahead = self.used + self.count
        if ahead < len(self.sources):
            self.copy(ahead).start()
        self.used += 1


def backward_kernel(dp_size, *refs):
    (
        lengths_ref,
        cls_grad,
        vectors,
        cot_hbm,
        wq_hbm,
        wo_hbm,
        wi_hbm,
        wb_hbm,
        tok_hbm,
        q_hbm,
        k_hbm,
        v_hbm,
        p_hbm,
        o_hbm,
        h1_hbm,
        n1_hbm,
        r1_hbm,
        g_hbm,
        gp_hbm,
        n2_hbm,
        r2_hbm,
        own_hbm,
        sums_hbm,
        grad_hbm,
        vec_out,
        own,
        cot,
        unit,
        inv1,
        inv2,
        acc,
        df,
        turned,
        h1,
        tok,
        q,
        k,
        v,
        probs,
        o,
        wo,
        w0,
        w1,
        w2,
        wq0,
        wq1,
        g0,
        g1,
        gp0,
        gp1,
        du,
        do,
        dq_pad,
        dkv,
        dqkv,
        vec,
        vec_in,
        vec_z,
        halo_in,
        load_sem,
        g_sem,
        w_sem,
        gp_sem,
        wq_sem,
        halo_sem,
        vec_s,
        vec_r,
        *bufs,
    ) = refs
    at = Places(dp_size)
    red = Reducer(at, bufs)
    rows, share, width = cot_hbm.shape
    region = share + HALO
    total = rows * region
    m = at.mp
    first = m * share
    left = (at.dp, (m + 3) % 4)
    right = (at.dp, (m + 1) % 4)
    gain1, gain2 = vectors[1:2], vectors[4:5]
    order = (1, 3, 2, 0)
    true_shard = shard_order(at)

    def loading(i, src, dst):
        return pltpu.make_async_copy(src, dst, load_sem.at[i])

    cots = [
        loading(r, cot_hbm.at[r], cot.at[pl.ds(r * region, share)]) for r in range(rows)
    ]
    early = cots + [
        loading(rows + i, src, dst)
        for i, (src, dst) in enumerate(
            [(own_hbm, own), (n2_hbm, unit), (r2_hbm, inv2), (r1_hbm, inv1)]
        )
    ]
    for copy in early:
        copy.start()
    g_ring = Ring((g0, g1), g_sem, [g_hbm.at[s] for s in order])
    w_sources = [ref.at[s] for s in order for ref in (wb_hbm, wi_hbm)]
    w_ring = Ring((w0, w1, w2), w_sem, w_sources)
    gp_ring = Ring((gp0, gp1), gp_sem, [gp_hbm.at[s] for s in order])
    late = [
        loading(rows + 4 + i, src, dst)
        for i, (src, dst) in enumerate(
            [
                (h1_hbm, h1),
                (tok_hbm, tok),
                (o_hbm, o),
                (wo_hbm, wo),
                (q_hbm, q),
                (k_hbm, k),
                (v_hbm, v),
                (p_hbm, probs),
            ]
        )
    ]
    for copy in late:
        copy.start()
    wq_ring = Ring((wq0, wq1), wq_sem, [wq_hbm.at[s] for s in order])

    peers = [(at.dp, (m + j) % 4) for j in range(1, 4)] + [at.across_x]
    greet(peers + [at.along_z(step) for step in range(1, at.depth)])
    halos = [
        remote(
            cot_hbm.at[r, pl.ds(0, HALO)],
            cot.at[pl.ds(r * region + share, HALO)],
            halo_sem.at[0, r],
            halo_sem.at[1, r],
            left,
        )
        for r in range(rows)
    ]
    for copy in halos:
        copy.start()

    expected = []
    for u in range(UNITS):
        arrives = 13.5 + 6.3 * (u + 1)
        expected.append((arrives, u, red.add_y))
        if red.plane:
            expected.append((arrives + 5.0, u, red.add_x))
            expected.append((arrives + 11.0, u, red.add_z))
            expected.append((arrives + 17.0, u, red.spread_x))
        expected.append((arrives + 22.0, u, lambda u: red.finish(u, sums_hbm)))
    expected.sort(key=lambda event: event[0])

    def pump(until):
        while expected and expected[0][0] <= until and expected[0][1] < red.ready:
            _, u, event = expected.pop(0)
            event(u)

    vec[0] = jnp.zeros(vec.shape[1:], jnp.float32)
    slots = cls_grad.shape[0] // rows
    for copy in early:
        copy.wait()
    for copy in halos:
        copy.wait()

    def norm_back(part, grad, gain, inv, base):
        normed, inv_dev = unit[part], inv[part]
        scaled = grad * gain
        centered = scaled - jnp.mean(scaled, axis=-1, keepdims=True)
        inner = jnp.mean(scaled * normed, axis=-1, keepdims=True)
        grad_in = inv_dev * (centered - normed * inner)
        acc[part] = grad_in
        df[part] = grad_in.astype(jnp.bfloat16)
        vec[0, base : base + 1] += jnp.sum(grad_in, axis=0, keepdims=True)
        vec[0, base + 1 : base + 2] += jnp.sum(grad * normed, axis=0, keepdims=True)
        vec[0, base + 2 : base + 3] += jnp.sum(grad, axis=0, keepdims=True)

    tile = 96
    for r in range(rows):
        starts = start_row(lengths_ref, r, first, slots)
        come = cls_grad[r * slots : (r + 1) * slots]
        terms = []
        for _ in range(3):
            term = come.astype(jnp.bfloat16)
            terms.append(term)
            come = come - term.astype(jnp.float32)

        @pl.loop(0, region // tile)
        def _(i):
            part = pl.ds(pl.multiple_of(r * region + i * tile, 32), tile)
            place = i * tile + lax.broadcasted_iota(jnp.int32, (tile, slots), 0)
            hit = (place == starts) & (place < share)
            pick = jnp.where(hit, 1.0, 0.0).astype(jnp.bfloat16)
            grad = cot[part].astype(jnp.float32)
            for term in terms:
                grad = grad + nn(pick, term)
            norm_back(part, grad * own[part], gain2, inv2, 3)

    first_unit = pltpu.make_async_copy(n1_hbm, unit, load_sem.at[1])
    first_unit.start()

    def put(s, u, half, values):
        low = values.astype(jnp.bfloat16)
        for i in range(values.shape[0] // UNIT):
            red.parts[s % 2, s // 2, u + i, half] = low[i * UNIT : (i + 1) * UNIT].reshape(
                red.pieces, UNIT // red.pieces, 384
            )

    def true_half(half):
        return (at.x + half) % 2

    def true_columns(half):
        return pl.ds(pl.multiple_of(true_half(half) * 384, 128), 384)

    def sent(i, units):
        if i == 1:
            for u in units:
                red.start(u)
        if i == 2:
            for u in units:
                red.add_far(u)
        if i == 3:
            for u in units:
                red.add_near(u)
            red.ready = units[-1] + 1

    for i in range(4):
        g = g_ring.take()
        turned[...] = g[...].T
        g_ring.free()

        for half in range(2):
            put(order[i], 0, half, nn(turned[...], df[:, true_columns(half)]))

        sent(i, range(4))
    late[0].wait()
    turned[...] = h1[...].T
    for i in range(4):
        s = order[i]
        wb = w_ring.take()
        slope = gp_ring.take()

        for half in range(2):
            columns = true_columns(half)
            rows_here = pl.ds(2 * true_half(half), 2)
            rise = nt(df[...], wb[rows_here].reshape(384, width))
            rise = (rise * slope[:, columns].astype(jnp.float32)).astype(jnp.bfloat16)
            du[:, columns] = rise
            vec[0, pl.ds(6 + true_shard[s], 1), columns] = jnp.sum(
                rise.astype(jnp.float32), axis=0, keepdims=True
            )
            put(s, 4, half, nn(turned[...], rise))

        w_ring.free()
        gp_ring.free()
        pump(16.5 + 7.5 * i)
        wi = w_ring.take()
        sent(i, range(4, 8))

        @pl.loop(0, rows)
        def _(r):
            part = pl.ds(pl.multiple_of(r * region, 32), region)
            acc[part] = acc[part] + nt(du[part], wi[...].reshape(width, width))

        w_ring.free()
        pump(20.0 + 7.5 * i)

    first_unit.wait()

    @pl.loop(0, total // tile)
    def _(i):
        part = pl.ds(pl.multiple_of(i * tile, tile), tile)
        norm_back(part, acc[part], gain1, inv1, 0)

    for copy in late[1:]:
        copy.wait()
    pump(46.0)

    heads = q.shape[3] // HDIM
    cols = heads * HDIM
    blocks = q.shape[2] // BLOCK
    for i in range(4):
        s = order[i]
        flat = jnp.concatenate([o[s, r, :region] for r in range(rows)], axis=0)
        for half in range(2):
            put(s, 8, half, tn(flat, df[:, true_columns(half)]))
        sent(i, [8])
    pump(50.0)
    do[...] = jnp.zeros_like(do)
    for i in range(4):
        s = order[i]
        back = nt(df[...], wo[s].reshape(cols, width)).astype(jnp.bfloat16)
        for r in range(rows):
            do[r, :region] = back[r * region : (r + 1) * region]
        dkv[...] = jnp.zeros_like(dkv)
        @pl.loop(0, blocks)
        def _(b):
            here = pl.ds(pl.multiple_of(b * BLOCK, BLOCK), BLOCK)
            window = pl.ds(pl.multiple_of(b * BLOCK, BLOCK), BLOCK + 2 * HALO)
            for r in range(rows):
                grads = head_stack(do[r, here])
                queries = head_stack(q[s, r, here])
                weight = probs[s, r * blocks + b]
                wide = weight.astype(jnp.float32)
                rise = nt(grads, v[s, r, window])
                inner = jnp.sum(wide * rise, axis=1, keepdims=True)
                fall = (wide * (rise - inner)).astype(jnp.bfloat16)
                dq = head_pick(nn(fall, k[s, r, window]), cols) * 0.125
                dq_pad[r, here] = dq.astype(jnp.bfloat16)
                dkv[0, r, window] += tn(fall, queries)
                dkv[1, r, window] += tn(weight, grads)

        for r in range(rows):
            dqkv[0, r * region : (r + 1) * region] = dq_pad[r, :region]
            for t in range(2):
                dqkv[1 + t, r * region : (r + 1) * region] = dkv[
                    t, r, HALO : HALO + region
                ].astype(jnp.bfloat16)
        pump(54.5 + 10.0 * i)
        wqs = wq_ring.take()
        for t, lane in ((0, 0), (1, None), (2, 256)):
            part = dqkv[t]
            if lane is not None:
                vec[0, pl.ds(10 + true_shard[s], 1), lane : lane + cols] = jnp.sum(
                    part.astype(jnp.float32), axis=0, keepdims=True
                )
            for half in range(2):
                put(s, 9 + t, half, tn(part, tok[:, true_columns(half)]))

            @pl.loop(0, rows)
            def _(r, t=t):
                here = pl.ds(pl.multiple_of(r * region, 32), region)
                acc[here] = acc[here] + nt(dqkv[t, here], wqs[t].reshape(width, cols))

        wq_ring.free()
        sent(i, range(9, 12))
        pump(59.0 + 10.0 * i)

    def mask_grad(part):
        acc[part] = acc[part] * own[part]

    norm_tiles(total, tile, mask_grad)
    settled = [
        remote(
            acc.at[pl.ds(r * region + share, HALO)],
            halo_in.at[r],
            halo_sem.at[2, r],
            halo_sem.at[3, r],
            right,
        )
        for r in range(rows)
    ]
    for copy in settled:
        copy.start()

    def vec_copy(i):
        device = (at.across_core, at.across_y, at.across_x)[i]
        return remote(vec.at[i], vec_in.at[i], vec_s.at[i], vec_r.at[i], device)

    def vec_z_copy(step):
        index = 2 + step
        return remote(
            vec.at[3], vec_z.at[step], vec_s.at[index], vec_r.at[index], at.along_z(step)
        )

    vec_copy(0).start()
    pump(94.0)
    grads = []
    for copy in settled:
        copy.wait()
    for r in range(rows):
        head = pl.ds(r * region, HALO)
        acc[head] = acc[head] + halo_in[r]
    for r in range(rows):
        copy = loading(r, acc.at[pl.ds(r * region, share)], grad_hbm.at[r])
        copy.start()
        grads.append(copy)
    for i in range(3):
        vec_copy(i).wait_recv()
        both = vec[i] + vec_in[i]
        if i < 2:
            vec[i + 1] = both
            vec_copy(i + 1).start()
        else:
            vec[3] = both
            vec_z[0] = both
            for step in range(1, at.depth):
                vec_z_copy(step).start()
        pump(97.0 + 4.0 * i)
    for step in range(1, at.depth):
        vec_z_copy(step).wait_recv()
    both = vec_z[at.back_z(0)]
    for z in range(1, at.depth):
        both = both + vec_z[at.back_z(z)]
    vec_out[...] = both
    pump(1000.0)
    for copy in grads:
        copy.wait()
    for i in range(3):
        vec_copy(i).wait_send()
    for step in range(1, at.depth):
        vec_z_copy(step).wait_send()

    @pl.loop(0, UNITS)
    def _(u):
        red.drain(u, sums_hbm)


def start_row(lengths_ref, row, first, slots):
    slot = lax.broadcasted_iota(jnp.int32, (1, slots), 1)

    def body(j, carry):
        line, begin = carry
        return (jnp.where(slot == j, begin - first, line), begin + lengths_ref[row, j])

    line, _ = lax.fori_loop(
        0, lengths_ref.shape[1], body, (jnp.full((1, slots), -1, jnp.int32), jnp.int32(0))
    )
    return line


def backward(lengths, cls_grad, vectors, cotangent, saved, dp_size):
    rows, share, width = cotangent.shape
    region = share + HALO
    total = rows * region
    q, k, probs, o = saved[5], saved[6], saved[8], saved[9]
    depth = dp_size // 2
    low, full = jnp.bfloat16, jnp.float32
    cols = q.shape[3]
    dma = pltpu.SemaphoreType.DMA
    vmem = pltpu.VMEM
    scratch = [
        vmem((total, 1), full),
        vmem((total, width), low),
        vmem((total, width), full),
        vmem((total, 1), full),
        vmem((total, 1), full),
        vmem((total, width), full),
        vmem((total, width), low),
        vmem((width, total), low),
        vmem((total, width), low),
        vmem((total, width), low),
        vmem(q.shape, low),
        vmem(k.shape, low),
        vmem(k.shape, low),
        vmem(probs.shape, low),
        vmem(o.shape, low),
        vmem(saved[1].shape, low),
        *[vmem(saved[2].shape[1:], low)] * 3,
        *[vmem(saved[0].shape[1:], low)] * 2,
        *[vmem((total, width), low)] * 4,
        vmem((total, width), low),
        vmem(q.shape[1:], low),
        vmem(q.shape[1:], low),
        vmem((2, *k.shape[1:]), full),
        vmem((3, total, cols), low),
        vmem((4, 16, width), full),
        vmem((3, 16, width), full),
        vmem((depth, 16, width), full),
        vmem((rows, HALO, width), full),
        dma((rows + 12,)),
        *[dma((8,))] * 4,
        dma((4, rows)),
        dma((2 + depth,)),
        dma((2 + depth,)),
    ] + reducer_scratch(depth)
    anywhere = pl.BlockSpec(memory_space=pl.ANY)
    in_vmem = pl.BlockSpec(memory_space=pltpu.VMEM)
    shape = jax.ShapeDtypeStruct
    return pl.pallas_call(
        lambda *refs: backward_kernel(dp_size, *refs),
        out_shape=[
            shape((UNITS, pieces_of(depth), UNIT // pieces_of(depth), width), low),
            shape((rows, share, width), full),
            shape((16, width), full),
        ],
        in_specs=[pl.BlockSpec(memory_space=pltpu.SMEM)] + [in_vmem] * 2 + [anywhere] * 19,
        out_specs=[anywhere, anywhere, in_vmem],
        scratch_shapes=scratch,
        compiler_params=pltpu.CompilerParams(
            collective_id=1, has_side_effects=True, vmem_limit_bytes=64 * 1024 * 1024 - 65536
        ),
        name="backward",
    )(lengths, cls_grad, vectors, cotangent, *saved)


def contrast_kernel(dp_size, sents, *refs):
    (
        cls_ref,
        vectors,
        w_hbm,
        masks_hbm,
        loss_ref,
        w_grad,
        b_grad,
        cls_grad,
        w_pool,
        masks,
        rows_in,
        mine,
        every,
        views,
        pooled,
        units,
        inverse,
        logit_grad,
        lowered,
        load_sem,
        rs_s,
        rs_r,
        own_sem,
        z_s,
        z_r,
        hop_s,
        hop_r,
    ) = refs
    at = Places(dp_size)
    width = w_pool.shape[0]
    slots = views.shape[1]
    group = slots // dp_size
    share = group // 4
    loads = [
        pltpu.make_async_copy(w_hbm, w_pool, load_sem.at[0]),
        pltpu.make_async_copy(masks_hbm, masks, load_sem.at[1]),
    ]
    for load in loads:
        load.start()
    others = [(at.dp, (at.mp + j) % 4) for j in range(1, 4)]
    greet(others + [at.across_x] + [at.along_z(step) for step in range(1, at.depth)])

    quarters = [
        remote(
            cls_ref.at[(at.mp + j) % 4],
            rows_in.at[j - 1],
            rs_s.at[j - 1],
            rs_r.at[j - 1],
            others[j - 1],
        )
        for j in range(1, 4)
    ]
    for copy in quarters:
        copy.start()
    total = cls_ref[at.mp].astype(jnp.float32)
    for j, copy in enumerate(quarters):
        copy.wait_recv()
        total = total + rows_in[j].astype(jnp.float32)
    mine[...] = total.astype(jnp.bfloat16)

    place = every.at[at.z, at.x, at.y, at.core]
    own = pltpu.make_async_copy(mine, place, own_sem)
    own.start()
    along = [
        remote(mine, place, z_s.at[step - 1], z_r.at[step - 1], at.along_z(step))
        for step in range(1, at.depth)
    ]
    for copy in along:
        copy.start()
    own.wait()
    for copy in along:
        copy.wait_recv()
    hops = []
    for i, (part, device) in enumerate(
        [
            (every.at[:, at.x, at.y, at.core], at.across_x),
            (every.at[:, :, at.y, at.core], at.across_y),
            (every.at[:, :, :, at.core], at.across_core),
        ]
    ):
        hop = remote(part, part, hop_s.at[i], hop_r.at[i], device)
        hop.start()
        hop.wait_recv()
        hops.append(hop)
    for load in loads:
        load.wait()

    per_z = slots // at.depth
    for t in range(2):
        for z in range(at.depth):
            part = slice(z * per_z, (z + 1) * per_z)
            cls_rows = every[z].reshape(per_z, width).astype(jnp.float32)
            keep = masks[z, :, t].reshape(per_z, width).astype(jnp.float32)
            view = (cls_rows * keep * KEEP_SCALE).astype(jnp.bfloat16)
            views[t, part] = view
            unit = jnp.tanh(nn(view, w_pool[...]) + vectors[6:7])
            pooled[t, part] = unit
            inv = lax.rsqrt(jnp.sum(unit * unit, axis=-1, keepdims=True) + 1e-06)
            inverse[t, part] = inv
            units[t, part] = (unit * inv).astype(jnp.bfloat16)

    def real(index):
        return index % 32 < sents

    loss = jnp.zeros((1, 1), jnp.float32)
    for z in range(at.depth):
        part = slice(z * per_z, (z + 1) * per_z)
        logits = nt(units[0, part], units[1]) * 20.0
        line = z * per_z + lax.broadcasted_iota(jnp.int32, logits.shape, 0)
        column = lax.broadcasted_iota(jnp.int32, logits.shape, 1)
        logits = jnp.where(real(column), logits, MASKED)
        peak = jnp.max(logits, axis=1, keepdims=True)
        raised = jnp.exp(logits - peak)
        row_total = jnp.sum(raised, axis=1, keepdims=True)
        partner = line == column
        chosen = jnp.sum(jnp.where(partner, logits, 0.0), axis=1, keepdims=True)
        row_loss = peak + jnp.log(row_total) - chosen
        row_loss = jnp.where(real(line[:, :1]), row_loss, 0.0)
        loss = loss + jnp.sum(row_loss, axis=0, keepdims=True)
        grad = raised / row_total - jnp.where(partner, 1.0, 0.0)
        logit_grad[part] = jnp.where(real(line), grad, 0.0).astype(jnp.bfloat16)
    count = slots // 32 * sents
    loss_ref[...] = jnp.broadcast_to(loss / count, loss_ref.shape)

    bias = jnp.zeros((1, width), jnp.float32)
    for t in range(2):
        for z in range(at.depth):
            part = slice(z * per_z, (z + 1) * per_z)
            if t == 0:
                unit_grad = nn(logit_grad[part], units[1]) * 20.0
            else:
                unit_grad = tn(logit_grad[:, part], units[0]) * 20.0
            before = pooled[t, part]
            inv = inverse[t, part]
            unit = before * inv
            inner = jnp.sum(unit_grad * unit, axis=-1, keepdims=True)
            grad = inv * (unit_grad - unit * inner) * (1.0 - before * before)
            low = grad.astype(jnp.bfloat16)
            lowered[t, part] = low
            bias = bias + jnp.sum(low.astype(jnp.float32), axis=0, keepdims=True)
    b_grad[...] = bias

    here = pl.ds(pl.multiple_of(at.dp * group, group), group)
    back = jnp.zeros((group, width), jnp.float32)
    for t in range(2):
        keep = masks[at.z, at.x, t].astype(jnp.float32)
        back = back + nt(lowered[t, here], w_pool[...]) * keep
    cls_grad[...] = back * KEEP_SCALE
    for half in range(2):
        columns = slice(half * width // 2, (half + 1) * width // 2)
        w_grad[:, columns] = tn(views[0], lowered[0, :, columns]) + tn(
            views[1], lowered[1, :, columns]
        )
    for copy in quarters + along + hops:
        copy.wait_send()


def contrast_whole(cls_part, masks, w_pool, vectors, dp_size, sents):
    group, width = cls_part.shape
    slots = group * dp_size
    depth = dp_size // 2
    share = group // 4
    low, full = jnp.bfloat16, jnp.float32
    dma = pltpu.SemaphoreType.DMA
    vmem = pltpu.VMEM
    anywhere = pl.BlockSpec(memory_space=pl.ANY)
    in_vmem = pl.BlockSpec(memory_space=pltpu.VMEM)
    shape = jax.ShapeDtypeStruct
    return pl.pallas_call(
        lambda *refs: contrast_kernel(dp_size, sents, *refs),
        out_shape=[
            shape((8, 128), full),
            shape((width, width), full),
            shape((1, width), full),
            shape((group, width), full),
        ],
        in_specs=[in_vmem, in_vmem, anywhere, anywhere],
        out_specs=[in_vmem] * 4,
        scratch_shapes=[
            vmem((width, width), low),
            vmem(masks.shape, low),
            vmem((3, share, width), low),
            vmem((share, width), low),
            vmem((depth, 2, 2, 2, share, width), low),
            vmem((2, slots, width), low),
            vmem((2, slots, width), full),
            vmem((2, slots, width), low),
            vmem((2, slots, 1), full),
            vmem((slots, slots), low),
            vmem((2, slots, width), low),
            dma((2,)),
            dma((3,)),
            dma((3,)),
            dma,
            dma((max(depth - 1, 1),)),
            dma((max(depth - 1, 1),)),
            dma((3,)),
            dma((3,)),
        ],
        compiler_params=pltpu.CompilerParams(
            collective_id=3, has_side_effects=True, vmem_limit_bytes=60 * 1024 * 1024
        ),
        name="contrast",
    )(cls_part.reshape(4, share, width), vectors, w_pool, masks)


def shards(
    tokens,
    lengths,
    view_masks,
    w_qkv,
    b_qv,
    w_out,
    b_out,
    ln1_gain,
    ln1_bias,
    w_in,
    b_in,
    w_back,
    b_back,
    ln2_gain,
    ln2_bias,
    w_pool,
    b_pool,
    cotangent,
):
    rows, share, width = tokens.shape
    ranks = lax.axis_size("dp")
    sents = lengths.shape[1]
    gathers = ranks * rows * 32 <= 1024
    masks = jnp.pad(view_masks, [(0, 0), (0, 32 - sents), (0, 0), (0, 0)]).astype(jnp.bfloat16)
    masks = masks.transpose(2, 0, 1, 3).reshape(2, rows * 32, width)
    vectors = jnp.stack(
        [b_out, ln1_gain, ln1_bias, b_back, ln2_gain, ln2_bias, b_pool, jnp.zeros_like(b_pool)]
    )
    hidden, cls_part, *saved, masks = forward(
        tokens, lengths, w_qkv, b_qv, w_out, w_in, b_in, w_back, vectors, masks, ranks, gathers
    )
    if gathers:
        loss, w_pool_grad, b_pool_grad, cls_grad = contrast_whole(
            cls_part, masks, w_pool, vectors, ranks, sents
        )
        loss, b_pool_grad = loss[0, 0], b_pool_grad[0]
    else:
        cls_rows = cls_part.reshape(rows, -1, width)[:, :sents]
        cls_rows = lax.psum(cls_rows, "mp").astype(jnp.float32)
        loss, w_pool_grad, b_pool_grad, cls_grad = contrast(
            cls_rows.reshape(-1, width), view_masks, w_pool, b_pool
        )
        cls_grad = cls_grad.reshape(rows, -1, width)
        cls_grad = jnp.pad(cls_grad, [(0, 0), (0, 32 - sents), (0, 0)]).reshape(-1, width)
    sums, token_grad, vectors = backward(
        lengths, cls_grad, vectors, cotangent, saved, ranks
    )
    if pieces_of(ranks // 2) != ranks // 2:
        sums = lax.psum(sums, "dp")
    sums = sums.reshape(UNITS, UNIT, width).astype(jnp.float32)
    own = lax.axis_index("mp")
    cols = b_qv.shape[1]
    own_qv = lax.dynamic_slice_in_dim(vectors, 10 + own, 1, axis=0)
    own_in = lax.dynamic_slice_in_dim(vectors, 6 + own, 1, axis=0)
    return (
        hidden,
        loss,
        token_grad,
        sums[9:12].transpose(0, 2, 1),
        jnp.concatenate([own_qv[:, :cols], own_qv[:, 256 : 256 + cols]], axis=0),
        sums[8],
        vectors[0],
        vectors[1],
        vectors[2],
        sums[4:8].reshape(width, width),
        own_in[0],
        sums[0:4].reshape(width, width),
        vectors[3],
        vectors[4],
        vectors[5],
        w_pool_grad,
        b_pool_grad,
    )


def solution(mesh):
    in_specs = (
        P("dp", "mp", None),
        P("dp", None),
        P("dp", None, None, None),
        P(None, None, "mp"),
        P(None, "mp"),
        P("mp", None),
        P(),
        P(),
        P(),
        P(None, "mp"),
        P("mp"),
        P("mp", None),
        P(),
        P(),
        P(),
        P(),
        P(),
        P("dp", "mp", None),
    )
    out_specs = (
        P("dp", "mp", None),
        P(),
        P("dp", "mp", None),
        P(None, None, "mp"),
        P(None, "mp"),
        P("mp", None),
        P(),
        P(),
        P(),
        P(None, "mp"),
        P("mp"),
        P("mp", None),
        P(),
        P(),
        P(),
        P(),
        P(),
    )
    return jax.shard_map(shards, mesh=mesh, in_specs=in_specs, out_specs=out_specs, check_vma=False)
```

```python
import jax
import jax.numpy as jnp
from jax import lax
from jax.experimental import pallas as pl
from jax.experimental.pallas import tpu as pltpu
from jax.sharding import PartitionSpec as P

HDIM = 64
HALO = 32
BLOCK = 64
KEEP_SCALE = 1.0 / 0.9
MASKED = -1000000000.0


def norm_forward(values, gain, shift):
    center = values - jnp.mean(values, axis=-1, keepdims=True)
    inv_dev = lax.rsqrt(jnp.mean(center * center, axis=-1, keepdims=True) + 1e-12)
    normed = center * inv_dev
    return (normed * gain + shift, normed, inv_dev)


def dot32(equation, left, right):
    return jnp.einsum(equation, left, right, preferred_element_type=jnp.float32)


def contrast(cls_rows, view_masks, w_pool, b_pool):
    local_sents = cls_rows.shape[0]
    own_ids = lax.axis_index("dp") * local_sents + jnp.arange(local_sents, dtype=jnp.int32)
    keep_masks = view_masks.astype(jnp.float32).reshape(local_sents, 2, -1)
    views = (cls_rows[:, None, :] * keep_masks * KEEP_SCALE).astype(jnp.bfloat16)
    pooled = jnp.tanh(dot32("svd,de->sve", views, w_pool) + b_pool)
    inv_length = lax.rsqrt(jnp.sum(pooled * pooled, axis=-1, keepdims=True) + 1e-06)
    unit = pooled * inv_length
    unit_low = unit.astype(jnp.bfloat16)
    anchors = unit_low[:, 0]
    every_target = lax.all_gather(unit_low[:, 1], "dp", axis=0, tiled=True)
    logits = dot32("sd,td->st", anchors, every_target) * 20.0
    sent_ids = jnp.arange(every_target.shape[0], dtype=jnp.int32)
    is_partner = sent_ids[None, :] == own_ids[:, None]
    row_peak = jnp.max(logits, axis=1, keepdims=True)
    raised = jnp.exp(logits - row_peak)
    row_total = jnp.sum(raised, axis=1, keepdims=True)
    log_total = row_peak[:, 0] + jnp.log(row_total[:, 0])
    loss_local = jnp.sum(log_total - jnp.sum(jnp.where(is_partner, logits, 0.0), axis=1))
    logit_grad = (raised / row_total - is_partner.astype(jnp.float32)).astype(jnp.bfloat16)
    anchor_grad = dot32("st,td->sd", logit_grad, every_target) * 20.0
    target_terms = dot32("st,sd->td", logit_grad, anchors) * 20.0
    target_grad = lax.psum_scatter(target_terms, "dp", scatter_dimension=0, tiled=True)
    unit_grad = jnp.stack([anchor_grad, target_grad], axis=1)
    pooled_grad = inv_length * (
        unit_grad - unit * jnp.sum(unit_grad * unit, axis=-1, keepdims=True)
    )
    before_grad = (pooled_grad * (1.0 - pooled * pooled)).astype(jnp.bfloat16)
    w_pool_grad = dot32("svd,sve->de", views, before_grad)
    b_pool_grad = jnp.sum(before_grad, axis=(0, 1), dtype=jnp.float32)
    view_grad = dot32("sve,de->svd", before_grad, w_pool)
    cls_grad = jnp.sum(view_grad * keep_masks, axis=1) * KEEP_SCALE
    sums = lax.psum((w_pool_grad, b_pool_grad, loss_local), "dp")
    loss = sums[2] / (local_sents * lax.axis_size("dp"))
    return (loss, sums[0], sums[1], cls_grad)


MESH = pl.DeviceIdType.MESH
UNIT = 192
UNITS = 12


def greet(peers):
    barrier = pltpu.get_barrier_semaphore()
    for peer in peers:
        pl.semaphore_signal(barrier, inc=1, device_id=peer, device_id_type=MESH)
    pl.semaphore_wait(barrier, len(peers))


class Places:
    def __init__(self, dp_size):
        self.dp = lax.axis_index("dp")
        self.mp = lax.axis_index("mp")
        self.core = self.mp % 2
        self.y = self.mp // 2
        self.x = self.dp % 2
        self.z = self.dp // 2
        self.depth = dp_size // 2
        self.across_core = (self.dp, self.y * 2 + (1 - self.core))
        self.across_y = (self.dp, (1 - self.y) * 2 + self.core)
        self.across_both = (self.dp, (1 - self.y) * 2 + (1 - self.core))
        self.across_x = (self.z * 2 + (1 - self.x), self.mp)

    def along_z(self, step):
        return ((self.z + step) % self.depth * 2 + self.x, self.mp)

    def back_z(self, step):
        return (self.z + self.depth - step) % self.depth


def remote(src, dst, send_sem, recv_sem, device):
    return pltpu.make_async_remote_copy(
        src_ref=src,
        dst_ref=dst,
        send_sem=send_sem,
        recv_sem=recv_sem,
        device_id=device,
        device_id_type=MESH,
    )


def norm_tiles(count, tile, body):
    @pl.loop(0, count // tile)
    def _(i):
        body(pl.ds(pl.multiple_of(i * tile, tile), tile))


def row_marks(lengths_ref, local, first, share, region):
    rows, sents = lengths_ref.shape
    row_id = lax.broadcasted_iota(jnp.int32, local.shape, 0)
    places = local + first

    def per_row(values):
        out = jnp.full(local.shape, values[-1], jnp.int32)
        for r in range(rows - 1):
            out = jnp.where(row_id == r, values[r], out)
        return out

    def body(j, carry):
        passed, begun, ends = carry
        ends = tuple(ends[r] + lengths_ref[r, j] for r in range(rows))
        edge = per_row(ends)
        reached = places >= edge
        return (
            passed + reached.astype(jnp.int32),
            jnp.where(reached, edge, begun),
            ends,
        )

    zero = jnp.zeros(local.shape, jnp.int32)
    start = tuple(jnp.int32(0) for _ in range(rows))
    passed, begun, ends = lax.fori_loop(0, sents, body, (zero, zero, start))
    inside = places < per_row(ends)
    here = (local >= 0) & (local < region)
    segment = jnp.where(here, jnp.where(inside, passed, places + sents), -2)
    begins = (begun >= first) & (begun < first + share)
    owned = here & ((inside & begins) | (~inside & (local < share)))
    return (segment, owned)


def start_column(lengths_ref, row, first, slots):
    slot = lax.broadcasted_iota(jnp.int32, (slots, 1), 0)

    def body(j, carry):
        column, begin = carry
        column = jnp.where(slot == j, begin - first, column)
        return (column, begin + lengths_ref[row, j])

    column, _ = lax.fori_loop(
        0, lengths_ref.shape[1], body, (jnp.full((slots, 1), -1, jnp.int32), jnp.int32(0))
    )
    return column


def head_stack(values):
    lane = lax.broadcasted_iota(jnp.int32, values.shape, 1) // HDIM
    zero = jnp.zeros_like(values)
    return jnp.concatenate(
        [jnp.where(lane == h, values, zero) for h in range(values.shape[1] // HDIM)], axis=0
    )


def head_pick(stacked, width):
    heads = width // HDIM
    rows = stacked.shape[0] // heads
    lane = lax.broadcasted_iota(jnp.int32, (rows, width), 1) // HDIM
    out = stacked[:rows]
    for h in range(1, heads):
        out = jnp.where(lane == h, stacked[h * rows : (h + 1) * rows], out)
    return out


def nn(left, right):
    return jnp.dot(left, right, preferred_element_type=jnp.float32)


def nt(left, right):
    return lax.dot_general(
        left, right, (((1,), (1,)), ((), ())), preferred_element_type=jnp.float32
    )


def tn(left, right):
    return lax.dot_general(
        left, right, (((0,), (0,)), ((), ())), preferred_element_type=jnp.float32
    )


def shard_order(at):
    return [
        at.mp,
        at.y * 2 + (1 - at.core),
        (1 - at.y) * 2 + at.core,
        (1 - at.y) * 2 + (1 - at.core),
    ]


def forward_kernel(dp_size, gathers, *refs):
    (
        lengths_ref,
        tokens_hbm,
        wq_hbm,
        wo_hbm,
        wi_hbm,
        wb_hbm,
        bq_hbm,
        bi_hbm,
        masks_hbm,
        vectors,
        hidden_hbm,
        cls_ref,
        wq_out,
        wo_out,
        wi_out,
        wb_out,
        tok_out,
        q_out,
        k_out,
        v_out,
        p_out,
        o_out,
        h1_out,
        n1_out,
        r1_out,
        g_out,
        gp_out,
        n2_out,
        r2_out,
        own_out,
        masks_out,
        tok,
        wq,
        wo,
        wi,
        wb,
        bq,
        bi,
        q,
        k,
        v,
        probs,
        o,
        h1,
        n1,
        r1,
        g,
        gp,
        n2,
        r2,
        own,
        acc,
        upper,
        seg,
        key_seg,
        hid,
        hid_in,
        local_sem,
        halo_sem,
        bias_s,
        bias_r,
        core_s,
        core_r,
        y_s,
        y_r,
        x_s,
        x_r,
        yc_s,
        yc_r,
        xc_s,
        xc_r,
        out_sem,
        mask_s,
        mask_r,
    ) = refs
    at = Places(dp_size)
    rows, share, width = tokens_hbm.shape
    region = share + HALO
    total = rows * region
    m = at.mp
    b_out, gain1, shift1, b_back, gain2, shift2 = (vectors[i : i + 1] for i in range(6))
    first = m * share
    left = (at.dp, (m + 3) % 4)
    right = (at.dp, (m + 1) % 4)
    chunks = (
        [(wq, wq_hbm, (t,)) for t in range(3)]
        + [(wo, wo_hbm, ())]
        + [(wi, wi_hbm, (b,)) for b in range(4)]
        + [(wb, wb_hbm, (b,)) for b in range(4)]
    )
    whole = [(wq, wq_hbm), (wo, wo_hbm), (wi, wi_hbm), (wb, wb_hbm)]

    peers = [(at.dp, (m + j) % 4) for j in range(1, 4)] + [at.across_x]
    greet(peers + [at.along_z(step) for step in range(1, at.depth if gathers else 1)])

    loads = [
        pltpu.make_async_copy(tokens_hbm.at[r], tok.at[pl.ds(r * region, share)], local_sem.at[r])
        for r in range(rows)
    ]
    loads += [
        pltpu.make_async_copy(src, dst.at[0], local_sem.at[rows + i])
        for i, (dst, src) in enumerate(whole + [(bq, bq_hbm), (bi, bi_hbm)])
    ]
    for load in loads:
        load.start()
    halos = [
        remote(
            tokens_hbm.at[r, pl.ds(0, HALO)],
            tok.at[pl.ds(r * region + share, HALO)],
            halo_sem.at[0, r],
            halo_sem.at[1, r],
            left,
        )
        for r in range(rows)
    ]
    for copy in halos:
        copy.start()
    biases = []
    for j, device in enumerate((at.across_core, at.across_y, at.across_both), start=1):
        for i, (dst, src) in enumerate([(bq, bq_hbm), (bi, bi_hbm)]):
            biases.append(
                remote(src, dst.at[j], bias_s.at[j - 1, i], bias_r.at[j - 1, i], device)
            )
    for copy in biases:
        copy.start()

    def core_copy(i):
        dst, src = whole[i]
        return remote(src, dst.at[1], core_s.at[i], core_r.at[i], at.across_core)

    def y_copy(c):
        dst, src, index = chunks[c]
        place = (*index, at.x)
        return remote(src.at[place], dst.at[(2, *place)], y_s.at[c], y_r.at[c], at.across_y)

    def x_copy(c):
        ref = chunks[c][0].at[(2, *chunks[c][2], at.x)]
        return remote(ref, ref, x_s.at[c], x_r.at[c], at.across_x)

    def yc_copy(c):
        ref, _, index = chunks[c]
        place = (*index, at.x)
        return remote(
            ref.at[(2, *place)], ref.at[(3, *place)], yc_s.at[c], yc_r.at[c], at.across_core
        )

    def xc_copy(c):
        ref, _, index = chunks[c]
        place = (*index, 1 - at.x)
        return remote(
            ref.at[(2, *place)], ref.at[(3, *place)], xc_s.at[c], xc_r.at[c], at.across_core
        )

    mask_hops = []
    if gathers:
        mask_own = pltpu.make_async_copy(
            masks_hbm.at[at.core], masks_out.at[at.z, at.x, at.core], mask_s.at[0]
        )
        mask_own.start()
        mask_hops = [
            remote(
                masks_hbm.at[at.core],
                masks_out.at[at.z, at.x, at.core],
                mask_s.at[at.depth],
                mask_r.at[at.depth],
                at.across_x,
            )
        ]
        for step in range(1, at.depth):
            pair = masks_out.at[at.z, :, at.core]
            mask_hops.append(
                remote(pair, pair, mask_s.at[step], mask_r.at[step], at.along_z(step))
            )
        view = masks_out.at[:, :, at.core]
        index = at.depth + 1
        mask_hops.append(
            remote(view, view, mask_s.at[index], mask_r.at[index], at.across_core)
        )
        mask_hops[0].start()

    def pass_masks(stage):
        if not gathers:
            return
        come = [mask_hops[:1], mask_hops[1:-1], mask_hops[-1:]]
        if stage == 0:
            mask_own.wait()
        for hop in come[stage]:
            hop.wait_recv()
        if stage < 2:
            for hop in come[stage + 1]:
                hop.start()

    for c in range(12):
        y_copy(c).start()
    for i in range(4):
        core_copy(i).start()

    def pass_y(*numbers):
        for c in numbers:
            y_copy(c).wait_recv()
            x_copy(c).start()
            yc_copy(c).start()

    def pass_x(*numbers):
        for c in numbers:
            x_copy(c).wait_recv()
            xc_copy(c).start()

    saves = []

    def save(src, dst):
        copy = pltpu.make_async_copy(src, dst, out_sem.at[len(saves)])
        copy.start()
        saves.append(copy)

    lane = lax.broadcasted_iota(jnp.int32, (8, 384), 1)
    segment, owned = row_marks(lengths_ref, lane, first, share, region)
    seg_cols = segment.astype(jnp.float32).T
    own_cols = owned.astype(jnp.float32).T
    for r in range(rows):
        seg[r] = jnp.broadcast_to(seg_cols[: seg.shape[1], r : r + 1], seg.shape[1:])
        own[pl.ds(r * region, region)] = own_cols[:region, r : r + 1]
    save(own, own_out)
    for r in range(rows):
        block = lax.broadcasted_iota(jnp.int32, (8, BLOCK + 2 * HALO), 0)
        offset = lax.broadcasted_iota(jnp.int32, (8, BLOCK + 2 * HALO), 1)
        keys, _ = row_marks(
            RowView(lengths_ref, r), block * BLOCK + offset - HALO, first, share, region
        )
        key_seg[r] = keys.astype(jnp.float32)
    blocks = q.shape[2] // BLOCK

    q[...] = jnp.zeros_like(q)
    k[...] = jnp.zeros_like(k)
    v[...] = jnp.zeros_like(v)

    for load in loads:
        load.wait()
    for copy in halos:
        copy.wait()
    for copy in biases:
        copy.wait_recv()
    save(tok, tok_out)

    def project(s):
        @pl.loop(0, rows)
        def _(r):
            x = tok[pl.ds(pl.multiple_of(r * region, 32), region)]
            for t, dst in enumerate((q, k, v)):
                y = nn(x, wq[s, t].reshape(width, -1))
                if t == 0:
                    y = (y + bq[s, 0:1]).astype(jnp.bfloat16) * jnp.bfloat16(0.125)
                elif t == 1:
                    y = y.astype(jnp.bfloat16)
                else:
                    y = (y + bq[s, 1:2]).astype(jnp.bfloat16)
                lead = 0 if t == 0 else HALO
                dst[s, r, lead : lead + region] = y

    def attend(s):
        heads = q.shape[3] // HDIM

        @pl.loop(0, rows)
        def _(r):
            for b in range(blocks):
                queries = head_stack(q[s, r, b * BLOCK : (b + 1) * BLOCK])
                window = slice(b * BLOCK, b * BLOCK + BLOCK + 2 * HALO)
                scores = nt(queries, k[s, r, window])
                allowed = seg[r, b * BLOCK : (b + 1) * BLOCK] == key_seg[r, b : b + 1]
                scores = jnp.where(jnp.concatenate([allowed] * heads, axis=0), scores, MASKED)
                peak = jnp.max(scores, axis=1, keepdims=True)
                raised = jnp.exp(scores - peak)
                weights = (raised / jnp.sum(raised, axis=1, keepdims=True)).astype(jnp.bfloat16)
                probs[s, r * blocks + b] = weights
                context = nn(weights, v[s, r, window])
                o[s, r, b * BLOCK : (b + 1) * BLOCK] = head_pick(context, heads * HDIM).astype(
                    jnp.bfloat16
                )

    project(0)
    attend(0)
    pass_y(0)
    core_copy(0).wait_recv()
    pass_y(1)
    pass_masks(0)
    project(1)
    pass_y(2)
    attend(1)
    pass_y(3)
    pass_x(0, 1, 2)
    project(2)
    attend(2)
    pass_y(4, 5)
    pass_x(3)
    for c in range(3):
        yc_copy(c).wait_recv()
        xc_copy(c).wait_recv()
    project(3)
    pass_y(6)
    attend(3)
    pass_y(7)
    pass_x(4, 5)
    save(wq, wq_out)
    save(q, q_out)
    save(k, k_out)
    save(v, v_out)
    save(probs, p_out)
    save(o, o_out)

    core_copy(1).wait_recv()
    yc_copy(3).wait_recv()
    xc_copy(3).wait_recv()
    save(wo, wo_out)

    @pl.loop(0, rows)
    def _(r):
        y = nn(o[0, r, :region], wo[0].reshape(-1, width))
        for s in range(1, 4):
            y = y + nn(o[s, r, :region], wo[s].reshape(-1, width))
        acc[pl.ds(pl.multiple_of(r * region, 32), region)] = y


    def first_norm(part):
        values = tok[part].astype(jnp.float32) + acc[part] + b_out
        normed, unit, inv = norm_forward(values, gain1, shift1)
        n1[part] = unit
        r1[part] = inv
        h1[part] = normed.astype(jnp.bfloat16)
        acc[part] = normed + b_back

    pass_y(8)
    norm_tiles(total, 96, first_norm)
    save(h1, h1_out)
    save(n1, n1_out)
    save(r1, r1_out)
    pass_x(6)

    def raise_units(s):
        @pl.loop(0, 3)
        def _(n):
            columns = pl.ds(pl.multiple_of(n * 256, 256), 256)
            upper[...] = nn(h1[...], wi[s, :, :, :, columns].reshape(width, 256))

            def activate(part):
                u = upper[part] + bi[s, :, columns]
                cdf = 0.5 * (1.0 + lax.erf(u * 0.7071067811865476))
                g[s, part, columns] = (u * cdf).astype(jnp.bfloat16)
                slope = cdf + u * jnp.exp(-0.5 * u * u) * 0.3989422804014327
                gp[s, part, columns] = slope.astype(jnp.bfloat16)

            norm_tiles(total, 96, activate)

    def lower_units(s):
        @pl.loop(0, rows)
        def _(r):
            part = pl.ds(pl.multiple_of(r * region, 32), region)
            acc[part] = acc[part] + nn(g[s, part], wb[s].reshape(width, width))

    core_copy(2).wait_recv()
    raise_units(0)
    pass_y(9)
    pass_x(7)
    core_copy(3).wait_recv()
    lower_units(0)
    pass_masks(1)
    raise_units(1)
    pass_y(10, 11)
    pass_x(8, 9)
    lower_units(1)
    for c in range(4, 8):
        yc_copy(c).wait_recv()
        xc_copy(c).wait_recv()
    save(wi, wi_out)
    raise_units(2)
    pass_x(10)
    raise_units(3)
    save(g, g_out)
    save(gp, gp_out)
    pass_x(11)
    lower_units(2)
    pass_masks(2)
    for c in range(8, 12):
        yc_copy(c).wait_recv()
        xc_copy(c).wait_recv()
    save(wb, wb_out)
    lower_units(3)

    def second_norm(part):
        normed, unit, inv = norm_forward(acc[part], gain2, shift2)
        n2[part] = unit
        r2[part] = inv
        hid[part] = normed.astype(jnp.bfloat16)

    norm_tiles(total, 96, second_norm)
    save(n2, n2_out)
    save(r2, r2_out)

    slots = cls_ref.shape[0] // rows
    for r in range(rows):
        place = lax.broadcasted_iota(jnp.int32, (slots, share), 1)
        pick = place == start_column(lengths_ref, r, first, slots)
        cls_ref[r * slots : (r + 1) * slots] = nn(
            pick.astype(jnp.bfloat16), hid[r * region : r * region + share]
        ).astype(jnp.bfloat16)

    def mask_hidden(part):
        hid[part] = (hid[part].astype(jnp.float32) * own[part]).astype(jnp.bfloat16)

    norm_tiles(total, 96, mask_hidden)
    settled = [
        remote(
            hid.at[pl.ds(r * region + share, HALO)],
            hid_in.at[r],
            halo_sem.at[2, r],
            halo_sem.at[3, r],
            right,
        )
        for r in range(rows)
    ]
    for copy in settled:
        copy.start()
    for copy in settled:
        copy.wait()
    for r in range(rows):
        head = pl.ds(r * region, HALO)
        hid[head] = hid[head] + hid_in[r]
    for r in range(rows):
        save(hid.at[pl.ds(r * region, share)], hidden_hbm.at[r])

    for copy in saves:
        copy.wait()
    for copy in biases + mask_hops:
        copy.wait_send()
    for i in range(4):
        core_copy(i).wait_send()
    for c in range(12):
        y_copy(c).wait_send()
        x_copy(c).wait_send()
        yc_copy(c).wait_send()
        xc_copy(c).wait_send()


class RowView:
    def __init__(self, ref, row):
        self.ref, self.row = ref, row
        self.shape = (1, ref.shape[1])

    def __getitem__(self, index):
        return self.ref[self.row, index[1]]


def forward(tokens, lengths, w_qkv, b_qv, w_out, w_in, b_in, w_back, vectors, masks, dp_size, gathers):
    rows, share, width = tokens.shape
    region = share + HALO
    total = rows * region
    blocks = -(-region // BLOCK)
    padded = blocks * BLOCK
    keyed = padded + 2 * HALO
    low, full = jnp.bfloat16, jnp.float32
    head_cols = w_qkv.shape[2]
    slots = 32
    shape = jax.ShapeDtypeStruct
    saved = [
        ((4, 3, 2, width // 2, head_cols), low),
        ((4, 2, head_cols // 2, width), low),
        ((4, 4, 2, width // 8, width), low),
        ((4, 4, 2, width // 8, width), low),
        ((total, width), low),
        ((4, rows, padded, head_cols), low),
        ((4, rows, keyed, head_cols), low),
        ((4, rows, keyed, head_cols), low),
        ((4, rows * blocks, head_cols // HDIM * BLOCK, BLOCK + 2 * HALO), low),
        ((4, rows, padded, head_cols), low),
        ((total, width), low),
        ((total, width), full),
        ((total, 1), full),
        ((4, total, width), low),
        ((4, total, width), low),
        ((total, width), full),
        ((total, 1), full),
        ((total, 1), full),
    ]
    out_shape = [shape((rows, share, width), low), shape((rows * slots, width), low)]
    out_shape += [shape(*item) for item in saved]
    out_shape += [shape((dp_size // 2, 2, *masks.shape) if gathers else (8, 128), low)]
    held = [pltpu.VMEM(*item) for item in saved]
    dma = pltpu.SemaphoreType.DMA
    scratch = [held[4]] + held[:4]
    scratch += [pltpu.VMEM((4, 2, head_cols), full), pltpu.VMEM((4, 1, width), full)]
    scratch += held[5:]
    scratch += [
        pltpu.VMEM((total, width), full),
        pltpu.VMEM((total, 256), full),
        pltpu.VMEM((rows, padded, BLOCK + 2 * HALO), full),
        pltpu.VMEM((rows, 8, BLOCK + 2 * HALO), full),
        pltpu.VMEM((total, width), low),
        pltpu.VMEM((rows, HALO, width), low),
        dma((rows + 6,)),
        dma((4, rows)),
        dma((3, 2)),
        dma((3, 2)),
        dma((4,)),
        dma((4,)),
        *[dma((12,))] * 8,
        dma((24,)),
        dma((dp_size // 2 + 2,)),
        dma((dp_size // 2 + 2,)),
    ]
    anywhere = pl.BlockSpec(memory_space=pl.ANY)
    vmem = pl.BlockSpec(memory_space=pltpu.VMEM)
    row = lambda vector: vector.reshape(1, -1)
    return pl.pallas_call(
        lambda *refs: forward_kernel(dp_size, gathers, *refs),
        out_shape=out_shape,
        in_specs=[pl.BlockSpec(memory_space=pltpu.SMEM)] + [anywhere] * 8 + [vmem],
        out_specs=[anywhere, vmem] + [anywhere] * (len(saved) + 1),
        scratch_shapes=scratch,
        compiler_params=pltpu.CompilerParams(
            collective_id=2, has_side_effects=True, vmem_limit_bytes=64 * 1024 * 1024 - 65536
        ),
        name="forward",
    )(
        lengths,
        tokens,
        w_qkv.reshape(3, 2, width // 2, head_cols),
        w_out.reshape(2, head_cols // 2, width),
        w_in.reshape(4, 2, width // 8, width),
        w_back.reshape(4, 2, width // 8, width),
        b_qv,
        row(b_in),
        masks,
        vectors,
    )


class Reducer:
    def __init__(self, at, bufs):
        self.at = at
        self.pieces = pieces_of(at.depth)
        self.plane = self.pieces == at.depth
        self.ready = 0
        (
            self.parts,
            self.core_in,
            self.y_in,
            self.x_in,
            self.z_in,
            self.whole,
            self.done,
            self.core_s,
            self.core_r,
            self.y_s,
            self.y_r,
            self.x_s,
            self.x_r,
            self.z_s,
            self.z_r,
            self.za_s,
            self.za_r,
            self.xa_s,
            self.xa_r,
            self.own_s,
            self.out_s,
        ) = bufs

    def core_copy(self, u):
        at = self.at
        return remote(
            self.parts.at[1, :, u],
            self.core_in.at[:, u],
            self.core_s.at[u],
            self.core_r.at[u],
            at.across_core,
        )

    def y_copy(self, u):
        at = self.at
        return remote(
            self.parts.at[0, 1, u],
            self.y_in.at[u],
            self.y_s.at[u],
            self.y_r.at[u],
            at.across_y,
        )

    def x_copy(self, u):
        return remote(
            self.parts.at[0, 0, u, 1],
            self.x_in.at[u],
            self.x_s.at[u],
            self.x_r.at[u],
            self.at.across_x,
        )

    def z_copy(self, u, step):
        at = self.at
        return remote(
            self.parts.at[0, 0, u, 0, (at.z + step) % at.depth],
            self.z_in.at[u, step - 1],
            self.z_s.at[u, step - 1],
            self.z_r.at[u, step - 1],
            at.along_z(step),
        )

    def za_copy(self, u, step):
        at = self.at
        return remote(
            self.done.at[u],
            self.whole.at[u, 0, at.z],
            self.za_s.at[u, step - 1],
            self.za_r.at[u, step - 1],
            at.along_z(step),
        )

    def own_copy(self, u):
        return pltpu.make_async_copy(
            self.done.at[u], self.whole.at[u, 0, self.at.z], self.own_s.at[u]
        )

    def xa_copy(self, u):
        return remote(
            self.whole.at[u, 0],
            self.whole.at[u, 1],
            self.xa_s.at[u],
            self.xa_r.at[u],
            self.at.across_x,
        )

    def out_copies(self, u, out):
        held = self.whole.at[u] if self.plane else self.parts.at[0, 0, u]
        return [
            pltpu.make_async_copy(
                held.at[half],
                out.at[u, :, :, pl.ds(pl.multiple_of(side * 384, 128), 384)],
                self.out_s.at[u, half],
            )
            for half, side in ((0, self.at.x), (1, 1 - self.at.x))
        ]

    def add(self, place, source, at):
        @pl.loop(0, self.pieces)
        def _(p):
            mine = self.parts[(*place, p)].astype(jnp.float32)
            both = mine + source[(*at, p)].astype(jnp.float32)
            self.parts[(*place, p)] = both.astype(jnp.bfloat16)

    def start(self, u):
        self.core_copy(u).start()

    def add_far(self, u):
        self.core_copy(u).wait_recv()
        for half in range(2):
            self.add((0, 1, u, half), self.core_in, (1, u, half))
        self.y_copy(u).start()

    def add_near(self, u):
        for half in range(2):
            self.add((0, 0, u, half), self.core_in, (0, u, half))

    def add_y(self, u):
        self.y_copy(u).wait_recv()
        self.add((0, 0, u, 1), self.y_in, (u, 1))
        if self.plane:
            self.x_copy(u).start()
        self.add((0, 0, u, 0), self.y_in, (u, 0))

    def add_x(self, u):
        self.x_copy(u).wait_recv()
        self.add((0, 0, u, 0), self.x_in, (u,))
        for step in range(1, self.at.depth):
            self.z_copy(u, step).start()

    def add_z(self, u):
        at = self.at
        total = self.parts[0, 0, u, 0, at.z].astype(jnp.float32)
        for step in range(1, at.depth):
            self.z_copy(u, step).wait_recv()
            total = total + self.z_in[u, step - 1].astype(jnp.float32)
        self.done[u] = total.astype(jnp.bfloat16)
        for step in range(1, at.depth):
            self.za_copy(u, step).start()
        self.own_copy(u).start()

    def spread_x(self, u):
        self.own_copy(u).wait()
        for step in range(1, self.at.depth):
            self.za_copy(u, step).wait_recv()
        self.xa_copy(u).start()

    def finish(self, u, out):
        if self.plane:
            self.xa_copy(u).wait_recv()
        for copy in self.out_copies(u, out):
            copy.start()

    def drain(self, u, out):
        self.core_copy(u).wait_send()
        self.y_copy(u).wait_send()
        for copy in self.out_copies(u, out):
            copy.wait()
        if not self.plane:
            return
        self.x_copy(u).wait_send()
        self.xa_copy(u).wait_send()
        for step in range(1, self.at.depth):
            self.z_copy(u, step).wait_send()
            self.za_copy(u, step).wait_send()


def pieces_of(depth):
    return depth if UNIT % (16 * depth) == 0 else 4


def reducer_scratch(depth):
    lanes = max(depth - 1, 1)
    depth = pieces_of(depth)
    rows = UNIT // depth
    dma = pltpu.SemaphoreType.DMA
    low = jnp.bfloat16
    return [
        pltpu.VMEM((2, 2, UNITS, 2, depth, rows, 384), low),
        pltpu.VMEM((2, UNITS, 2, depth, rows, 384), low),
        pltpu.VMEM((UNITS, 2, depth, rows, 384), low),
        pltpu.VMEM((UNITS, depth, rows, 384), low),
        pltpu.VMEM((UNITS, lanes if depth == lanes + 1 else 1, rows, 384), low),
        pltpu.VMEM((UNITS, 2, depth, rows, 384), low),
        pltpu.VMEM((UNITS, rows, 384), low),
        *[dma((UNITS,))] * 6,
        *[dma((UNITS, lanes if depth == lanes + 1 else 1))] * 4,
        *[dma((UNITS,))] * 3,
        dma((UNITS, 2)),
    ]


class Ring:
    def __init__(self, slots, sem, sources):
        self.slots, self.sem, self.sources = slots, sem, sources
        self.count = len(slots)
        self.used = 0
        for i in range(min(self.count, len(sources))):
            self.copy(i).start()

    def copy(self, i):
        return pltpu.make_async_copy(
            self.sources[i], self.slots[i % self.count], self.sem.at[i]
        )

    def take(self):
        self.copy(self.used).wait()
        return self.slots[self.used % self.count]

    def free(self):
        ahead = self.used + self.count
        if ahead < len(self.sources):
            self.copy(ahead).start()
        self.used += 1


def backward_kernel(dp_size, *refs):
    (
        lengths_ref,
        cls_grad,
        vectors,
        cot_hbm,
        wq_hbm,
        wo_hbm,
        wi_hbm,
        wb_hbm,
        tok_hbm,
        q_hbm,
        k_hbm,
        v_hbm,
        p_hbm,
        o_hbm,
        h1_hbm,
        n1_hbm,
        r1_hbm,
        g_hbm,
        gp_hbm,
        n2_hbm,
        r2_hbm,
        own_hbm,
        sums_hbm,
        grad_hbm,
        vec_out,
        own,
        cot,
        unit,
        inv1,
        inv2,
        acc,
        df,
        turned,
        h1,
        tok,
        q,
        k,
        v,
        probs,
        o,
        wo,
        w0,
        w1,
        w2,
        wq0,
        wq1,
        g0,
        g1,
        gp0,
        gp1,
        du,
        do,
        dq_pad,
        dkv,
        dqkv,
        vec,
        vec_in,
        vec_z,
        halo_in,
        load_sem,
        g_sem,
        w_sem,
        gp_sem,
        wq_sem,
        halo_sem,
        vec_s,
        vec_r,
        *bufs,
    ) = refs
    at = Places(dp_size)
    red = Reducer(at, bufs)
    rows, share, width = cot_hbm.shape
    region = share + HALO
    total = rows * region
    m = at.mp
    first = m * share
    left = (at.dp, (m + 3) % 4)
    right = (at.dp, (m + 1) % 4)
    gain1, gain2 = vectors[1:2], vectors[4:5]
    order = (1, 3, 2, 0)
    true_shard = shard_order(at)

    def loading(i, src, dst):
        return pltpu.make_async_copy(src, dst, load_sem.at[i])

    cots = [
        loading(r, cot_hbm.at[r], cot.at[pl.ds(r * region, share)]) for r in range(rows)
    ]
    early = cots + [
        loading(rows + i, src, dst)
        for i, (src, dst) in enumerate(
            [(own_hbm, own), (n2_hbm, unit), (r2_hbm, inv2), (r1_hbm, inv1)]
        )
    ]
    for copy in early:
        copy.start()
    g_ring = Ring((g0, g1), g_sem, [g_hbm.at[s] for s in order])
    w_sources = [ref.at[s] for s in order for ref in (wb_hbm, wi_hbm)]
    w_ring = Ring((w0, w1, w2), w_sem, w_sources)
    gp_ring = Ring((gp0, gp1), gp_sem, [gp_hbm.at[s] for s in order])
    late = [
        loading(rows + 4 + i, src, dst)
        for i, (src, dst) in enumerate(
            [
                (h1_hbm, h1),
                (tok_hbm, tok),
                (o_hbm, o),
                (wo_hbm, wo),
                (q_hbm, q),
                (k_hbm, k),
                (v_hbm, v),
                (p_hbm, probs),
            ]
        )
    ]
    for copy in late:
        copy.start()
    wq_ring = Ring((wq0, wq1), wq_sem, [wq_hbm.at[s] for s in order])

    peers = [(at.dp, (m + j) % 4) for j in range(1, 4)] + [at.across_x]
    greet(peers + [at.along_z(step) for step in range(1, at.depth)])
    halos = [
        remote(
            cot_hbm.at[r, pl.ds(0, HALO)],
            cot.at[pl.ds(r * region + share, HALO)],
            halo_sem.at[0, r],
            halo_sem.at[1, r],
            left,
        )
        for r in range(rows)
    ]
    for copy in halos:
        copy.start()

    expected = []
    for u in range(UNITS):
        arrives = 13.5 + 6.3 * (u + 1)
        expected.append((arrives, u, red.add_y))
        if red.plane:
            expected.append((arrives + 5.0, u, red.add_x))
            expected.append((arrives + 11.0, u, red.add_z))
            expected.append((arrives + 17.0, u, red.spread_x))
        expected.append((arrives + 22.0, u, lambda u: red.finish(u, sums_hbm)))
    expected.sort(key=lambda event: event[0])

    def pump(until):
        while expected and expected[0][0] <= until and expected[0][1] < red.ready:
            _, u, event = expected.pop(0)
            event(u)

    vec[0] = jnp.zeros(vec.shape[1:], jnp.float32)
    slots = cls_grad.shape[0] // rows
    for copy in early:
        copy.wait()
    for copy in halos:
        copy.wait()

    def norm_back(part, grad, gain, inv, base):
        normed, inv_dev = unit[part], inv[part]
        scaled = grad * gain
        centered = scaled - jnp.mean(scaled, axis=-1, keepdims=True)
        inner = jnp.mean(scaled * normed, axis=-1, keepdims=True)
        grad_in = inv_dev * (centered - normed * inner)
        acc[part] = grad_in
        df[part] = grad_in.astype(jnp.bfloat16)
        vec[0, base : base + 1] += jnp.sum(grad_in, axis=0, keepdims=True)
        vec[0, base + 1 : base + 2] += jnp.sum(grad * normed, axis=0, keepdims=True)
        vec[0, base + 2 : base + 3] += jnp.sum(grad, axis=0, keepdims=True)

    tile = 96
    for r in range(rows):
        starts = start_row(lengths_ref, r, first, slots)
        come = cls_grad[r * slots : (r + 1) * slots]
        terms = []
        for _ in range(3):
            term = come.astype(jnp.bfloat16)
            terms.append(term)
            come = come - term.astype(jnp.float32)

        @pl.loop(0, region // tile)
        def _(i):
            part = pl.ds(pl.multiple_of(r * region + i * tile, 32), tile)
            place = i * tile + lax.broadcasted_iota(jnp.int32, (tile, slots), 0)
            hit = (place == starts) & (place < share)
            pick = jnp.where(hit, 1.0, 0.0).astype(jnp.bfloat16)
            grad = cot[part].astype(jnp.float32)
            for term in terms:
                grad = grad + nn(pick, term)
            norm_back(part, grad * own[part], gain2, inv2, 3)

    first_unit = pltpu.make_async_copy(n1_hbm, unit, load_sem.at[1])
    first_unit.start()

    def put(s, u, half, values):
        low = values.astype(jnp.bfloat16)
        for i in range(values.shape[0] // UNIT):
            red.parts[s % 2, s // 2, u + i, half] = low[i * UNIT : (i + 1) * UNIT].reshape(
                red.pieces, UNIT // red.pieces, 384
            )

    def true_half(half):
        return (at.x + half) % 2

    def true_columns(half):
        return pl.ds(pl.multiple_of(true_half(half) * 384, 128), 384)

    def sent(i, units):
        if i == 1:
            for u in units:
                red.start(u)
        if i == 2:
            for u in units:
                red.add_far(u)
        if i == 3:
            for u in units:
                red.add_near(u)
            red.ready = units[-1] + 1

    for i in range(4):
        g = g_ring.take()
        turned[...] = g[...].T
        g_ring.free()

        for half in range(2):
            put(order[i], 0, half, nn(turned[...], df[:, true_columns(half)]))

        sent(i, range(4))
    late[0].wait()
    turned[...] = h1[...].T
    for i in range(4):
        s = order[i]
        wb = w_ring.take()
        slope = gp_ring.take()

        for half in range(2):
            columns = true_columns(half)
            rows_here = pl.ds(2 * true_half(half), 2)
            rise = nt(df[...], wb[rows_here].reshape(384, width))
            rise = (rise * slope[:, columns].astype(jnp.float32)).astype(jnp.bfloat16)
            du[:, columns] = rise
            vec[0, pl.ds(6 + true_shard[s], 1), columns] = jnp.sum(
                rise.astype(jnp.float32), axis=0, keepdims=True
            )
            put(s, 4, half, nn(turned[...], rise))

        w_ring.free()
        gp_ring.free()
        pump(16.5 + 7.5 * i)
        wi = w_ring.take()
        sent(i, range(4, 8))

        @pl.loop(0, rows)
        def _(r):
            part = pl.ds(pl.multiple_of(r * region, 32), region)
            acc[part] = acc[part] + nt(du[part], wi[...].reshape(width, width))

        w_ring.free()
        pump(20.0 + 7.5 * i)

    first_unit.wait()

    @pl.loop(0, total // tile)
    def _(i):
        part = pl.ds(pl.multiple_of(i * tile, tile), tile)
        norm_back(part, acc[part], gain1, inv1, 0)

    for copy in late[1:]:
        copy.wait()
    pump(46.0)

    heads = q.shape[3] // HDIM
    cols = heads * HDIM
    blocks = q.shape[2] // BLOCK
    for i in range(4):
        s = order[i]
        flat = jnp.concatenate([o[s, r, :region] for r in range(rows)], axis=0)
        for half in range(2):
            put(s, 8, half, tn(flat, df[:, true_columns(half)]))
        sent(i, [8])
    pump(50.0)
    do[...] = jnp.zeros_like(do)
    for i in range(4):
        s = order[i]
        back = nt(df[...], wo[s].reshape(cols, width)).astype(jnp.bfloat16)
        for r in range(rows):
            do[r, :region] = back[r * region : (r + 1) * region]
        dkv[...] = jnp.zeros_like(dkv)
        @pl.loop(0, blocks)
        def _(b):
            here = pl.ds(pl.multiple_of(b * BLOCK, BLOCK), BLOCK)
            window = pl.ds(pl.multiple_of(b * BLOCK, BLOCK), BLOCK + 2 * HALO)
            for r in range(rows):
                grads = head_stack(do[r, here])
                queries = head_stack(q[s, r, here])
                weight = probs[s, r * blocks + b]
                wide = weight.astype(jnp.float32)
                rise = nt(grads, v[s, r, window])
                inner = jnp.sum(wide * rise, axis=1, keepdims=True)
                fall = (wide * (rise - inner)).astype(jnp.bfloat16)
                dq = head_pick(nn(fall, k[s, r, window]), cols) * 0.125
                dq_pad[r, here] = dq.astype(jnp.bfloat16)
                dkv[0, r, window] += tn(fall, queries)
                dkv[1, r, window] += tn(weight, grads)

        for r in range(rows):
            dqkv[0, r * region : (r + 1) * region] = dq_pad[r, :region]
            for t in range(2):
                dqkv[1 + t, r * region : (r + 1) * region] = dkv[
                    t, r, HALO : HALO + region
                ].astype(jnp.bfloat16)
        pump(54.5 + 10.0 * i)
        wqs = wq_ring.take()
        for t, lane in ((0, 0), (1, None), (2, 256)):
            part = dqkv[t]
            if lane is not None:
                vec[0, pl.ds(10 + true_shard[s], 1), lane : lane + cols] = jnp.sum(
                    part.astype(jnp.float32), axis=0, keepdims=True
                )
            for half in range(2):
                put(s, 9 + t, half, tn(part, tok[:, true_columns(half)]))

            @pl.loop(0, rows)
            def _(r, t=t):
                here = pl.ds(pl.multiple_of(r * region, 32), region)
                acc[here] = acc[here] + nt(dqkv[t, here], wqs[t].reshape(width, cols))

        wq_ring.free()
        sent(i, range(9, 12))
        pump(59.0 + 10.0 * i)

    def mask_grad(part):
        acc[part] = acc[part] * own[part]

    norm_tiles(total, tile, mask_grad)
    settled = [
        remote(
            acc.at[pl.ds(r * region + share, HALO)],
            halo_in.at[r],
            halo_sem.at[2, r],
            halo_sem.at[3, r],
            right,
        )
        for r in range(rows)
    ]
    for copy in settled:
        copy.start()

    def vec_copy(i):
        device = (at.across_core, at.across_y, at.across_x)[i]
        return remote(vec.at[i], vec_in.at[i], vec_s.at[i], vec_r.at[i], device)

    def vec_z_copy(step):
        index = 2 + step
        return remote(
            vec.at[3], vec_z.at[step], vec_s.at[index], vec_r.at[index], at.along_z(step)
        )

    vec_copy(0).start()
    pump(94.0)
    grads = []
    for copy in settled:
        copy.wait()
    for r in range(rows):
        head = pl.ds(r * region, HALO)
        acc[head] = acc[head] + halo_in[r]
    for r in range(rows):
        copy = loading(r, acc.at[pl.ds(r * region, share)], grad_hbm.at[r])
        copy.start()
        grads.append(copy)
    for i in range(3):
        vec_copy(i).wait_recv()
        both = vec[i] + vec_in[i]
        if i < 2:
            vec[i + 1] = both
            vec_copy(i + 1).start()
        else:
            vec[3] = both
            vec_z[0] = both
            for step in range(1, at.depth):
                vec_z_copy(step).start()
        pump(97.0 + 4.0 * i)
    for step in range(1, at.depth):
        vec_z_copy(step).wait_recv()
    both = vec_z[at.back_z(0)]
    for z in range(1, at.depth):
        both = both + vec_z[at.back_z(z)]
    vec_out[...] = both
    pump(1000.0)
    for copy in grads:
        copy.wait()
    for i in range(3):
        vec_copy(i).wait_send()
    for step in range(1, at.depth):
        vec_z_copy(step).wait_send()

    @pl.loop(0, UNITS)
    def _(u):
        red.drain(u, sums_hbm)


def start_row(lengths_ref, row, first, slots):
    slot = lax.broadcasted_iota(jnp.int32, (1, slots), 1)

    def body(j, carry):
        line, begin = carry
        return (jnp.where(slot == j, begin - first, line), begin + lengths_ref[row, j])

    line, _ = lax.fori_loop(
        0, lengths_ref.shape[1], body, (jnp.full((1, slots), -1, jnp.int32), jnp.int32(0))
    )
    return line


def backward(lengths, cls_grad, vectors, cotangent, saved, dp_size):
    rows, share, width = cotangent.shape
    region = share + HALO
    total = rows * region
    q, k, probs, o = saved[5], saved[6], saved[8], saved[9]
    depth = dp_size // 2
    low, full = jnp.bfloat16, jnp.float32
    cols = q.shape[3]
    dma = pltpu.SemaphoreType.DMA
    vmem = pltpu.VMEM
    scratch = [
        vmem((total, 1), full),
        vmem((total, width), low),
        vmem((total, width), full),
        vmem((total, 1), full),
        vmem((total, 1), full),
        vmem((total, width), full),
        vmem((total, width), low),
        vmem((width, total), low),
        vmem((total, width), low),
        vmem((total, width), low),
        vmem(q.shape, low),
        vmem(k.shape, low),
        vmem(k.shape, low),
        vmem(probs.shape, low),
        vmem(o.shape, low),
        vmem(saved[1].shape, low),
        *[vmem(saved[2].shape[1:], low)] * 3,
        *[vmem(saved[0].shape[1:], low)] * 2,
        *[vmem((total, width), low)] * 4,
        vmem((total, width), low),
        vmem(q.shape[1:], low),
        vmem(q.shape[1:], low),
        vmem((2, *k.shape[1:]), full),
        vmem((3, total, cols), low),
        vmem((4, 16, width), full),
        vmem((3, 16, width), full),
        vmem((depth, 16, width), full),
        vmem((rows, HALO, width), full),
        dma((rows + 12,)),
        *[dma((8,))] * 4,
        dma((4, rows)),
        dma((2 + depth,)),
        dma((2 + depth,)),
    ] + reducer_scratch(depth)
    anywhere = pl.BlockSpec(memory_space=pl.ANY)
    in_vmem = pl.BlockSpec(memory_space=pltpu.VMEM)
    shape = jax.ShapeDtypeStruct
    return pl.pallas_call(
        lambda *refs: backward_kernel(dp_size, *refs),
        out_shape=[
            shape((UNITS, pieces_of(depth), UNIT // pieces_of(depth), width), low),
            shape((rows, share, width), full),
            shape((16, width), full),
        ],
        in_specs=[pl.BlockSpec(memory_space=pltpu.SMEM)] + [in_vmem] * 2 + [anywhere] * 19,
        out_specs=[anywhere, anywhere, in_vmem],
        scratch_shapes=scratch,
        compiler_params=pltpu.CompilerParams(
            collective_id=1, has_side_effects=True, vmem_limit_bytes=64 * 1024 * 1024 - 65536
        ),
        name="backward",
    )(lengths, cls_grad, vectors, cotangent, *saved)


def contrast_kernel(dp_size, sents, *refs):
    (
        cls_ref,
        vectors,
        w_hbm,
        masks_hbm,
        loss_ref,
        w_grad,
        b_grad,
        cls_grad,
        w_pool,
        masks,
        rows_in,
        mine,
        every,
        views,
        pooled,
        units,
        inverse,
        logit_grad,
        lowered,
        load_sem,
        rs_s,
        rs_r,
        own_sem,
        z_s,
        z_r,
        hop_s,
        hop_r,
    ) = refs
    at = Places(dp_size)
    width = w_pool.shape[0]
    slots = views.shape[1]
    group = slots // dp_size
    share = group // 4
    loads = [
        pltpu.make_async_copy(w_hbm, w_pool, load_sem.at[0]),
        pltpu.make_async_copy(masks_hbm, masks, load_sem.at[1]),
    ]
    for load in loads:
        load.start()
    others = [(at.dp, (at.mp + j) % 4) for j in range(1, 4)]
    greet(others + [at.across_x] + [at.along_z(step) for step in range(1, at.depth)])

    quarters = [
        remote(
            cls_ref.at[(at.mp + j) % 4],
            rows_in.at[j - 1],
            rs_s.at[j - 1],
            rs_r.at[j - 1],
            others[j - 1],
        )
        for j in range(1, 4)
    ]
    for copy in quarters:
        copy.start()
    total = cls_ref[at.mp].astype(jnp.float32)
    for j, copy in enumerate(quarters):
        copy.wait_recv()
        total = total + rows_in[j].astype(jnp.float32)
    mine[...] = total.astype(jnp.bfloat16)

    place = every.at[at.z, at.x, at.y, at.core]
    own = pltpu.make_async_copy(mine, place, own_sem)
    own.start()
    along = [
        remote(mine, place, z_s.at[step - 1], z_r.at[step - 1], at.along_z(step))
        for step in range(1, at.depth)
    ]
    for copy in along:
        copy.start()
    own.wait()
    for copy in along:
        copy.wait_recv()
    hops = []
    for i, (part, device) in enumerate(
        [
            (every.at[:, at.x, at.y, at.core], at.across_x),
            (every.at[:, :, at.y, at.core], at.across_y),
            (every.at[:, :, :, at.core], at.across_core),
        ]
    ):
        hop = remote(part, part, hop_s.at[i], hop_r.at[i], device)
        hop.start()
        hop.wait_recv()
        hops.append(hop)
    for load in loads:
        load.wait()

    per_z = slots // at.depth
    for t in range(2):
        for z in range(at.depth):
            part = slice(z * per_z, (z + 1) * per_z)
            cls_rows = every[z].reshape(per_z, width).astype(jnp.float32)
            keep = masks[z, :, t].reshape(per_z, width).astype(jnp.float32)
            view = (cls_rows * keep * KEEP_SCALE).astype(jnp.bfloat16)
            views[t, part] = view
            unit = jnp.tanh(nn(view, w_pool[...]) + vectors[6:7])
            pooled[t, part] = unit
            inv = lax.rsqrt(jnp.sum(unit * unit, axis=-1, keepdims=True) + 1e-06)
            inverse[t, part] = inv
            units[t, part] = (unit * inv).astype(jnp.bfloat16)

    def real(index):
        return index % 32 < sents

    loss = jnp.zeros((1, 1), jnp.float32)
    for z in range(at.depth):
        part = slice(z * per_z, (z + 1) * per_z)
        logits = nt(units[0, part], units[1]) * 20.0
        line = z * per_z + lax.broadcasted_iota(jnp.int32, logits.shape, 0)
        column = lax.broadcasted_iota(jnp.int32, logits.shape, 1)
        logits = jnp.where(real(column), logits, MASKED)
        peak = jnp.max(logits, axis=1, keepdims=True)
        raised = jnp.exp(logits - peak)
        row_total = jnp.sum(raised, axis=1, keepdims=True)
        partner = line == column
        chosen = jnp.sum(jnp.where(partner, logits, 0.0), axis=1, keepdims=True)
        row_loss = peak + jnp.log(row_total) - chosen
        row_loss = jnp.where(real(line[:, :1]), row_loss, 0.0)
        loss = loss + jnp.sum(row_loss, axis=0, keepdims=True)
        grad = raised / row_total - jnp.where(partner, 1.0, 0.0)
        logit_grad[part] = jnp.where(real(line), grad, 0.0).astype(jnp.bfloat16)
    count = slots // 32 * sents
    loss_ref[...] = jnp.broadcast_to(loss / count, loss_ref.shape)

    bias = jnp.zeros((1, width), jnp.float32)
    for t in range(2):
        for z in range(at.depth):
            part = slice(z * per_z, (z + 1) * per_z)
            if t == 0:
                unit_grad = nn(logit_grad[part], units[1]) * 20.0
            else:
                unit_grad = tn(logit_grad[:, part], units[0]) * 20.0
            before = pooled[t, part]
            inv = inverse[t, part]
            unit = before * inv
            inner = jnp.sum(unit_grad * unit, axis=-1, keepdims=True)
            grad = inv * (unit_grad - unit * inner) * (1.0 - before * before)
            low = grad.astype(jnp.bfloat16)
            lowered[t, part] = low
            bias = bias + jnp.sum(low.astype(jnp.float32), axis=0, keepdims=True)
    b_grad[...] = bias

    here = pl.ds(pl.multiple_of(at.dp * group, group), group)
    back = jnp.zeros((group, width), jnp.float32)
    for t in range(2):
        keep = masks[at.z, at.x, t].astype(jnp.float32)
        back = back + nt(lowered[t, here], w_pool[...]) * keep
    cls_grad[...] = back * KEEP_SCALE
    for half in range(2):
        columns = slice(half * width // 2, (half + 1) * width // 2)
        w_grad[:, columns] = tn(views[0], lowered[0, :, columns]) + tn(
            views[1], lowered[1, :, columns]
        )
    for copy in quarters + along + hops:
        copy.wait_send()


def contrast_whole(cls_part, masks, w_pool, vectors, dp_size, sents):
    group, width = cls_part.shape
    slots = group * dp_size
    depth = dp_size // 2
    share = group // 4
    low, full = jnp.bfloat16, jnp.float32
    dma = pltpu.SemaphoreType.DMA
    vmem = pltpu.VMEM
    anywhere = pl.BlockSpec(memory_space=pl.ANY)
    in_vmem = pl.BlockSpec(memory_space=pltpu.VMEM)
    shape = jax.ShapeDtypeStruct
    return pl.pallas_call(
        lambda *refs: contrast_kernel(dp_size, sents, *refs),
        out_shape=[
            shape((8, 128), full),
            shape((width, width), full),
            shape((1, width), full),
            shape((group, width), full),
        ],
        in_specs=[in_vmem, in_vmem, anywhere, anywhere],
        out_specs=[in_vmem] * 4,
        scratch_shapes=[
            vmem((width, width), low),
            vmem(masks.shape, low),
            vmem((3, share, width), low),
            vmem((share, width), low),
            vmem((depth, 2, 2, 2, share, width), low),
            vmem((2, slots, width), low),
            vmem((2, slots, width), full),
            vmem((2, slots, width), low),
            vmem((2, slots, 1), full),
            vmem((slots, slots), low),
            vmem((2, slots, width), low),
            dma((2,)),
            dma((3,)),
            dma((3,)),
            dma,
            dma((max(depth - 1, 1),)),
            dma((max(depth - 1, 1),)),
            dma((3,)),
            dma((3,)),
        ],
        compiler_params=pltpu.CompilerParams(
            collective_id=3, has_side_effects=True, vmem_limit_bytes=60 * 1024 * 1024
        ),
        name="contrast",
    )(cls_part.reshape(4, share, width), vectors, w_pool, masks)


def shards(
    tokens,
    lengths,
    view_masks,
    w_qkv,
    b_qv,
    w_out,
    b_out,
    ln1_gain,
    ln1_bias,
    w_in,
    b_in,
    w_back,
    b_back,
    ln2_gain,
    ln2_bias,
    w_pool,
    b_pool,
    cotangent,
):
    rows, share, width = tokens.shape
    ranks = lax.axis_size("dp")
    sents = lengths.shape[1]
    gathers = ranks * rows * 32 <= 1024
    masks = jnp.pad(view_masks, [(0, 0), (0, 32 - sents), (0, 0), (0, 0)]).astype(jnp.bfloat16)
    masks = masks.transpose(2, 0, 1, 3).reshape(2, rows * 32, width)
    vectors = jnp.stack(
        [b_out, ln1_gain, ln1_bias, b_back, ln2_gain, ln2_bias, b_pool, jnp.zeros_like(b_pool)]
    )
    hidden, cls_part, *saved, masks = forward(
        tokens, lengths, w_qkv, b_qv, w_out, w_in, b_in, w_back, vectors, masks, ranks, gathers
    )
    if gathers:
        loss, w_pool_grad, b_pool_grad, cls_grad = contrast_whole(
            cls_part, masks, w_pool, vectors, ranks, sents
        )
        loss, b_pool_grad = loss[0, 0], b_pool_grad[0]
    else:
        cls_rows = cls_part.reshape(rows, -1, width)[:, :sents]
        cls_rows = lax.psum(cls_rows, "mp").astype(jnp.float32)
        loss, w_pool_grad, b_pool_grad, cls_grad = contrast(
            cls_rows.reshape(-1, width), view_masks, w_pool, b_pool
        )
        cls_grad = cls_grad.reshape(rows, -1, width)
        cls_grad = jnp.pad(cls_grad, [(0, 0), (0, 32 - sents), (0, 0)]).reshape(-1, width)
    sums, token_grad, vectors = backward(
        lengths, cls_grad, vectors, cotangent, saved, ranks
    )
    if pieces_of(ranks // 2) != ranks // 2:
        sums = lax.psum(sums, "dp")
    sums = sums.reshape(UNITS, UNIT, width).astype(jnp.float32)
    own = lax.axis_index("mp")
    cols = b_qv.shape[1]
    own_qv = lax.dynamic_slice_in_dim(vectors, 10 + own, 1, axis=0)
    own_in = lax.dynamic_slice_in_dim(vectors, 6 + own, 1, axis=0)
    return (
        hidden,
        loss,
        token_grad,
        sums[9:12].transpose(0, 2, 1),
        jnp.concatenate([own_qv[:, :cols], own_qv[:, 256 : 256 + cols]], axis=0),
        sums[8],
        vectors[0],
        vectors[1],
        vectors[2],
        sums[4:8].reshape(width, width),
        own_in[0],
        sums[0:4].reshape(width, width),
        vectors[3],
        vectors[4],
        vectors[5],
        w_pool_grad,
        b_pool_grad,
    )


def solution(mesh):
    in_specs = (
        P("dp", "mp", None),
        P("dp", None),
        P("dp", None, None, None),
        P(None, None, "mp"),
        P(None, "mp"),
        P("mp", None),
        P(),
        P(),
        P(),
        P(None, "mp"),
        P("mp"),
        P("mp", None),
        P(),
        P(),
        P(),
        P(),
        P(),
        P("dp", "mp", None),
    )
    out_specs = (
        P("dp", "mp", None),
        P(),
        P("dp", "mp", None),
        P(None, None, "mp"),
        P(None, "mp"),
        P("mp", None),
        P(),
        P(),
        P(),
        P(None, "mp"),
        P("mp"),
        P("mp", None),
        P(),
        P(),
        P(),
        P(),
        P(),
    )
    return jax.shard_map(shards, mesh=mesh, in_specs=in_specs, out_specs=out_specs, check_vma=False)
```
